128 devices in a mesh: len: 16 (over z, x), xs: 8 (over y, core).
Axes of the slice: x: 4, y: 4, z: 4, core: 2. Of those that a mesh axis runs over, the one named last changes fastest.
Arguments:
- right_side: float32 [3, 16, 64, 16384], P(None, None, None, ('len', 'xs')), may hold values from -19 to 19
- mass_field: float32 [16, 64, 16384], P(None, None, ('len', 'xs')), may hold values from 0.5 to 2
- span_lengths: int32 [128], replicated, may hold values from 1 to 256, 16384 in all
- stick_flags: int32 [256], replicated, may hold values from 0 to 1
- normal_load: float32 [256], replicated, may hold values from 0.5 to 4
- prior_friction: float32 [2, 256], replicated, may hold values from -4 to 4
Outputs:
- increment: float32 [3, 16, 64, 16384], P(None, None, None, ('len', 'xs'))
- residual: float32 [3, 16, 64, 16384], P(None, None, None, ('len', 'xs'))
- friction: float32 [2, 256], replicated
The draws below stay inside these ranges and needn't reach their ends.
Inputs may be any that keep to these rules, and one draw needn't show every extreme that they name: `span_lengths`: the spans sum to 16384; the longest is exactly 256. `stick_flags`: 1 marks a sticking bearing, 0 a sliding one.
All inputs are finite; a program needn't handle non-finite values.
Results may differ from the reference program's by a relative error of at most 0.0003.
Values sent between devices are 32-bit elements; how exact they have to be, the bound alone decides.
A program may use at most 64 MiB of HBM per device.

```python
import math
import jax
import jax.numpy as jnp
import numpy as np
from jax import lax

DEPTH = 16
NS = 64
ITERS = 3
NL = 16384
NPIER = 128
NB = 256
SPAN_MOST = 256


def draw_right_side(key, part):
    first = jax.random.fold_in(key, 0)
    along = jnp.arange(NL, dtype=jnp.float32) / max(NL - 1, 1)
    rough = jnp.clip(jax.random.normal(first, (3, DEPTH, NS, NL), jnp.float32), -3.0, 3.0)
    return rough * (1.0 + 2.0 * along)


def set_ends(values, rng, least, high):
    index_at = [jax.random.randint(jax.random.fold_in(rng, axis), (), 0, length) for axis, length in enumerate(values.shape)]
    widest = values.shape.index(max(values.shape))
    next_to = index_at[:widest] + [(index_at[widest] + 1) % values.shape[widest]] + index_at[widest + 1:]
    return values.at[tuple(index_at)].set(least).at[tuple(next_to)].set(high)


def shard_levels(own_key, shape, cuts, smallest, high):
    factor_of, own = 1.0, jax.random.fold_in(own_key, 6)
    for axis_at, blocks in cuts:
        heights = jnp.exp(jax.random.uniform(jax.random.fold_in(own, axis_at), (blocks,), jnp.float32, smallest / len(cuts), high / len(cuts)))
        factor_of = factor_of * jnp.repeat(heights, shape[axis_at] // blocks).reshape([-1 if axis == axis_at else 1 for axis in range(len(shape))])
    return factor_of


def length_profile(amount, total, most, lean):
    loads = [(1 << 20) // math.isqrt(rank ** lean) + 1 for rank in range(2, amount + 1)]
    spare, holding = total - most - (amount - 1), [1] * (amount - 1)
    while spare > 0:
        candidates = [i for i in range(amount - 1) if holding[i] < most]
        whole, budget = sum([loads[i] for i in candidates]), spare
        for i in candidates:
            more = min(most - holding[i], max(1, budget * loads[i] // whole), spare)
            holding[i] = holding[i] + more
            spare = spare - more
    return np.array([most] + holding)


def ragged(stream_key, number_of, total, limit, slope):
    if number_of == 2:
        one = jax.random.randint(stream_key, (), max(1, total - limit), min(limit, total - 1) + 1)
        return jnp.stack([one, total - one])
    tallies = jnp.asarray(length_profile(number_of, total, limit, slope), jnp.int32)
    couples = (number_of - 1) // 2
    source_of, sink = tallies[1:1 + 2 * couples:2], tallies[2:2 + 2 * couples:2]
    room = jnp.minimum(source_of - 1, limit - sink)
    moved = jax.random.randint(jax.random.fold_in(stream_key, 1), (couples,), 0, 1 << 20) % (room + 1)
    tallies = tallies.at[1:1 + 2 * couples:2].set(source_of - moved).at[2:2 + 2 * couples:2].set(sink + moved)
    return tallies[jax.random.permutation(jax.random.fold_in(stream_key, 2), number_of)]


def centred(rng, extent, scale, limit, kind=jnp.bfloat16):
    return jnp.clip(scale * jax.random.normal(rng, extent, jnp.float32), -limit, limit).astype(kind)


def setup_inputs(seed: int = 0) -> dict:
    splits = jax.random.split(jax.random.key(seed), 7)
    return {
        "right_side": draw_right_side(jax.random.fold_in(splits[6], 71), 0),
        "mass_field": jnp.clip(jnp.exp(math.log(2.0) - 1.3862944 * jax.random.uniform(splits[1], (DEPTH, NS, NL), jnp.float32) ** shard_levels(splits[1], (DEPTH, NS, NL), ((2, 128),), -0.2, 0.2)), 0.5, 2.0),
        "span_lengths": ragged(splits[2], NPIER, NL, SPAN_MOST, 2).astype(jnp.int32),
        "stick_flags": set_ends(jax.random.randint(splits[3], (NB,), 0, 2), jax.random.fold_in(splits[3], 1), 0, 1).astype(jnp.int32),
        "normal_load": jnp.clip(jnp.exp(jax.random.uniform(splits[4], (NB,), jnp.float32, math.log(0.5), math.log(4.0))), 0.5, 4.0),
        "prior_friction": centred(splits[5], (2, NB), 1.0, 4.0, jnp.float32),
    }


shear_modulus = 1.0
bulk_modulus = 1.5
elastic_stiffness = 8.0
pendulum_radius = 4.0
vertical_stiffness = 5.0
static_friction = 0.6
kinetic_friction = 0.45

def central(array, along_dim):
    widths = [(0, 0)] * array.ndim
    widths[along_dim] = (1, 1)
    padded = jnp.pad(array, widths)
    count = array.shape[along_dim]
    upper = lax.slice_in_dim(padded, 2, count + 2, axis=along_dim)
    lower = lax.slice_in_dim(padded, 0, count, axis=along_dim)
    return 0.5 * (upper - lower)

def laplace(array):
    padded = jnp.pad(array, 1)
    total = 6.0 * array
    total = total - padded[2:, 1:-1, 1:-1] - padded[:-2, 1:-1, 1:-1]
    total = total - padded[1:-1, 2:, 1:-1] - padded[1:-1, :-2, 1:-1]
    total = total - padded[1:-1, 1:-1, 2:] - padded[1:-1, 1:-1, :-2]
    return total

def operate(field, mass_field):
    dims_of = (2, 1, 0)
    divergence = central(field[0], 2) + central(field[1], 1) + central(field[2], 0)
    pieces = []
    for component in range(3):
        pieces.append(mass_field * field[component] + shear_modulus * laplace(field[component]) - bulk_modulus * central(divergence, dims_of[component]))
    return jnp.stack(pieces)

def bearing_sites(span_lengths):
    ends = (jnp.cumsum(span_lengths) - 1).astype(jnp.int32)
    along = jnp.repeat(ends, 2).astype(jnp.int32)
    across = jnp.tile(jnp.array([NS // 4, 3 * NS // 4], dtype=jnp.int32), NPIER)
    return (along, across)

def return_map(readout, stick_flags, normal_load, prior_friction):
    coeff = jnp.where(stick_flags == 1, static_friction, kinetic_friction)
    radius = coeff * normal_load
    trial = prior_friction + elastic_stiffness * readout[0:2]
    magnitude = jnp.sqrt(trial[0] * trial[0] + trial[1] * trial[1])
    friction = trial * (radius / jnp.maximum(magnitude, radius))
    horizontal = friction + normal_load / pendulum_radius * readout[0:2]
    vertical = vertical_stiffness * readout[2]
    force = jnp.concatenate([horizontal, vertical[None]], axis=0)
    return (friction, force)

def reference(right_side, mass_field, span_lengths, stick_flags, normal_load, prior_friction):
    increment = jnp.zeros_like(right_side)
    solved = right_side
    direction = right_side
    norm_now = jnp.sum(solved * solved)
    for iteration in range(ITERS):
        image = operate(direction, mass_field)
        alpha = norm_now / jnp.sum(direction * image)
        increment = increment + alpha * direction
        solved = solved - alpha * image
        norm_next = jnp.sum(solved * solved)
        direction = solved + norm_next / norm_now * direction
        norm_now = norm_next
    along, across = bearing_sites(span_lengths)
    readout = increment[:, 0, across, along]
    friction, force = return_map(readout, stick_flags, normal_load, prior_friction)
    residual = solved.at[:, 0, across, along].add(-force)
    return (increment, residual, friction)
```

```python
import jax
import jax.numpy as jnp
from jax import lax
from jax.experimental import pallas as pl
from jax.experimental.pallas import tpu as pltpu
from jax.sharding import PartitionSpec as P

shear_modulus = 1.0
bulk_modulus = 1.5
elastic_stiffness = 8.0
pendulum_radius = 4.0
vertical_stiffness = 5.0
static_friction = 0.6
kinetic_friction = 0.45

DEPTH = 16
NS = 64
LANES = 128
PITCH = NS + 8
PADDED = (DEPTH + 2) * PITCH
HALO = 6
MASS_HALO = 4
EDGE = 6
STRIP = 24
PAIRS = DEPTH * NS // LANES
STRIP_ROWS = (PAIRS + 2) * STRIP
MESSAGE = (3 * HALO + MASS_HALO) * PAIRS
PARTIALS = 24

MESH = pl.DeviceIdType.MESH
HIGHEST = lax.Precision.HIGHEST
F32 = jnp.float32


def two_sum(a, b):
    s = a + b
    t = s - a
    return s, (a - (s - t)) + (b - t)


def fold(block):
    return jnp.sum(block.reshape(block.shape[0] // 8, 8, LANES), axis=0)


def bearing_ends(spans):
    piers = spans.shape[1]
    upto = (
        lax.broadcasted_iota(jnp.int32, (piers, 2 * piers), 0)
        <= lax.broadcasted_iota(jnp.int32, (piers, 2 * piers), 1) // 2
    ).astype(F32)
    return (
        jnp.dot(
            jnp.broadcast_to(spans.astype(F32), (8, piers)),
            upto,
            precision=HIGHEST,
            preferred_element_type=F32,
        )[0:1]
        - 1.0
    )


def bearing_hits(ends, start):
    bearings = ends.shape[1]
    along = lax.broadcasted_iota(jnp.int32, (LANES, bearings), 0) + start
    side = lax.rem(lax.broadcasted_iota(jnp.int32, (LANES, bearings), 1), 2)
    here = along.astype(F32) == ends
    return [jnp.where(here & (side == s), 1.0, 0.0).astype(F32) for s in range(2)]


def krylov_kernel(
    sizes,
    b_ref,
    mass_ref,
    spans_ref,
    out1_ref,
    out2_ref,
    out3_ref,
    sums_ref,
    v,
    mass,
    w,
    sv,
    sm,
    sw,
    valid,
    send_left,
    send_right,
    from_left,
    from_right,
    part_a,
    part_b,
    slots_a,
    slots_b,
    in_sem,
    halo_send,
    halo_recv,
    a_send,
    a_recv,
    b_send,
    b_recv,
):
    len_size, xs_size = sizes
    count = len_size * xs_size
    at_len, at_xs = lax.axis_index("len"), lax.axis_index("xs")
    me = at_len * xs_size + at_xs
    left, right = lax.rem(me + count - 1, count), lax.rem(me + 1, count)
    place = lambda i: (i // xs_size, lax.rem(i, xs_size))
    group_a = [(at_len, lax.rem(at_xs + k, xs_size)) for k in range(1, xs_size)]
    group_b = [(lax.rem(at_len + k, len_size), at_xs) for k in range(1, len_size)]

    barrier = pltpu.get_barrier_semaphore()
    partners = [place(left), place(right)] + group_a + group_b
    for partner in partners:
        pl.semaphore_signal(barrier, inc=1, device_id=partner, device_id_type=MESH)

    def load(d, carry):
        for c in range(3):
            pltpu.make_async_copy(
                b_ref.at[c, pl.ds(d * NS, NS)],
                v.at[0, c, pl.ds((d + 1) * PITCH, NS)],
                in_sem.at[c],
            ).start()
        return carry

    lax.fori_loop(0, DEPTH, load, 0)
    pltpu.make_async_copy(mass_ref, mass, in_sem.at[3]).start()

    def guard(d, carry):
        row = (d + 1) * PITCH + NS
        for c in range(3):
            for k in range(3):
                v[k, c, pl.ds(row, 8)] = jnp.zeros((8, LANES), F32)
        w[pl.ds(row, 8)] = jnp.zeros((8, LANES), F32)
        return carry

    lax.fori_loop(0, DEPTH, guard, 0)

    for start in (0, (DEPTH + 1) * PITCH):
        for c in range(3):
            for k in range(3):
                v[k, c, pl.ds(start, PITCH)] = jnp.zeros((PITCH, LANES), F32)
        w[pl.ds(start, PITCH)] = jnp.zeros((PITCH, LANES), F32)
    for start in (0, (PAIRS + 1) * STRIP):
        for side in range(2):
            sw[side, pl.ds(start, STRIP)] = jnp.zeros((STRIP, LANES), F32)
            for c in range(3):
                for k in range(3):
                    sv[k, side, c, pl.ds(start, STRIP)] = jnp.zeros((STRIP, LANES), F32)

    has_left = jnp.where(me > 0, 1.0, 0.0).astype(F32)
    has_right = jnp.where(me < count - 1, 1.0, 0.0).astype(F32)
    row = lax.broadcasted_iota(jnp.int32, (STRIP, LANES), 0)
    valid[0] = jnp.where(row < HALO, has_left, 1.0)
    valid[1] = jnp.where(row >= 2 * EDGE, has_right, 1.0)

    for c in range(4):
        if c < 3:
            pltpu.make_async_copy(
                b_ref.at[c], v.at[0, c, pl.ds(0, DEPTH * NS)], in_sem.at[c]
            ).wait()
        else:
            pltpu.make_async_copy(mass_ref, mass, in_sem.at[3]).wait()
        width = HALO if c < 3 else MASS_HALO

        def edges(t, carry, c=c, width=width):
            if c < 3:
                tile = jnp.concatenate(
                    [v[0, c, pl.ds((2 * t + 1 + i) * PITCH, NS)] for i in range(2)], axis=0
                )
            else:
                tile = mass[pl.ds(t * LANES, LANES)]
            turned = tile.T
            strip = (t + 1) * STRIP
            if c < 3:
                sv[0, 0, c, pl.ds(strip + HALO, 2 * EDGE)] = turned[: 2 * EDGE]
                sv[0, 1, c, pl.ds(strip, 2 * EDGE)] = turned[LANES - 2 * EDGE :]
            else:
                sm[0, pl.ds(strip + HALO, 2 * EDGE)] = turned[: 2 * EDGE]
                sm[1, pl.ds(strip, 2 * EDGE)] = turned[LANES - 2 * EDGE :]
            send_left[pl.ds(c * HALO * PAIRS + t, width, stride=PAIRS), :] = turned[:width]
            send_right[pl.ds(c * HALO * PAIRS + t, width, stride=PAIRS), :] = turned[
                LANES - width :
            ]
            return carry

        lax.fori_loop(0, PAIRS, edges, 0)

    pl.semaphore_wait(barrier, len(partners))
    halos = [
        pltpu.make_async_remote_copy(
            src_ref=send_left,
            dst_ref=from_right,
            send_sem=halo_send.at[0],
            recv_sem=halo_recv.at[0],
            device_id=place(left),
            device_id_type=MESH,
        ),
        pltpu.make_async_remote_copy(
            src_ref=send_right,
            dst_ref=from_left,
            send_sem=halo_send.at[1],
            recv_sem=halo_recv.at[1],
            device_id=place(right),
            device_id_type=MESH,
        ),
    ]
    for copy in halos:
        copy.start()

    def main_divergence(k):
        def body(d, carry):
            base = (d + 1) * PITCH
            first = v[k, 0, pl.ds(base, NS)]
            along = pltpu.roll(first, LANES - 1, 1) - pltpu.roll(first, 1, 1)
            across = v[k, 1, pl.ds(base + 1, NS)] - v[k, 1, pl.ds(base - 1, NS)]
            depth = v[k, 2, pl.ds(base + PITCH, NS)] - v[k, 2, pl.ds(base - PITCH, NS)]
            w[pl.ds(base, NS)] = (0.25 * bulk_modulus) * (along + across + depth)
            return carry

        lax.fori_loop(0, DEPTH, body, 0)

    def main_image(k, dots):
        zero = jnp.zeros((8, LANES), F32)

        def body(d, sums):
            base = (d + 1) * PITCH
            heavy = mass[pl.ds(d * NS, NS)] + 6.0
            terms = [zero] * len(dots)
            for c in range(3):
                here = v[k, c, pl.ds(base, NS)]
                image = heavy * here
                image = image - (v[k, c, pl.ds(base + 1, NS)] + v[k, c, pl.ds(base - 1, NS)])
                image = image - (
                    v[k, c, pl.ds(base + PITCH, NS)] + v[k, c, pl.ds(base - PITCH, NS)]
                )
                if c == 0:
                    local = w[pl.ds(base, NS)]
                    image = image - (
                        pltpu.roll(here + local, LANES - 1, 1) + pltpu.roll(here - local, 1, 1)
                    )
                else:
                    step = 1 if c == 1 else PITCH
                    image = image - (pltpu.roll(here, LANES - 1, 1) + pltpu.roll(here, 1, 1))
                    image = image - (w[pl.ds(base + step, NS)] - w[pl.ds(base - step, NS)])
                if k < 2:
                    v[k + 1, c, pl.ds(base, NS)] = image
                else:
                    out3_ref[c, pl.ds(d * NS, NS)] = image
                for n, kind in enumerate(dots):
                    terms[n] = terms[n] + fold(
                        {"vv": here * here, "vi": here * image, "ii": image * image}[kind]
                    )
            return tuple(s + t for s, t in zip(sums, terms))

        return lax.fori_loop(0, DEPTH, body, (zero,) * len(dots))

    main_divergence(0)
    mu0, mu1, mu2 = main_image(0, ("vv", "vi", "ii"))
    main_divergence(1)
    mu3, mu4 = main_image(1, ("vi", "ii"))
    main_divergence(2)
    (mu5,) = main_image(2, ("vi",))
    lane = lax.broadcasted_iota(jnp.int32, (8, LANES), 1)
    inner = (lane >= EDGE) & (lane < LANES - EDGE)
    moments = tuple(jnp.where(inner, mu, 0.0) for mu in (mu0, mu1, mu2, mu3, mu4, mu5))

    for copy in halos:
        copy.wait_recv()
    for c in range(4):
        width = HALO if c < 3 else MASS_HALO

        def unpack(t, carry, c=c, width=width):
            strip = (t + 1) * STRIP
            rows = pl.ds(c * HALO * PAIRS + t, width, stride=PAIRS)
            before = from_left[rows, :] * has_left
            after = from_right[rows, :] * has_right
            if c < 3:
                sv[0, 0, c, pl.ds(strip, width)] = before
                sv[0, 1, c, pl.ds(strip + 2 * EDGE, width)] = after
            else:
                sm[0, pl.ds(strip + HALO - width, width)] = before
                sm[1, pl.ds(strip + 2 * EDGE, width)] = after
            return carry

        lax.fori_loop(0, PAIRS, unpack, 0)

    half = LANES // 2

    def low(n):
        return lax.broadcasted_iota(jnp.int32, (n, LANES), 1) < half

    def across_pair(x):
        at = lax.rem(lax.broadcasted_iota(jnp.int32, x.shape, 1), half)
        after = jnp.where(at == half - 1, 0.0, pltpu.roll(x, LANES - 1, 1))
        before = jnp.where(at == 0, 0.0, pltpu.roll(x, 1, 1))
        return after, before

    def depth_diff(ref, base, n):
        x = ref[pl.ds(base, n)]
        up, down = ref[pl.ds(base + STRIP, n)], ref[pl.ds(base - STRIP, n)]
        return pltpu.roll(jnp.where(low(n), up - x, x - down), half, 1)

    def depth_sum(x, ref, base, n):
        up, down = ref[pl.ds(base + STRIP, n)], ref[pl.ds(base - STRIP, n)]
        return pltpu.roll(x + jnp.where(low(n), up, down), half, 1)

    for k, n in ((0, 16), (1, 16), (2, 8)):

        def strip_divergence(i, carry, k=k, n=n):
            side, t = i // PAIRS, lax.rem(i, PAIRS)
            at = 2 * k + 1
            base = (t + 1) * STRIP + at
            first = sv.at[k, side, 0]
            along = first[pl.ds(base + 1, n)] - first[pl.ds(base - 1, n)]
            after, before = across_pair(sv[k, side, 1, pl.ds(base, n)])
            depth = depth_diff(sv.at[k, side, 2], base, n)
            sw[side, pl.ds(base, n)] = (
                (0.25 * bulk_modulus)
                * (along + (after - before) + depth)
                * valid[side, pl.ds(at, n)]
            )
            return carry

        lax.fori_loop(0, 2 * PAIRS, strip_divergence, 0)

        def strip_image(i, sums, k=k, n=n):
            side, t = i // PAIRS, lax.rem(i, PAIRS)
            at = 2 * k + 2
            base = (t + 1) * STRIP + at
            heavy = sm[side, pl.ds(base, n)] + 6.0
            sw_side = sw.at[side]
            local = sw_side[pl.ds(base, n)]
            for c in range(3):
                ref = sv.at[k, side, c]
                here = ref[pl.ds(base, n)]
                image = heavy * here - (ref[pl.ds(base + 1, n)] + ref[pl.ds(base - 1, n)])
                after, before = across_pair(here)
                image = image - (after + before) - depth_sum(here, ref, base, n)
                if c == 0:
                    image = image - (sw_side[pl.ds(base + 1, n)] - sw_side[pl.ds(base - 1, n)])
                elif c == 1:
                    after, before = across_pair(local)
                    image = image - (after - before)
                else:
                    image = image - depth_diff(sw_side, base, n)
                sv[k + 1, side, c, pl.ds(base, n)] = image * valid[side, pl.ds(at, n)]
            return sums

        lax.fori_loop(0, 2 * PAIRS, strip_image, 0)

    def strip_dots(i, sums):
        side, t = i // PAIRS, lax.rem(i, PAIRS)
        base = (t + 1) * STRIP + HALO
        mine = lax.broadcasted_iota(jnp.int32, (8, LANES), 0) < EDGE
        sums = list(sums)
        for c in range(3):
            x = [jnp.where(mine, sv[k, side, c, pl.ds(base, 8)], 0.0) for k in range(4)]
            for n, (p, q) in enumerate(((0, 0), (0, 1), (1, 1), (1, 2), (2, 2), (2, 3))):
                sums[n] = sums[n] + x[p] * x[q]
        return tuple(sums)

    zero = jnp.zeros((8, LANES), F32)
    strips = lax.fori_loop(0, 2 * PAIRS, strip_dots, (zero,) * 6)

    lanes = lax.broadcasted_iota(jnp.int32, (LANES, LANES), 1)
    outer = (lanes < EDGE) | (lanes >= LANES - EDGE)

    def merge(k, c, t):
        base = (t + 1) * STRIP + EDGE
        rows = jnp.concatenate(
            [
                sv[k, 0, c, pl.ds(base, 8)],
                jnp.zeros((LANES - 16, LANES), F32),
                sv[k, 1, c, pl.ds(base - 2, 8)],
            ],
            axis=0,
        ).T
        out = (out1_ref, out2_ref, out3_ref)[k - 1]
        if k < 3:
            main = jnp.concatenate(
                [v[k, c, pl.ds((2 * t + 1 + i) * PITCH, NS)] for i in range(2)], axis=0
            )
        else:
            main = out[c, pl.ds(t * LANES, LANES)]
        out[c, pl.ds(t * LANES, LANES)] = jnp.where(outer, rows, main)

    for k in (1, 2):
        for c in (0, 1):
            merge(k, c, 0)

    head, rest = [], []
    for total in range(6):
        hi, lo = two_sum(moments[total], strips[total])
        for shift in (4, 2, 1):
            hi, more = two_sum(hi, pltpu.roll(hi, shift, 0))
            lo = lo + pltpu.roll(lo, shift, 0) + more
        head.append(hi[0:1])
        rest.append(lo[0:1])
    hits = bearing_hits(bearing_ends(spans_ref[...]), me * LANES)
    site = jnp.zeros((8, hits[0].shape[1]), F32)
    for s, across in ((0, NS // 4), (1, 3 * NS // 4)):
        rows = [v[0, c, pl.ds(PITCH + across, 1)] for c in (0, 1)]
        rows += [out1_ref[c, pl.ds(across, 1)] for c in (0, 1)]
        rows += [out2_ref[c, pl.ds(across, 1)] for c in (0, 1)]
        rows += [jnp.zeros((2, LANES), F32)]
        site = site + jnp.dot(
            jnp.concatenate(rows, axis=0),
            hits[s],
            precision=HIGHEST,
            preferred_element_type=F32,
        )
    halves = [site[:, :LANES], site[:, LANES:]]
    part_a[...] = jnp.concatenate(
        head
        + [halves[0][0:2]]
        + rest
        + [halves[1][0:2]]
        + [halves[0][2:4], halves[1][2:4], halves[0][4:6], halves[1][4:6]],
        axis=0,
    )

    def exchange(source, slots, partners, own, send_sems, recv_sems):
        copies = []
        for k, partner in enumerate(partners):
            copy = pltpu.make_async_remote_copy(
                src_ref=source,
                dst_ref=slots.at[own],
                send_sem=send_sems.at[k],
                recv_sem=recv_sems.at[k],
                device_id=partner,
                device_id_type=MESH,
            )
            copy.start()
            copies.append(copy)
        slots[own] = source[...]
        return copies

    def total(slots, number):
        parts = [(slots[i, 0:8], slots[i, 8:16], slots[i, 16:]) for i in range(number)]
        while len(parts) > 1:
            merged = []
            for i in range(0, len(parts) - 1, 2):
                hi, more = two_sum(parts[i][0], parts[i + 1][0])
                merged.append(
                    (hi, parts[i][1] + parts[i + 1][1] + more, parts[i][2] + parts[i + 1][2])
                )
            if len(parts) % 2:
                merged.append(parts[-1])
            parts = merged
        return jnp.concatenate(parts[0], axis=0)

    copies_a = exchange(part_a, slots_a, group_a, at_xs, a_send, a_recv)

    def merge_rest(t, carry, ks=(1,)):
        for k in ks:
            for c in range(3):
                merge(k, c, t)
        return carry

    lax.fori_loop(1, PAIRS, merge_rest, 0)
    merge(1, 2, 0)
    for copy in copies_a:
        copy.wait_recv()
    part_b[...] = total(slots_a, xs_size)
    copies_b = exchange(part_b, slots_b, group_b, at_len, b_send, b_recv)

    def merge_last(t, carry):
        for k in (2, 3):
            for c in range(3):
                merge(k, c, t)
        return carry

    lax.fori_loop(1, PAIRS, merge_last, 0)
    merge(2, 2, 0)
    for c in range(3):
        merge(3, c, 0)
    for copy in copies_b:
        copy.wait_recv()
    sums_ref[...] = total(slots_b, len_size)
    for copy in halos + copies_a + copies_b:
        copy.wait_send()


def steps(sums):
    hi, lo = sums[0:8], sums[8:16]
    for shift in (64, 32, 16, 8, 4, 2, 1):
        hi, more = two_sum(hi, pltpu.roll(hi, shift, 1))
        lo = lo + pltpu.roll(lo, shift, 1) + more
    hi, lo = two_sum(hi, lo)
    theta = jnp.round(hi[1:2] / hi[0:1] * 64.0) * (1.0 / 64.0)
    central = [hi[0:1]]
    for order in range(5):
        n = 5 - order
        big = hi[:n] * 4097.0
        upper = big - (big - hi[:n])
        lower = hi[:n] - upper
        value, more = two_sum(hi[1 : n + 1], -theta * upper)
        value, extra = two_sum(value, -theta * lower)
        low_part = lo[1 : n + 1] - theta * lo[:n] + (more + extra)
        hi, lo = two_sum(value, low_part)
        central.append(hi[0:1])
    scale = 1.0 / central[0]
    c = [x * scale for x in central]
    c1 = [c[i + 1] + theta * c[i] for i in range(5)]

    def form(p, moments):
        terms = None
        for i in range(len(p)):
            for j in range(i, len(p)):
                term = (1.0 if i == j else 2.0) * (p[i] * p[j]) * moments[i + j]
                terms = term if terms is None else terms + term
        return terms

    one, zero = jnp.ones_like(theta), jnp.zeros_like(theta)
    left, ahead, norm = [one], [one], c[0]
    increment = [zero, zero, zero]
    for iteration in range(3):
        alpha = norm / form(ahead, c1)
        increment = [
            x + alpha * ahead[i] if i < len(ahead) else x for i, x in enumerate(increment)
        ]
        image = [theta * x for x in ahead] + [zero]
        image = [image[i] + (ahead[i - 1] if i else zero) for i in range(len(image))]
        left = left + [zero]
        left = [x - alpha * y for x, y in zip(left, image)]
        if iteration < 2:
            after = form(left, c)
            beta = after / norm
            ahead = ahead + [zero]
            ahead = [x + beta * y for x, y in zip(left, ahead)]
            norm = after
    x0, x1, x2 = increment
    r0, r1, r2, r3 = left
    increment = (x0 - theta * (x1 - theta * x2), x1 - 2.0 * theta * x2, x2)
    solved = (
        r0 - theta * (r1 - theta * (r2 - theta * r3)),
        r1 - theta * (2.0 * r2 - 3.0 * theta * r3),
        r2 - 3.0 * theta * r3,
        r3,
    )
    return increment, solved


def finish_kernel(
    b_ref,
    v1_ref,
    v2_ref,
    v3_ref,
    sums_ref,
    spans_ref,
    stick_ref,
    load_ref,
    prior_ref,
    inc_ref,
    res_ref,
    friction_ref,
    b,
    x,
    r,
    in_sem,
    out_sem,
):
    loads = [pltpu.make_async_copy(b_ref.at[c], b.at[c], in_sem.at[c]) for c in range(3)]
    for copy in loads:
        copy.start()
    me = lax.axis_index("len") * lax.axis_size("xs") + lax.axis_index("xs")
    sums = sums_ref[...]
    (x0, x1, x2), (r0, r1, r2, r3) = steps(sums)

    def site(first, second):
        return jnp.concatenate([sums[first : first + 2], sums[second : second + 2]], axis=1)

    wide = lambda a: jnp.concatenate([a, a], axis=1)
    readout = wide(x0) * site(6, 14) + wide(x1) * site(16, 18) + wide(x2) * site(20, 22)
    radius = jnp.where(stick_ref[...] == 1, static_friction, kinetic_friction) * load_ref[...]
    trial = prior_ref[...] + elastic_stiffness * readout
    magnitude = jnp.sqrt(trial[0:1] * trial[0:1] + trial[1:2] * trial[1:2])
    friction = trial * (radius / jnp.maximum(magnitude, radius))
    friction_ref[...] = friction
    force = friction + load_ref[...] / pendulum_radius * readout
    bearings = force.shape[1]
    rows = jnp.concatenate(
        [force, jnp.ones((1, bearings), F32), jnp.zeros((5, bearings), F32)], axis=0
    )
    hits = bearing_hits(bearing_ends(spans_ref[...]), me * LANES)
    placed = [
        lax.dot_general(
            rows,
            hit,
            (((1,), (1,)), ((), ())),
            precision=HIGHEST,
            preferred_element_type=F32,
        )
        for hit in hits
    ]

    chunk = DEPTH * NS // 2
    stores = []
    for c in range(3):
        loads[c].wait()
        for part in range(2):

            def body(i, carry, c=c, part=part):
                at = pl.ds(pl.multiple_of(part * chunk + i * NS, NS), NS)
                p0, p1, p2, p3 = b[c, at], v1_ref[c, at], v2_ref[c, at], v3_ref[c, at]
                x[c, at] = x0 * p0 + x1 * p1 + x2 * p2
                r[c, at] = r0 * p0 + r1 * p1 + r2 * p2 + r3 * p3
                return carry

            lax.fori_loop(0, chunk // NS, body, 0)
            if part == 0:
                for s, across in ((0, NS // 4), (1, 3 * NS // 4)):
                    at = pl.ds(across, 1)
                    if c < 2:
                        drop = placed[s][c : c + 1]
                    else:
                        drop = vertical_stiffness * x[c, at] * placed[s][2:3]
                    r[c, at] = r[c, at] - drop
            for ref, dst in ((x, inc_ref), (r, res_ref)):
                at = pl.ds(part * chunk, chunk)
                copy = pltpu.make_async_copy(
                    ref.at[c, at], dst.at[c, at], out_sem.at[len(stores)]
                )
                copy.start()
                stores.append(copy)
    for copy in stores:
        copy.wait()


def shards(right_side, mass_field, span_lengths, stick_flags, normal_load, prior_friction):
    sizes = (lax.axis_size("len"), lax.axis_size("xs"))
    rows = DEPTH * NS
    field = (3, rows, LANES)
    b = right_side.reshape(field)
    mass = mass_field.reshape(rows, LANES)
    spans = span_lengths.reshape(1, -1)
    stick = stick_flags.reshape(1, -1)
    load = normal_load.reshape(1, -1)
    anywhere = pl.BlockSpec(memory_space=pl.ANY)
    vmem = pl.BlockSpec(memory_space=pltpu.VMEM)
    v1, v2, v3, sums = pl.pallas_call(
        lambda *refs: krylov_kernel(sizes, *refs),
        name="krylov",
        out_shape=[jax.ShapeDtypeStruct(field, F32)] * 3
        + [jax.ShapeDtypeStruct((PARTIALS, LANES), F32)],
        in_specs=[anywhere, anywhere, vmem],
        out_specs=[vmem] * 4,
        scratch_shapes=[
            pltpu.VMEM((3, 3, PADDED, LANES), F32),
            pltpu.VMEM((rows, LANES), F32),
            pltpu.VMEM((PADDED, LANES), F32),
            pltpu.VMEM((4, 2, 3, STRIP_ROWS, LANES), F32),
            pltpu.VMEM((2, STRIP_ROWS, LANES), F32),
            pltpu.VMEM((2, STRIP_ROWS, LANES), F32),
            pltpu.VMEM((2, STRIP, LANES), F32),
            pltpu.VMEM((MESSAGE, LANES), F32),
            pltpu.VMEM((MESSAGE, LANES), F32),
            pltpu.VMEM((MESSAGE, LANES), F32),
            pltpu.VMEM((MESSAGE, LANES), F32),
            pltpu.VMEM((PARTIALS, LANES), F32),
            pltpu.VMEM((PARTIALS, LANES), F32),
            pltpu.VMEM((sizes[1], PARTIALS, LANES), F32),
            pltpu.VMEM((sizes[0], PARTIALS, LANES), F32),
            pltpu.SemaphoreType.DMA((4,)),
            pltpu.SemaphoreType.DMA((2,)),
            pltpu.SemaphoreType.DMA((2,)),
            pltpu.SemaphoreType.DMA((sizes[1],)),
            pltpu.SemaphoreType.DMA((sizes[1],)),
            pltpu.SemaphoreType.DMA((sizes[0],)),
            pltpu.SemaphoreType.DMA((sizes[0],)),
        ],
        compiler_params=pltpu.CompilerParams(collective_id=0, has_side_effects=True),
    )(b, mass, spans)
    increment, residual, friction = pl.pallas_call(
        finish_kernel,
        name="finish",
        out_shape=[
            jax.ShapeDtypeStruct(field, F32),
            jax.ShapeDtypeStruct(field, F32),
            jax.ShapeDtypeStruct(prior_friction.shape, F32),
        ],
        in_specs=[anywhere] + [vmem] * 8,
        out_specs=[anywhere, anywhere, vmem],
        scratch_shapes=[
            pltpu.VMEM(field, F32),
            pltpu.VMEM(field, F32),
            pltpu.VMEM(field, F32),
            pltpu.SemaphoreType.DMA((3,)),
            pltpu.SemaphoreType.DMA((12,)),
        ],
    )(b, v1, v2, v3, sums, spans, stick, load, prior_friction)
    return (
        increment.reshape(right_side.shape),
        residual.reshape(right_side.shape),
        friction,
    )


def solution(mesh):
    along = ("len", "xs")
    in_specs = (P(None, None, None, along), P(None, None, along), P(), P(), P(), P())
    out_specs = (P(None, None, None, along), P(None, None, None, along), P())
    return jax.shard_map(shards, mesh=mesh, in_specs=in_specs, out_specs=out_specs, check_vma=False)
```

```python
import jax
import jax.numpy as jnp
from jax import lax
from jax.experimental import pallas as pl
from jax.experimental.pallas import tpu as pltpu
from jax.sharding import PartitionSpec as P

shear_modulus = 1.0
bulk_modulus = 1.5
elastic_stiffness = 8.0
pendulum_radius = 4.0
vertical_stiffness = 5.0
static_friction = 0.6
kinetic_friction = 0.45

DEPTH = 16
NS = 64
LANES = 128
PITCH = NS + 8
PADDED = (DEPTH + 3) * PITCH
HALO = 6
PAIRS = DEPTH * NS // LANES
WIDE = 3 * HALO
SECTION = 24
STRIP = WIDE * SECTION
OWN = 2 * HALO * 4 * PAIRS
LANDED = HALO * 4 * PAIRS

UNROLL = 2

MESH = pl.DeviceIdType.MESH
HIGHEST = lax.Precision.HIGHEST
F32 = jnp.float32


def two_sum(a, b):
    s = a + b
    t = s - a
    return s, (a - (s - t)) + (b - t)


def fold(block):
    return jnp.sum(block.reshape(block.shape[0] // 8, 8, LANES), axis=0)


def bearing_ends(spans):
    piers = spans.shape[1]
    upto = (
        lax.broadcasted_iota(jnp.int32, (piers, 2 * piers), 0)
        <= lax.broadcasted_iota(jnp.int32, (piers, 2 * piers), 1) // 2
    ).astype(F32)
    return (
        jnp.dot(
            jnp.broadcast_to(spans.astype(F32), (8, piers)),
            upto,
            precision=HIGHEST,
            preferred_element_type=F32,
        )[0:1]
        - 1.0
    )


def bearing_hits(ends, start):
    bearings = ends.shape[1]
    along = lax.broadcasted_iota(jnp.int32, (LANES, bearings), 0) + start
    side = lax.rem(lax.broadcasted_iota(jnp.int32, (LANES, bearings), 1), 2)
    here = along.astype(F32) == ends
    return [jnp.where(here & (side == s), 1.0, 0.0).astype(F32) for s in range(2)]


def krylov_kernel(
    sizes,
    b_ref,
    mass_ref,
    spans_ref,
    out1_ref,
    out2_ref,
    out3_ref,
    coefficients_ref,
    sites_ref,
    v0,
    v1,
    v2,
    mass,
    w,
    x0,
    x1,
    x2,
    x3,
    strip_mass,
    strip_w,
    near_left,
    near_right,
    valid,
    back,
    hit,
    part_a,
    part_b,
    slots_a,
    slots_b,
    site_a,
    site_b,
    site_slots_a,
    site_slots_b,
    in_sem,
    halo_send,
    halo_recv,
    a_send,
    a_recv,
    b_send,
    b_recv,
    site_a_send,
    site_a_recv,
    site_b_send,
    site_b_recv,
):
    len_size, xs_size = sizes
    count = len_size * xs_size
    at_len, at_xs = lax.axis_index("len"), lax.axis_index("xs")
    me = at_len * xs_size + at_xs
    left, right = lax.rem(me + count - 1, count), lax.rem(me + 1, count)
    place = lambda i: (i // xs_size, lax.rem(i, xs_size))
    group_a = [(at_len, lax.rem(at_xs + k, xs_size)) for k in range(1, xs_size)]
    group_b = [(lax.rem(at_len + k, len_size), at_xs) for k in range(1, len_size)]

    def load(d, carry):
        for c in range(3):
            pltpu.make_async_copy(
                b_ref.at[c, pl.ds(d * NS, NS)],
                v0.at[c, pl.ds((d + 1) * PITCH, NS)],
                in_sem.at[c],
            ).start()
        return carry

    lax.fori_loop(0, DEPTH, load, 0)
    pltpu.make_async_copy(mass_ref, mass, in_sem.at[3]).start()

    barrier = pltpu.get_barrier_semaphore()
    partners = [place(left), place(right)] + group_b + group_a
    for partner in partners:
        pl.semaphore_signal(barrier, inc=1, device_id=partner, device_id_type=MESH)

    for c in range(4):
        if c < 3:
            pltpu.make_async_copy(
                b_ref.at[c], v0.at[c, pl.ds(0, DEPTH * NS)], in_sem.at[c]
            ).wait()
        else:
            pltpu.make_async_copy(mass_ref, mass, in_sem.at[3]).wait()

        def edges(i, carry, c=c):
            for j in range(4):
                t = i * 4 + j
                if c < 3:
                    tile = jnp.concatenate(
                        [v0[c, pl.ds((2 * t + 1 + e) * PITCH, NS)] for e in range(2)], axis=0
                    )
                else:
                    tile = mass[pl.ds(t * LANES, LANES)]
                turned = tile.T
                at = c * PAIRS + t
                pitch = 4 * PAIRS
                near_left[pl.ds(LANDED + at, 8, stride=pitch), :] = turned[0:8]
                near_left[pl.ds(LANDED + 8 * pitch + at, 4, stride=pitch), :] = turned[8:12]
                near_right[pl.ds(at, 4, stride=pitch), :] = turned[LANES - 12 : LANES - 8]
                near_right[pl.ds(4 * pitch + at, 8, stride=pitch), :] = turned[LANES - 8 :]
            return carry

        lax.fori_loop(0, PAIRS // 4, edges, 0)

    pl.semaphore_wait(barrier, len(partners))
    middle = pl.ds(LANDED, LANDED)
    halos = [
        pltpu.make_async_remote_copy(
            src_ref=near_left.at[middle],
            dst_ref=near_right.at[pl.ds(2 * LANDED, LANDED)],
            send_sem=halo_send.at[0],
            recv_sem=halo_recv.at[0],
            device_id=place(left),
            device_id_type=MESH,
        ),
        pltpu.make_async_remote_copy(
            src_ref=near_right.at[middle],
            dst_ref=near_left.at[pl.ds(0, LANDED)],
            send_sem=halo_send.at[1],
            recv_sem=halo_recv.at[1],
            device_id=place(right),
            device_id_type=MESH,
        ),
    ]
    for copy in halos:
        copy.start()

    def guard(d, carry):
        row = (d + 1) * PITCH + NS
        for ref in (v0, v1, v2):
            for c in range(3):
                ref[c, pl.ds(row, 8)] = jnp.zeros((8, LANES), F32)
        w[pl.ds(row, 8)] = jnp.zeros((8, LANES), F32)
        return carry

    lax.fori_loop(0, DEPTH, guard, 0)
    for start in (0, (DEPTH + 1) * PITCH):
        for ref in (v0, v1, v2):
            for c in range(3):
                ref[c, pl.ds(start, PITCH)] = jnp.zeros((PITCH, LANES), F32)
        w[pl.ds(start, PITCH)] = jnp.zeros((PITCH, LANES), F32)
    for c in range(3):
        for ref in (v0, v1, v2):
            ref[c, pl.ds((DEPTH + 2) * PITCH, PITCH)] = jnp.zeros((PITCH, LANES), F32)

    has_left = jnp.where(me > 0, 1.0, 0.0).astype(F32)
    has_right = jnp.where(me < count - 1, 1.0, 0.0).astype(F32)
    low = lax.broadcasted_iota(jnp.int32, (8, LANES), 1) < LANES // 2

    def guard_strip(p, carry):
        row = p * SECTION + 8
        for ref in (x0, x1, x2):
            for c in range(3):
                ref[c, pl.ds(row, 8)] = jnp.zeros((8, LANES), F32)
        strip_w[pl.ds(row, 8)] = jnp.zeros((8, LANES), F32)
        valid[p] = jnp.where(
            low,
            jnp.where(p < HALO, has_left, 1.0),
            jnp.where(p >= 2 * HALO, has_right, 1.0),
        )
        return carry

    lax.fori_loop(0, WIDE, guard_strip, 0)

    def apply(source, target, last, dots):
        quarter = 0.25 * bulk_modulus

        def divergence(base, scale):
            first = source[0, pl.ds(base, NS)]
            along = pltpu.roll(first, LANES - 1, 1) - pltpu.roll(first, 1, 1)
            across = source[1, pl.ds(base + 1, NS)] - source[1, pl.ds(base - 1, NS)]
            depth = source[2, pl.ds(base + PITCH, NS)] - source[2, pl.ds(base - PITCH, NS)]
            return scale * (along + across + depth)

        w[pl.ds(PITCH, NS)] = divergence(PITCH, quarter)
        zero = jnp.zeros((8, LANES), F32)

        def body(d, sums):
            base = (d + 1) * PITCH
            heavy = mass[pl.ds(d * NS, NS)] + 6.0
            ahead = divergence(base + PITCH, jnp.where(d < DEPTH - 1, quarter, 0.0))
            local = w[pl.ds(base, NS)]
            beside = (
                w[pl.ds(base + 1, NS)] - w[pl.ds(base - 1, NS)],
                ahead - w[pl.ds(base - PITCH, NS)],
            )
            terms = [zero] * len(dots)
            for c in range(3):
                here = source[c, pl.ds(base, NS)]
                if c == 0:
                    swept = pltpu.roll(here + local, LANES - 1, 1) + pltpu.roll(
                        here - local, 1, 1
                    )
                else:
                    swept = (
                        pltpu.roll(here, LANES - 1, 1)
                        + pltpu.roll(here, 1, 1)
                        + beside[c - 1]
                    )
                image = heavy * here
                image = image - (
                    source[c, pl.ds(base + 1, NS)] + source[c, pl.ds(base - 1, NS)]
                )
                image = image - (
                    source[c, pl.ds(base + PITCH, NS)] + source[c, pl.ds(base - PITCH, NS)]
                )
                image = image - swept
                if last:
                    target[c, pl.ds(d * NS, NS)] = image
                else:
                    target[c, pl.ds(base, NS)] = image
                for n, kind in enumerate(dots):
                    terms[n] = terms[n] + fold(
                        {"vv": here * here, "vi": here * image, "ii": image * image}[kind]
                    )
            w[pl.ds(base + PITCH, NS)] = ahead
            return tuple(s + t for s, t in zip(sums, terms))

        return lax.fori_loop(0, DEPTH, body, (zero,) * len(dots), unroll=UNROLL)

    mu0, mu1, mu2 = apply(v0, v1, False, ("vv", "vi", "ii"))
    mu3, mu4 = apply(v1, v2, False, ("vi", "ii"))
    (mu5,) = apply(v2, out3_ref, True, ("vi",))
    lane = lax.broadcasted_iota(jnp.int32, (8, LANES), 1)
    inner = (lane >= HALO) & (lane < LANES - HALO)
    moments = tuple(jnp.where(inner, mu, 0.0) for mu in (mu0, mu1, mu2, mu3, mu4, mu5))
    hits = bearing_hits(bearing_ends(spans_ref[...]), me * LANES)
    for s in range(2):
        hit[s] = hits[s]

    half = LANES // 2
    for copy in halos:
        copy.wait_recv()

    def mix(first, second):
        turned = pltpu.roll(jnp.where(low, second, first), half, 1)
        return jnp.where(low, first, turned), jnp.where(low, turned, second)

    def gather(p, carry):
        for c in range(4):
            at = pl.ds(pl.multiple_of((p * 4 + c) * PAIRS, 8), PAIRS)
            even, odd = mix(near_left[at], near_right[at])
            for part, value in ((0, even), (16, odd)):
                to = pl.ds(pl.multiple_of(p * SECTION + part, 8), 8)
                if c < 3:
                    x0[c, to] = value * valid[p]
                else:
                    strip_mass[to] = value
        return carry

    lax.fori_loop(0, WIDE, gather, 0, unroll=6)

    across_at = lax.rem(lax.broadcasted_iota(jnp.int32, (8, LANES), 1), half)

    def after(x):
        return jnp.where(across_at == half - 1, 0.0, pltpu.roll(x, LANES - 1, 1))

    def before(x):
        return jnp.where(across_at == 0, 0.0, pltpu.roll(x, 1, 1))

    def rows(ref, row):
        return ref[pl.ds(row, 8)], ref[pl.ds(row + 16, 8)]

    def beside(ref, row, pair):
        even, odd = pair
        return (odd, ref[pl.ds(row + 15, 8)]), (ref[pl.ds(row + 1, 8)], even)

    zero = jnp.zeros((8, LANES), F32)
    sums = (zero,) * 6
    xs = (x0, x1, x2, x3)
    for k in range(3):
        source, target = xs[k], xs[k + 1]

        def strip_divergence(i, carry, k=k, source=source):
            p = i + 2 * k + 1
            row = p * SECTION
            first, second = rows(source.at[0], row - SECTION), rows(source.at[0], row + SECTION)
            middle = rows(source.at[1], row)
            third = beside(source.at[2], row, rows(source.at[2], row))
            for e in range(2):
                strip_w[pl.ds(row + 16 * e, 8)] = (
                    (0.25 * bulk_modulus)
                    * (
                        (second[e] - first[e])
                        + (after(middle[e]) - before(middle[e]))
                        + (third[e][0] - third[e][1])
                    )
                    * valid[p]
                )
            return carry

        lax.fori_loop(0, WIDE - 2 - 4 * k, strip_divergence, 0, unroll=4)

        def strip_image(i, sums, k=k, source=source, target=target):
            p = i + 2 * k + 2
            row = p * SECTION
            heavy = rows(strip_mass, row)
            local = rows(strip_w, row)
            around = rows(strip_w, row - SECTION), rows(strip_w, row + SECTION)
            upright = beside(strip_w, row, local)
            images, heres = [], []
            for c in range(3):
                ref = source.at[c]
                here = rows(ref, row)
                along = rows(ref, row - SECTION), rows(ref, row + SECTION)
                depth = beside(ref, row, here)
                for e in range(2):
                    image = (heavy[e] + 6.0) * here[e] - (along[0][e] + along[1][e])
                    image = image - (depth[e][0] + depth[e][1])
                    if c == 1:
                        image = image - (after(here[e] + local[e]) + before(here[e] - local[e]))
                    else:
                        image = image - (after(here[e]) + before(here[e]))
                    if c == 0:
                        image = image - (around[1][e] - around[0][e])
                    elif c == 2:
                        image = image - (upright[e][0] - upright[e][1])
                    images.append(image * valid[p])
                    heres.append(here[e])
            sums = list(sums)
            for n, (image, here) in enumerate(zip(images, heres)):
                at = pl.ds(row + 16 * (n % 2), 8)
                target[n // 2, at] = image
                if k == 2:
                    z0, z1 = x0[n // 2, at], x1[n // 2, at]
                    for m, (p0, p1) in enumerate(
                        ((z0, z0), (z0, z1), (z1, z1), (z1, here), (here, here), (here, image))
                    ):
                        sums[m] = sums[m] + p0 * p1
            return tuple(sums)

        sums = lax.fori_loop(0, WIDE - 4 - 4 * k, strip_image, sums, unroll=2)
    strips = sums

    def exchange(source, slots, partners, own, send_sems, recv_sems):
        copies = []
        for k, partner in enumerate(partners):
            copy = pltpu.make_async_remote_copy(
                src_ref=source,
                dst_ref=slots.at[own],
                send_sem=send_sems.at[k],
                recv_sem=recv_sems.at[k],
                device_id=partner,
                device_id_type=MESH,
            )
            copy.start()
            copies.append(copy)
        slots[own] = source[...]
        return copies

    def tree(parts, join):
        while len(parts) > 1:
            joined = [join(parts[i], parts[i + 1]) for i in range(0, len(parts) - 1, 2)]
            parts = joined + parts[len(parts) - len(parts) % 2 :]
        return parts[0]

    def join(p, q):
        hi, more = two_sum(p[0], q[0])
        return hi, p[1] + q[1] + more

    def total(slots, number):
        return tree([(slots[i, 0:8], slots[i, 8:16]) for i in range(number)], join)

    head, rest = [], []
    for n in range(6):
        hi, lo = two_sum(moments[n], strips[n])
        for shift in (4, 2, 1):
            hi, more = two_sum(hi, pltpu.roll(hi, shift, 0))
            lo = lo + pltpu.roll(lo, shift, 0) + more
        head.append(hi[0:1])
        rest.append(lo[0:1])
    blank = [jnp.zeros((2, LANES), F32)]
    part_a[...] = jnp.concatenate(head + blank + rest + blank, axis=0)
    copies = list(halos)
    copies_a = exchange(part_a, slots_a, group_a, at_xs, a_send, a_recv)

    edge_rows = 16 * PAIRS
    lanes = lax.broadcasted_iota(jnp.int32, (LANES, LANES), 1)
    outer = (lanes < HALO) | (lanes >= LANES - HALO)
    mains = (v1, v2, None)
    outs = (out1_ref, out2_ref, out3_ref)

    def back_edges(i, carry, ks=(0, 1, 2)):
        for k in ks:
            for c in range(3):
                even, odd = rows(xs[k + 1].at[c], (i + HALO) * SECTION)
                first, second = mix(even, odd)
                slot = (k * 3 + c) * edge_rows
                back[pl.ds(slot + (8 + i) * PAIRS, PAIRS)] = first
                back[pl.ds(slot + (2 + i) * PAIRS, PAIRS)] = second
        return carry

    def merge(k, c, t):
        slot = (k * 3 + c) * edge_rows + t
        edge = jnp.concatenate(
            [
                back[pl.ds(slot + 8 * PAIRS, 8, stride=PAIRS), :],
                jnp.zeros((LANES - 16, LANES), F32),
                back[pl.ds(slot, 8, stride=PAIRS), :],
            ],
            axis=0,
        ).T
        if k < 2:
            main = jnp.concatenate(
                [mains[k][c, pl.ds((2 * t + 1 + e) * PITCH, NS)] for e in range(2)], axis=0
            )
        else:
            main = out3_ref[c, pl.ds(t * LANES, LANES)]
        outs[k][c, pl.ds(t * LANES, LANES)] = jnp.where(outer, edge, main)

    for slot in range(9):
        for r in (0, 1, 14, 15):
            back[pl.ds(slot * edge_rows + r * PAIRS, PAIRS)] = jnp.zeros((PAIRS, LANES), F32)
    lax.fori_loop(0, HALO, back_edges, 0)
    for k in (0, 1):
        for c in (0, 1):
            merge(k, c, 0)

    site = jnp.zeros((8, 2 * LANES), F32)
    for s, across in ((0, NS // 4), (1, 3 * NS // 4)):
        picked = [v0[c, pl.ds(PITCH + across, 1)] for c in (0, 1)]
        picked += [out1_ref[c, pl.ds(across, 1)] for c in (0, 1)]
        picked += [out2_ref[c, pl.ds(across, 1)] for c in (0, 1)]
        picked += [jnp.zeros((2, LANES), F32)]
        site = site + jnp.dot(
            jnp.concatenate(picked, axis=0),
            hit[s],
            precision=HIGHEST,
            preferred_element_type=F32,
        )
    site_a[...] = jnp.concatenate([site[:, :LANES], site[:, LANES:]], axis=0)
    copies_sa = exchange(site_a, site_slots_a, group_a, at_xs, site_a_send, site_a_recv)

    for copy in copies_a:
        copy.wait_recv()
    part_b[...] = jnp.concatenate(total(slots_a, xs_size), axis=0)
    copies_b = exchange(part_b, slots_b, group_b, at_len, b_send, b_recv)

    for copy in copies_sa:
        copy.wait_recv()
    site_b[...] = tree([site_slots_a[i] for i in range(xs_size)], jnp.add)
    copies_sb = exchange(site_b, site_slots_b, group_b, at_len, site_b_send, site_b_recv)

    for k, c in ((0, 2), (1, 2), (2, 0), (2, 1), (2, 2)):
        merge(k, c, 0)

    def merge_rest(t, carry):
        for k in range(3):
            for c in range(3):
                merge(k, c, t)
        return carry

    lax.fori_loop(1, PAIRS, merge_rest, 0)

    for copy in copies_b:
        copy.wait_recv()
    increment, solved = steps(*total(slots_b, len_size))
    coefficients_ref[...] = jnp.concatenate(
        list(increment) + list(solved) + [jnp.zeros((1, LANES), F32)], axis=0
    )
    for copy in copies_sb:
        copy.wait_recv()
    sites_ref[...] = tree([site_slots_b[i] for i in range(len_size)], jnp.add)
    for copy in halos + copies_a + copies_b + copies_sa + copies_sb:
        copy.wait_send()


def steps(hi, lo):
    for shift in (64, 32, 16, 8, 4, 2, 1):
        hi, more = two_sum(hi, pltpu.roll(hi, shift, 1))
        lo = lo + pltpu.roll(lo, shift, 1) + more
    hi, lo = two_sum(hi, lo)
    theta = jnp.round(hi[1:2] / hi[0:1] * 64.0) * (1.0 / 64.0)
    central = [hi[0:1]]
    for order in range(5):
        n = 5 - order
        big = hi[:n] * 4097.0
        upper = big - (big - hi[:n])
        lower = hi[:n] - upper
        value, more = two_sum(hi[1 : n + 1], -theta * upper)
        value, extra = two_sum(value, -theta * lower)
        low_part = lo[1 : n + 1] - theta * lo[:n] + (more + extra)
        hi, lo = two_sum(value, low_part)
        central.append(hi[0:1])
    scale = 1.0 / central[0]
    c = [x * scale for x in central]
    c1 = [c[i + 1] + theta * c[i] for i in range(5)]

    def form(p, moments):
        terms = None
        for i in range(len(p)):
            for j in range(i, len(p)):
                term = (1.0 if i == j else 2.0) * (p[i] * p[j]) * moments[i + j]
                terms = term if terms is None else terms + term
        return terms

    one, zero = jnp.ones_like(theta), jnp.zeros_like(theta)
    left, ahead, norm = [one], [one], c[0]
    increment = [zero, zero, zero]
    for iteration in range(3):
        alpha = norm / form(ahead, c1)
        increment = [
            x + alpha * ahead[i] if i < len(ahead) else x for i, x in enumerate(increment)
        ]
        image = [theta * x for x in ahead] + [zero]
        image = [image[i] + (ahead[i - 1] if i else zero) for i in range(len(image))]
        left = left + [zero]
        left = [x - alpha * y for x, y in zip(left, image)]
        if iteration < 2:
            after = form(left, c)
            beta = after / norm
            ahead = ahead + [zero]
            ahead = [x + beta * y for x, y in zip(left, ahead)]
            norm = after
    x0, x1, x2 = increment
    r0, r1, r2, r3 = left
    increment = (x0 - theta * (x1 - theta * x2), x1 - 2.0 * theta * x2, x2)
    solved = (
        r0 - theta * (r1 - theta * (r2 - theta * r3)),
        r1 - theta * (2.0 * r2 - 3.0 * theta * r3),
        r2 - 3.0 * theta * r3,
        r3,
    )
    return increment, solved


def finish_kernel(
    b_ref,
    v1_ref,
    v2_ref,
    v3_ref,
    coefficients_ref,
    sites_ref,
    spans_ref,
    stick_ref,
    load_ref,
    prior_ref,
    inc_ref,
    res_ref,
    friction_ref,
    b,
    x,
    r,
    in_sem,
    out_sem,
):
    loads = [pltpu.make_async_copy(b_ref.at[c], b.at[c], in_sem.at[c]) for c in range(3)]
    for copy in loads:
        copy.start()
    me = lax.axis_index("len") * lax.axis_size("xs") + lax.axis_index("xs")
    row = lambda n: coefficients_ref[pl.ds(n, 1)]
    x0, x1, x2 = row(0), row(1), row(2)
    stores = []

    def combine(c, at):
        p0, p1, p2, p3 = b[c, at], v1_ref[c, at], v2_ref[c, at], v3_ref[c, at]
        x[c, at] = x0 * p0 + x1 * p1 + x2 * p2
        r[c, at] = row(3) * p0 + row(4) * p1 + row(5) * p2 + row(6) * p3

    def store(c, at):
        for ref, dst in ((x, inc_ref), (r, res_ref)):
            copy = pltpu.make_async_copy(ref.at[c, at], dst.at[c, at], out_sem.at[len(stores)])
            copy.start()
            stores.append(copy)

    rows = DEPTH * NS
    for c in range(3):
        loads[c].wait()
        for first, last in ((NS, rows // 2), (rows // 2, rows)):

            def body(i, carry, c=c, first=first):
                combine(c, pl.ds(pl.multiple_of(first + i * NS, NS), NS))
                return carry

            lax.fori_loop(0, (last - first) // NS, body, 0)
            store(c, pl.ds(first, last - first))

    wide = lambda a: jnp.concatenate([a, a], axis=1)
    site = jnp.concatenate([sites_ref[0:8], sites_ref[8:16]], axis=1)
    readout = wide(x0) * site[0:2] + wide(x1) * site[2:4] + wide(x2) * site[4:6]
    radius = jnp.where(stick_ref[...] == 1, static_friction, kinetic_friction) * load_ref[...]
    trial = prior_ref[...] + elastic_stiffness * readout
    magnitude = jnp.sqrt(trial[0:1] * trial[0:1] + trial[1:2] * trial[1:2])
    friction = trial * (radius / jnp.maximum(magnitude, radius))
    friction_ref[...] = friction
    force = friction + load_ref[...] / pendulum_radius * readout
    bearings = force.shape[1]
    forces = jnp.concatenate(
        [force, jnp.ones((1, bearings), F32), jnp.zeros((5, bearings), F32)], axis=0
    )
    hits = bearing_hits(bearing_ends(spans_ref[...]), me * LANES)
    placed = [
        lax.dot_general(
            forces,
            hit,
            (((1,), (1,)), ((), ())),
            precision=HIGHEST,
            preferred_element_type=F32,
        )
        for hit in hits
    ]
    for c in range(3):
        combine(c, pl.ds(0, NS))
        for s, across in ((0, NS // 4), (1, 3 * NS // 4)):
            at = pl.ds(across, 1)
            if c < 2:
                drop = placed[s][c : c + 1]
            else:
                drop = vertical_stiffness * x[c, at] * placed[s][2:3]
            r[c, at] = r[c, at] - drop
        store(c, pl.ds(0, NS))
    for copy in stores:
        copy.wait()


def shards(right_side, mass_field, span_lengths, stick_flags, normal_load, prior_friction):
    sizes = (lax.axis_size("len"), lax.axis_size("xs"))
    rows = DEPTH * NS
    field = (3, rows, LANES)
    b = right_side.reshape(field)
    mass = mass_field.reshape(rows, LANES)
    spans = span_lengths.reshape(1, -1)
    stick = stick_flags.reshape(1, -1)
    load = normal_load.reshape(1, -1)
    anywhere = pl.BlockSpec(memory_space=pl.ANY)
    vmem = pl.BlockSpec(memory_space=pltpu.VMEM)
    v1, v2, v3, coefficients, sites = pl.pallas_call(
        lambda *refs: krylov_kernel(sizes, *refs),
        name="krylov",
        out_shape=[pltpu.VMEM(field, F32)] * 3
        + [pltpu.VMEM((8, LANES), F32), pltpu.VMEM((16, LANES), F32)],
        in_specs=[anywhere, anywhere, vmem],
        out_specs=[vmem] * 5,
        scratch_shapes=[pltpu.VMEM((3, PADDED, LANES), F32)] * 3
        + [pltpu.VMEM((rows, LANES), F32), pltpu.VMEM((PADDED, LANES), F32)]
        + [pltpu.VMEM((3, STRIP, LANES), F32)] * 4
        + [pltpu.VMEM((STRIP, LANES), F32)] * 2
        + [pltpu.VMEM((OWN + LANDED, LANES), F32)] * 2
        + [
            pltpu.VMEM((WIDE, 8, LANES), F32),
            pltpu.VMEM((9 * 16 * PAIRS, LANES), F32),
            pltpu.VMEM((2, LANES, 2 * LANES), F32),
        ]
        + [pltpu.VMEM((16, LANES), F32)] * 2
        + [pltpu.VMEM((n, 16, LANES), F32) for n in (sizes[1], sizes[0])]
        + [pltpu.VMEM((16, LANES), F32)] * 2
        + [pltpu.VMEM((n, 16, LANES), F32) for n in (sizes[1], sizes[0])]
        + [
            pltpu.SemaphoreType.DMA((n,))
            for n in (4, 2, 2) + 2 * (sizes[1], sizes[1], sizes[0], sizes[0])
        ],
        compiler_params=pltpu.CompilerParams(
            collective_id=0, has_side_effects=True, vmem_limit_bytes=32 * 2**20
        ),
    )(b, mass, spans)
    increment, residual, friction = pl.pallas_call(
        finish_kernel,
        name="finish",
        out_shape=[
            jax.ShapeDtypeStruct(field, F32),
            jax.ShapeDtypeStruct(field, F32),
            jax.ShapeDtypeStruct(prior_friction.shape, F32),
        ],
        in_specs=[anywhere] + [vmem] * 9,
        out_specs=[anywhere, anywhere, vmem],
        scratch_shapes=[
            pltpu.VMEM(field, F32),
            pltpu.VMEM(field, F32),
            pltpu.VMEM(field, F32),
            pltpu.SemaphoreType.DMA((3,)),
            pltpu.SemaphoreType.DMA((18,)),
        ],
        compiler_params=pltpu.CompilerParams(vmem_limit_bytes=24 * 2**20),
    )(b, v1, v2, v3, coefficients, sites, spans, stick, load, prior_friction)
    return (
        increment.reshape(right_side.shape),
        residual.reshape(right_side.shape),
        friction,
    )


def solution(mesh):
    along = ("len", "xs")
    in_specs = (P(None, None, None, along), P(None, None, along), P(), P(), P(), P())
    out_specs = (P(None, None, None, along), P(None, None, None, along), P())
    return jax.shard_map(shards, mesh=mesh, in_specs=in_specs, out_specs=out_specs, check_vma=False)
```

```python
import jax
import jax.numpy as jnp
from jax import lax
from jax.experimental import pallas as pl
from jax.experimental.pallas import tpu as pltpu
from jax.sharding import PartitionSpec as P

shear_modulus = 1.0
bulk_modulus = 1.5
elastic_stiffness = 8.0
pendulum_radius = 4.0
vertical_stiffness = 5.0
static_friction = 0.6
kinetic_friction = 0.45

DEPTH = 16
NS = 64
LANES = 128
PITCH = NS + 8
PADDED = (DEPTH + 3) * PITCH
HALO = 6
PAIRS = DEPTH * NS // LANES
WIDE = 3 * HALO
SECTION = 24
STRIP = WIDE * SECTION
OWN = 2 * HALO * 4 * PAIRS
LANDED = HALO * 4 * PAIRS

UNROLL = 2

MESH = pl.DeviceIdType.MESH
HIGHEST = lax.Precision.HIGHEST
F32 = jnp.float32


def two_sum(a, b):
    s = a + b
    t = s - a
    return s, (a - (s - t)) + (b - t)


def fold(block):
    return jnp.sum(block.reshape(block.shape[0] // 8, 8, LANES), axis=0)


def bearing_ends(spans):
    piers = spans.shape[1]
    upto = (
        lax.broadcasted_iota(jnp.int32, (piers, 2 * piers), 0)
        <= lax.broadcasted_iota(jnp.int32, (piers, 2 * piers), 1) // 2
    ).astype(F32)
    return (
        jnp.dot(
            jnp.broadcast_to(spans.astype(F32), (8, piers)),
            upto,
            precision=HIGHEST,
            preferred_element_type=F32,
        )[0:1]
        - 1.0
    )


def bearing_hits(ends, start):
    bearings = ends.shape[1]
    along = lax.broadcasted_iota(jnp.int32, (LANES, bearings), 0) + start
    side = lax.rem(lax.broadcasted_iota(jnp.int32, (LANES, bearings), 1), 2)
    here = along.astype(F32) == ends
    return [jnp.where(here & (side == s), 1.0, 0.0).astype(F32) for s in range(2)]


def krylov_kernel(
    sizes,
    b_ref,
    mass_ref,
    spans_ref,
    out0_ref,
    out1_ref,
    out2_ref,
    out3_ref,
    coefficients_ref,
    sites_ref,
    v0,
    v1,
    v2,
    mass,
    w,
    x0,
    x1,
    x2,
    x3,
    strip_mass,
    strip_w,
    near_left,
    near_right,
    valid,
    back,
    hit,
    spans,
    part_a,
    part_b,
    slots_a,
    slots_b,
    site_a,
    site_b,
    site_slots_a,
    site_slots_b,
    in_sem,
    halo_send,
    halo_recv,
    a_send,
    a_recv,
    b_send,
    b_recv,
    site_a_send,
    site_a_recv,
    site_b_send,
    site_b_recv,
):
    len_size, xs_size = sizes
    count = len_size * xs_size
    at_len, at_xs = lax.axis_index("len"), lax.axis_index("xs")
    me = at_len * xs_size + at_xs
    left, right = lax.rem(me + count - 1, count), lax.rem(me + 1, count)
    place = lambda i: (i // xs_size, lax.rem(i, xs_size))
    group_a = [(at_len, lax.rem(at_xs + k, xs_size)) for k in range(1, xs_size)]
    group_b = [(lax.rem(at_len + k, len_size), at_xs) for k in range(1, len_size)]

    def load(d, carry):
        for c in range(3):
            pltpu.make_async_copy(
                b_ref.at[c, pl.ds(d * NS, NS)],
                v0.at[c, pl.ds((d + 1) * PITCH, NS)],
                in_sem.at[c],
            ).start()
        return carry

    lax.fori_loop(0, DEPTH, load, 0)
    pltpu.make_async_copy(mass_ref, mass, in_sem.at[3]).start()
    spans_copy = pltpu.make_async_copy(spans_ref, spans, in_sem.at[4])
    spans_copy.start()
    whole_copy = pltpu.make_async_copy(b_ref, out0_ref, in_sem.at[5])

    barrier = pltpu.get_barrier_semaphore()
    partners = [place(left), place(right)] + group_b + group_a
    for partner in partners:
        pl.semaphore_signal(barrier, inc=1, device_id=partner, device_id_type=MESH)

    for c in range(4):
        if c < 3:
            pltpu.make_async_copy(
                b_ref.at[c], v0.at[c, pl.ds(0, DEPTH * NS)], in_sem.at[c]
            ).wait()
        else:
            pltpu.make_async_copy(mass_ref, mass, in_sem.at[3]).wait()

        def edges(i, carry, c=c):
            for j in range(4):
                t = i * 4 + j
                if c < 3:
                    tile = jnp.concatenate(
                        [v0[c, pl.ds((2 * t + 1 + e) * PITCH, NS)] for e in range(2)], axis=0
                    )
                else:
                    tile = mass[pl.ds(t * LANES, LANES)]
                turned = tile.T
                at = c * PAIRS + t
                pitch = 4 * PAIRS
                near_left[pl.ds(LANDED + at, 8, stride=pitch), :] = turned[0:8]
                near_left[pl.ds(LANDED + 8 * pitch + at, 4, stride=pitch), :] = turned[8:12]
                near_right[pl.ds(at, 4, stride=pitch), :] = turned[LANES - 12 : LANES - 8]
                near_right[pl.ds(4 * pitch + at, 8, stride=pitch), :] = turned[LANES - 8 :]
            return carry

        lax.fori_loop(0, PAIRS // 4, edges, 0)

    pl.semaphore_wait(barrier, len(partners))
    middle = pl.ds(LANDED, LANDED)
    halos = [
        pltpu.make_async_remote_copy(
            src_ref=near_left.at[middle],
            dst_ref=near_right.at[pl.ds(2 * LANDED, LANDED)],
            send_sem=halo_send.at[0],
            recv_sem=halo_recv.at[0],
            device_id=place(left),
            device_id_type=MESH,
        ),
        pltpu.make_async_remote_copy(
            src_ref=near_right.at[middle],
            dst_ref=near_left.at[pl.ds(0, LANDED)],
            send_sem=halo_send.at[1],
            recv_sem=halo_recv.at[1],
            device_id=place(right),
            device_id_type=MESH,
        ),
    ]
    for copy in halos:
        copy.start()

    whole_copy.start()

    def guard(d, carry):
        row = (d + 1) * PITCH + NS
        for ref in (v0, v1, v2):
            for c in range(3):
                ref[c, pl.ds(row, 8)] = jnp.zeros((8, LANES), F32)
        w[pl.ds(row, 8)] = jnp.zeros((8, LANES), F32)
        return carry

    lax.fori_loop(0, DEPTH, guard, 0)
    for start in (0, (DEPTH + 1) * PITCH):
        for ref in (v0, v1, v2):
            for c in range(3):
                ref[c, pl.ds(start, PITCH)] = jnp.zeros((PITCH, LANES), F32)
        w[pl.ds(start, PITCH)] = jnp.zeros((PITCH, LANES), F32)
    for c in range(3):
        for ref in (v0, v1, v2):
            ref[c, pl.ds((DEPTH + 2) * PITCH, PITCH)] = jnp.zeros((PITCH, LANES), F32)

    has_left = jnp.where(me > 0, 1.0, 0.0).astype(F32)
    has_right = jnp.where(me < count - 1, 1.0, 0.0).astype(F32)
    low = lax.broadcasted_iota(jnp.int32, (8, LANES), 1) < LANES // 2

    def guard_strip(p, carry):
        row = p * SECTION + 8
        for ref in (x0, x1, x2):
            for c in range(3):
                ref[c, pl.ds(row, 8)] = jnp.zeros((8, LANES), F32)
        strip_w[pl.ds(row, 8)] = jnp.zeros((8, LANES), F32)
        valid[p] = jnp.where(
            low,
            jnp.where(p < HALO, has_left, 1.0),
            jnp.where(p >= 2 * HALO, has_right, 1.0),
        )
        return carry

    lax.fori_loop(0, WIDE, guard_strip, 0)

    def apply(source, target, last, dots):
        quarter = 0.25 * bulk_modulus

        def divergence(base, scale):
            first = source[0, pl.ds(base, NS)]
            along = pltpu.roll(first, LANES - 1, 1) - pltpu.roll(first, 1, 1)
            across = source[1, pl.ds(base + 1, NS)] - source[1, pl.ds(base - 1, NS)]
            depth = source[2, pl.ds(base + PITCH, NS)] - source[2, pl.ds(base - PITCH, NS)]
            return scale * (along + across + depth)

        w[pl.ds(PITCH, NS)] = divergence(PITCH, quarter)
        zero = jnp.zeros((8, LANES), F32)

        def body(d, sums):
            base = (d + 1) * PITCH
            heavy = mass[pl.ds(d * NS, NS)] + 6.0
            ahead = divergence(base + PITCH, jnp.where(d < DEPTH - 1, quarter, 0.0))
            local = w[pl.ds(base, NS)]
            beside = (
                w[pl.ds(base + 1, NS)] - w[pl.ds(base - 1, NS)],
                ahead - w[pl.ds(base - PITCH, NS)],
            )
            terms = [zero] * len(dots)
            for c in range(3):
                here = source[c, pl.ds(base, NS)]
                if c == 0:
                    swept = pltpu.roll(here + local, LANES - 1, 1) + pltpu.roll(
                        here - local, 1, 1
                    )
                else:
                    swept = (
                        pltpu.roll(here, LANES - 1, 1)
                        + pltpu.roll(here, 1, 1)
                        + beside[c - 1]
                    )
                image = heavy * here
                image = image - (
                    source[c, pl.ds(base + 1, NS)] + source[c, pl.ds(base - 1, NS)]
                )
                image = image - (
                    source[c, pl.ds(base + PITCH, NS)] + source[c, pl.ds(base - PITCH, NS)]
                )
                image = image - swept
                if last:
                    target[c, pl.ds(d * NS, NS)] = image
                else:
                    target[c, pl.ds(base, NS)] = image
                for n, kind in enumerate(dots):
                    terms[n] = terms[n] + fold(
                        {"vv": here * here, "vi": here * image, "ii": image * image}[kind]
                    )
            w[pl.ds(base + PITCH, NS)] = ahead
            return tuple(s + t for s, t in zip(sums, terms))

        return lax.fori_loop(0, DEPTH, body, (zero,) * len(dots), unroll=UNROLL)

    mu0, mu1, mu2 = apply(v0, v1, False, ("vv", "vi", "ii"))
    mu3, mu4 = apply(v1, v2, False, ("vi", "ii"))
    (mu5,) = apply(v2, out3_ref, True, ("vi",))
    lane = lax.broadcasted_iota(jnp.int32, (8, LANES), 1)
    inner = (lane >= HALO) & (lane < LANES - HALO)
    moments = tuple(jnp.where(inner, mu, 0.0) for mu in (mu0, mu1, mu2, mu3, mu4, mu5))
    spans_copy.wait()
    whole_copy.wait()
    hits = bearing_hits(bearing_ends(spans[...]), me * LANES)
    for s in range(2):
        hit[s] = hits[s]

    half = LANES // 2
    for copy in halos:
        copy.wait_recv()

    def mix(first, second):
        turned = pltpu.roll(jnp.where(low, second, first), half, 1)
        return jnp.where(low, first, turned), jnp.where(low, turned, second)

    def gather(p, carry):
        for c in range(4):
            at = pl.ds(pl.multiple_of((p * 4 + c) * PAIRS, 8), PAIRS)
            even, odd = mix(near_left[at], near_right[at])
            for part, value in ((0, even), (16, odd)):
                to = pl.ds(pl.multiple_of(p * SECTION + part, 8), 8)
                if c < 3:
                    x0[c, to] = value * valid[p]
                else:
                    strip_mass[to] = value
        return carry

    lax.fori_loop(0, WIDE, gather, 0, unroll=6)

    across_at = lax.rem(lax.broadcasted_iota(jnp.int32, (8, LANES), 1), half)

    def after(x):
        return jnp.where(across_at == half - 1, 0.0, pltpu.roll(x, LANES - 1, 1))

    def before(x):
        return jnp.where(across_at == 0, 0.0, pltpu.roll(x, 1, 1))

    def rows(ref, row):
        return ref[pl.ds(row, 8)], ref[pl.ds(row + 16, 8)]

    def beside(ref, row, pair):
        even, odd = pair
        return (odd, ref[pl.ds(row + 15, 8)]), (ref[pl.ds(row + 1, 8)], even)

    zero = jnp.zeros((8, LANES), F32)
    sums = (zero,) * 6
    xs = (x0, x1, x2, x3)
    for k in range(3):
        source, target = xs[k], xs[k + 1]

        def strip_divergence(i, carry, k=k, source=source):
            p = i + 2 * k + 1
            row = p * SECTION
            first, second = rows(source.at[0], row - SECTION), rows(source.at[0], row + SECTION)
            middle = rows(source.at[1], row)
            third = beside(source.at[2], row, rows(source.at[2], row))
            for e in range(2):
                strip_w[pl.ds(row + 16 * e, 8)] = (
                    (0.25 * bulk_modulus)
                    * (
                        (second[e] - first[e])
                        + (after(middle[e]) - before(middle[e]))
                        + (third[e][0] - third[e][1])
                    )
                    * valid[p]
                )
            return carry

        lax.fori_loop(0, WIDE - 2 - 4 * k, strip_divergence, 0, unroll=4)

        def strip_image(i, sums, k=k, source=source, target=target):
            p = i + 2 * k + 2
            row = p * SECTION
            heavy = rows(strip_mass, row)
            local = rows(strip_w, row)
            around = rows(strip_w, row - SECTION), rows(strip_w, row + SECTION)
            upright = beside(strip_w, row, local)
            images, heres = [], []
            for c in range(3):
                ref = source.at[c]
                here = rows(ref, row)
                along = rows(ref, row - SECTION), rows(ref, row + SECTION)
                depth = beside(ref, row, here)
                for e in range(2):
                    image = (heavy[e] + 6.0) * here[e] - (along[0][e] + along[1][e])
                    image = image - (depth[e][0] + depth[e][1])
                    if c == 1:
                        image = image - (after(here[e] + local[e]) + before(here[e] - local[e]))
                    else:
                        image = image - (after(here[e]) + before(here[e]))
                    if c == 0:
                        image = image - (around[1][e] - around[0][e])
                    elif c == 2:
                        image = image - (upright[e][0] - upright[e][1])
                    images.append(image * valid[p])
                    heres.append(here[e])
            sums = list(sums)
            for n, (image, here) in enumerate(zip(images, heres)):
                at = pl.ds(row + 16 * (n % 2), 8)
                target[n // 2, at] = image
                if k == 2:
                    z0, z1 = x0[n // 2, at], x1[n // 2, at]
                    for m, (p0, p1) in enumerate(
                        ((z0, z0), (z0, z1), (z1, z1), (z1, here), (here, here), (here, image))
                    ):
                        sums[m] = sums[m] + p0 * p1
            return tuple(sums)

        sums = lax.fori_loop(0, WIDE - 4 - 4 * k, strip_image, sums, unroll=2)
    strips = sums

    def exchange(source, slots, partners, own, send_sems, recv_sems):
        copies = []
        for k, partner in enumerate(partners):
            copy = pltpu.make_async_remote_copy(
                src_ref=source,
                dst_ref=slots.at[own],
                send_sem=send_sems.at[k],
                recv_sem=recv_sems.at[k],
                device_id=partner,
                device_id_type=MESH,
            )
            copy.start()
            copies.append(copy)
        slots[own] = source[...]
        return copies

    def tree(parts, join):
        while len(parts) > 1:
            joined = [join(parts[i], parts[i + 1]) for i in range(0, len(parts) - 1, 2)]
            parts = joined + parts[len(parts) - len(parts) % 2 :]
        return parts[0]

    def join(p, q):
        hi, more = two_sum(p[0], q[0])
        return hi, p[1] + q[1] + more

    def total(slots, number):
        return tree([(slots[i, 0:8], slots[i, 8:16]) for i in range(number)], join)

    head, rest = [], []
    for n in range(6):
        hi, lo = two_sum(moments[n], strips[n])
        for shift in (4, 2, 1):
            hi, more = two_sum(hi, pltpu.roll(hi, shift, 0))
            lo = lo + pltpu.roll(lo, shift, 0) + more
        head.append(hi[0:1])
        rest.append(lo[0:1])
    blank = [jnp.zeros((2, LANES), F32)]
    part_a[...] = jnp.concatenate(head + blank + rest + blank, axis=0)
    copies = list(halos)
    copies_a = exchange(part_a, slots_a, group_a, at_xs, a_send, a_recv)

    edge_rows = 16 * PAIRS
    lanes = lax.broadcasted_iota(jnp.int32, (LANES, LANES), 1)
    outer = (lanes < HALO) | (lanes >= LANES - HALO)
    mains = (v1, v2, None)
    outs = (out1_ref, out2_ref, out3_ref)

    def back_edges(i, carry, ks=(0, 1, 2)):
        for k in ks:
            for c in range(3):
                even, odd = rows(xs[k + 1].at[c], (i + HALO) * SECTION)
                first, second = mix(even, odd)
                slot = (k * 3 + c) * edge_rows
                back[pl.ds(slot + (8 + i) * PAIRS, PAIRS)] = first
                back[pl.ds(slot + (2 + i) * PAIRS, PAIRS)] = second
        return carry

    def merge(k, c, t):
        slot = (k * 3 + c) * edge_rows + t
        edge = jnp.concatenate(
            [
                back[pl.ds(slot + 8 * PAIRS, 8, stride=PAIRS), :],
                jnp.zeros((LANES - 16, LANES), F32),
                back[pl.ds(slot, 8, stride=PAIRS), :],
            ],
            axis=0,
        ).T
        if k < 2:
            main = jnp.concatenate(
                [mains[k][c, pl.ds((2 * t + 1 + e) * PITCH, NS)] for e in range(2)], axis=0
            )
        else:
            main = out3_ref[c, pl.ds(t * LANES, LANES)]
        outs[k][c, pl.ds(t * LANES, LANES)] = jnp.where(outer, edge, main)

    for slot in range(9):
        for r in (0, 1, 14, 15):
            back[pl.ds(slot * edge_rows + r * PAIRS, PAIRS)] = jnp.zeros((PAIRS, LANES), F32)
    lax.fori_loop(0, HALO, back_edges, 0)
    for k in (0, 1):
        for c in (0, 1):
            merge(k, c, 0)

    site = jnp.zeros((8, 2 * LANES), F32)
    for s, across in ((0, NS // 4), (1, 3 * NS // 4)):
        picked = [v0[c, pl.ds(PITCH + across, 1)] for c in (0, 1)]
        picked += [out1_ref[c, pl.ds(across, 1)] for c in (0, 1)]
        picked += [out2_ref[c, pl.ds(across, 1)] for c in (0, 1)]
        picked += [jnp.zeros((2, LANES), F32)]
        site = site + jnp.dot(
            jnp.concatenate(picked, axis=0),
            hit[s],
            precision=HIGHEST,
            preferred_element_type=F32,
        )
    site_a[...] = jnp.concatenate([site[:, :LANES], site[:, LANES:]], axis=0)
    copies_sa = exchange(site_a, site_slots_a, group_a, at_xs, site_a_send, site_a_recv)

    for copy in copies_a:
        copy.wait_recv()
    part_b[...] = jnp.concatenate(total(slots_a, xs_size), axis=0)
    copies_b = exchange(part_b, slots_b, group_b, at_len, b_send, b_recv)

    for copy in copies_sa:
        copy.wait_recv()
    site_b[...] = tree([site_slots_a[i] for i in range(xs_size)], jnp.add)
    copies_sb = exchange(site_b, site_slots_b, group_b, at_len, site_b_send, site_b_recv)

    for k, c in ((0, 2), (1, 2), (2, 0), (2, 1), (2, 2)):
        merge(k, c, 0)

    def merge_rest(t, carry):
        for k in range(3):
            for c in range(3):
                merge(k, c, t)
        return carry

    lax.fori_loop(1, PAIRS, merge_rest, 0)

    for copy in copies_b:
        copy.wait_recv()
    increment, solved = steps(*total(slots_b, len_size))
    coefficients_ref[...] = jnp.concatenate(
        list(increment) + list(solved) + [jnp.zeros((1, LANES), F32)], axis=0
    )
    for copy in copies_sb:
        copy.wait_recv()
    sites_ref[...] = tree([site_slots_b[i] for i in range(len_size)], jnp.add)
    for copy in halos + copies_a + copies_b + copies_sa + copies_sb:
        copy.wait_send()


def steps(hi, lo):
    for shift in (64, 32, 16, 8, 4, 2, 1):
        hi, more = two_sum(hi, pltpu.roll(hi, shift, 1))
        lo = lo + pltpu.roll(lo, shift, 1) + more
    hi, lo = two_sum(hi, lo)
    theta = jnp.round(hi[1:2] / hi[0:1] * 64.0) * (1.0 / 64.0)
    central = [hi[0:1]]
    for order in range(5):
        n = 5 - order
        big = hi[:n] * 4097.0
        upper = big - (big - hi[:n])
        lower = hi[:n] - upper
        value, more = two_sum(hi[1 : n + 1], -theta * upper)
        value, extra = two_sum(value, -theta * lower)
        low_part = lo[1 : n + 1] - theta * lo[:n] + (more + extra)
        hi, lo = two_sum(value, low_part)
        central.append(hi[0:1])
    scale = 1.0 / central[0]
    c = [x * scale for x in central]
    c1 = [c[i + 1] + theta * c[i] for i in range(5)]

    def form(p, moments):
        terms = None
        for i in range(len(p)):
            for j in range(i, len(p)):
                term = (1.0 if i == j else 2.0) * (p[i] * p[j]) * moments[i + j]
                terms = term if terms is None else terms + term
        return terms

    one, zero = jnp.ones_like(theta), jnp.zeros_like(theta)
    left, ahead, norm = [one], [one], c[0]
    increment = [zero, zero, zero]
    for iteration in range(3):
        alpha = norm / form(ahead, c1)
        increment = [
            x + alpha * ahead[i] if i < len(ahead) else x for i, x in enumerate(increment)
        ]
        image = [theta * x for x in ahead] + [zero]
        image = [image[i] + (ahead[i - 1] if i else zero) for i in range(len(image))]
        left = left + [zero]
        left = [x - alpha * y for x, y in zip(left, image)]
        if iteration < 2:
            after = form(left, c)
            beta = after / norm
            ahead = ahead + [zero]
            ahead = [x + beta * y for x, y in zip(left, ahead)]
            norm = after
    x0, x1, x2 = increment
    r0, r1, r2, r3 = left
    increment = (x0 - theta * (x1 - theta * x2), x1 - 2.0 * theta * x2, x2)
    solved = (
        r0 - theta * (r1 - theta * (r2 - theta * r3)),
        r1 - theta * (2.0 * r2 - 3.0 * theta * r3),
        r2 - 3.0 * theta * r3,
        r3,
    )
    return increment, solved


def finish_kernel(
    b_ref,
    v1_ref,
    v2_ref,
    v3_ref,
    coefficients_ref,
    sites_ref,
    spans_ref,
    stick_ref,
    load_ref,
    prior_ref,
    inc_ref,
    res_ref,
    friction_ref,
    x,
    r,
    out_sem,
):
    me = lax.axis_index("len") * lax.axis_size("xs") + lax.axis_index("xs")
    row = lambda n: coefficients_ref[pl.ds(n, 1)]
    x0, x1, x2 = row(0), row(1), row(2)
    stores = []

    def combine(c, at):
        p0, p1, p2, p3 = b_ref[c, at], v1_ref[c, at], v2_ref[c, at], v3_ref[c, at]
        x[c, at] = x0 * p0 + x1 * p1 + x2 * p2
        r[c, at] = row(3) * p0 + row(4) * p1 + row(5) * p2 + row(6) * p3

    def store(c, at):
        for ref, dst in ((x, inc_ref), (r, res_ref)):
            copy = pltpu.make_async_copy(ref.at[c, at], dst.at[c, at], out_sem.at[len(stores)])
            copy.start()
            stores.append(copy)

    rows = DEPTH * NS
    for c in range(3):
        for first, last in ((NS, rows // 2), (rows // 2, rows)):

            def body(i, carry, c=c, first=first):
                combine(c, pl.ds(pl.multiple_of(first + i * NS, NS), NS))
                return carry

            lax.fori_loop(0, (last - first) // NS, body, 0)
            store(c, pl.ds(first, last - first))

    wide = lambda a: jnp.concatenate([a, a], axis=1)
    site = jnp.concatenate([sites_ref[0:8], sites_ref[8:16]], axis=1)
    readout = wide(x0) * site[0:2] + wide(x1) * site[2:4] + wide(x2) * site[4:6]
    radius = jnp.where(stick_ref[...] == 1, static_friction, kinetic_friction) * load_ref[...]
    trial = prior_ref[...] + elastic_stiffness * readout
    magnitude = jnp.sqrt(trial[0:1] * trial[0:1] + trial[1:2] * trial[1:2])
    friction = trial * (radius / jnp.maximum(magnitude, radius))
    friction_ref[...] = friction
    force = friction + load_ref[...] / pendulum_radius * readout
    bearings = force.shape[1]
    forces = jnp.concatenate(
        [force, jnp.ones((1, bearings), F32), jnp.zeros((5, bearings), F32)], axis=0
    )
    hits = bearing_hits(bearing_ends(spans_ref[...]), me * LANES)
    placed = [
        lax.dot_general(
            forces,
            hit,
            (((1,), (1,)), ((), ())),
            precision=HIGHEST,
            preferred_element_type=F32,
        )
        for hit in hits
    ]
    for c in range(3):
        combine(c, pl.ds(0, NS))
        for s, across in ((0, NS // 4), (1, 3 * NS // 4)):
            at = pl.ds(across, 1)
            if c < 2:
                drop = placed[s][c : c + 1]
            else:
                drop = vertical_stiffness * x[c, at] * placed[s][2:3]
            r[c, at] = r[c, at] - drop
        store(c, pl.ds(0, NS))
    for copy in stores:
        copy.wait()


def shards(right_side, mass_field, span_lengths, stick_flags, normal_load, prior_friction):
    sizes = (lax.axis_size("len"), lax.axis_size("xs"))
    rows = DEPTH * NS
    field = (3, rows, LANES)
    b = right_side.reshape(field)
    mass = mass_field.reshape(rows, LANES)
    spans = span_lengths.reshape(1, -1)
    stick = stick_flags.reshape(1, -1)
    load = normal_load.reshape(1, -1)
    anywhere = pl.BlockSpec(memory_space=pl.ANY)
    hbm = pl.BlockSpec(memory_space=pltpu.HBM)
    far = lambda a: pltpu.with_memory_space_constraint(a, pltpu.HBM)
    vmem = pl.BlockSpec(memory_space=pltpu.VMEM)
    v0, v1, v2, v3, coefficients, sites = pl.pallas_call(
        lambda *refs: krylov_kernel(sizes, *refs),
        name="krylov",
        out_shape=[pltpu.VMEM(field, F32)] * 4
        + [pltpu.VMEM((8, LANES), F32), pltpu.VMEM((16, LANES), F32)],
        in_specs=[hbm] * 3,
        out_specs=[vmem] * 6,
        scratch_shapes=[pltpu.VMEM((3, PADDED, LANES), F32)] * 3
        + [pltpu.VMEM((rows, LANES), F32), pltpu.VMEM((PADDED, LANES), F32)]
        + [pltpu.VMEM((3, STRIP, LANES), F32)] * 4
        + [pltpu.VMEM((STRIP, LANES), F32)] * 2
        + [pltpu.VMEM((OWN + LANDED, LANES), F32)] * 2
        + [
            pltpu.VMEM((WIDE, 8, LANES), F32),
            pltpu.VMEM((9 * 16 * PAIRS, LANES), F32),
            pltpu.VMEM((2, LANES, 2 * LANES), F32),
            pltpu.VMEM(spans.shape, jnp.int32),
        ]
        + [pltpu.VMEM((16, LANES), F32)] * 2
        + [pltpu.VMEM((n, 16, LANES), F32) for n in (sizes[1], sizes[0])]
        + [pltpu.VMEM((16, LANES), F32)] * 2
        + [pltpu.VMEM((n, 16, LANES), F32) for n in (sizes[1], sizes[0])]
        + [
            pltpu.SemaphoreType.DMA((n,))
            for n in (6, 2, 2) + 2 * (sizes[1], sizes[1], sizes[0], sizes[0])
        ],
        compiler_params=pltpu.CompilerParams(
            collective_id=0, has_side_effects=True, vmem_limit_bytes=32 * 2**20
        ),
    )(far(b), far(mass), far(spans))
    increment, residual, friction = pl.pallas_call(
        finish_kernel,
        name="finish",
        out_shape=[
            jax.ShapeDtypeStruct(field, F32),
            jax.ShapeDtypeStruct(field, F32),
            jax.ShapeDtypeStruct(prior_friction.shape, F32),
        ],
        in_specs=[vmem] * 10,
        out_specs=[anywhere, anywhere, vmem],
        scratch_shapes=[
            pltpu.VMEM(field, F32),
            pltpu.VMEM(field, F32),
            pltpu.SemaphoreType.DMA((18,)),
        ],
        compiler_params=pltpu.CompilerParams(vmem_limit_bytes=24 * 2**20),
    )(v0, v1, v2, v3, coefficients, sites, spans, stick, load, prior_friction)
    return (
        increment.reshape(right_side.shape),
        residual.reshape(right_side.shape),
        friction,
    )


def solution(mesh):
    along = ("len", "xs")
    in_specs = (P(None, None, None, along), P(None, None, along), P(), P(), P(), P())
    out_specs = (P(None, None, None, along), P(None, None, None, along), P())
    return jax.shard_map(shards, mesh=mesh, in_specs=in_specs, out_specs=out_specs, check_vma=False)
```

```python
import jax
import jax.numpy as jnp
from jax import lax
from jax.experimental import pallas as pl
from jax.experimental.pallas import tpu as pltpu
from jax.sharding import PartitionSpec as P

shear_modulus = 1.0
bulk_modulus = 1.5
elastic_stiffness = 8.0
pendulum_radius = 4.0
vertical_stiffness = 5.0
static_friction = 0.6
kinetic_friction = 0.45

DEPTH = 16
NS = 64
LANES = 128
PITCH = NS + 8
PADDED = (DEPTH + 3) * PITCH
HALO = 6
PAIRS = DEPTH * NS // LANES
WIDE = 3 * HALO
SECTION = 24
STRIP = WIDE * SECTION
OWN = 2 * HALO * 4 * PAIRS
LANDED = HALO * 4 * PAIRS

UNROLL = 4
DIV_UNROLL = (16, 12, 8)
IMG_UNROLL = (7, 5, 6)

MESH = pl.DeviceIdType.MESH
HIGHEST = lax.Precision.HIGHEST
F32 = jnp.float32


def two_sum(a, b):
    s = a + b
    t = s - a
    return s, (a - (s - t)) + (b - t)


def fold(block):
    return jnp.sum(block.reshape(block.shape[0] // 8, 8, LANES), axis=0)


def bearing_ends(spans):
    piers = spans.shape[1]
    upto = (
        lax.broadcasted_iota(jnp.int32, (piers, 2 * piers), 0)
        <= lax.broadcasted_iota(jnp.int32, (piers, 2 * piers), 1) // 2
    ).astype(F32)
    return (
        jnp.dot(
            jnp.broadcast_to(spans.astype(F32), (8, piers)),
            upto,
            precision=HIGHEST,
            preferred_element_type=F32,
        )[0:1]
        - 1.0
    )


def bearing_hits(ends, start):
    bearings = ends.shape[1]
    along = lax.broadcasted_iota(jnp.int32, (LANES, bearings), 0) + start
    side = lax.rem(lax.broadcasted_iota(jnp.int32, (LANES, bearings), 1), 2)
    here = along.astype(F32) == ends
    return [jnp.where(here & (side == s), 1.0, 0.0).astype(F32) for s in range(2)]


def krylov_kernel(
    sizes,
    b_ref,
    mass_ref,
    spans_ref,
    out0_ref,
    out1_ref,
    out2_ref,
    out3_ref,
    coefficients_ref,
    sites_ref,
    v0,
    v1,
    v2,
    mass,
    w,
    x0,
    x1,
    x2,
    x3,
    strip_mass,
    strip_w,
    near_left,
    near_right,
    valid,
    back,
    hit,
    spans,
    part_a,
    part_b,
    slots_a,
    slots_b,
    site_a,
    site_b,
    site_slots_a,
    site_slots_b,
    in_sem,
    halo_send,
    halo_recv,
    a_send,
    a_recv,
    b_send,
    b_recv,
    site_a_send,
    site_a_recv,
    site_b_send,
    site_b_recv,
):
    len_size, xs_size = sizes
    count = len_size * xs_size
    at_len, at_xs = lax.axis_index("len"), lax.axis_index("xs")
    me = at_len * xs_size + at_xs
    left, right = lax.rem(me + count - 1, count), lax.rem(me + 1, count)
    place = lambda i: (i // xs_size, lax.rem(i, xs_size))
    group_a = [(at_len, lax.rem(at_xs + k, xs_size)) for k in range(1, xs_size)]
    group_b = [(lax.rem(at_len + k, len_size), at_xs) for k in range(1, len_size)]

    spans_copy = pltpu.make_async_copy(spans_ref, spans, in_sem.at[4])
    spans_copy.start()
    def load(d, carry):
        for c in range(3):
            pltpu.make_async_copy(
                b_ref.at[c, pl.ds(d * NS, NS)],
                v0.at[c, pl.ds((d + 1) * PITCH, NS)],
                in_sem.at[c],
            ).start()
        return carry

    lax.fori_loop(0, DEPTH, load, 0)
    pltpu.make_async_copy(mass_ref, mass, in_sem.at[3]).start()
    whole_copy = pltpu.make_async_copy(b_ref, out0_ref, in_sem.at[5])

    barrier = pltpu.get_barrier_semaphore()
    partners = [place(left), place(right)] + group_b + group_a
    for partner in partners:
        pl.semaphore_signal(barrier, inc=1, device_id=partner, device_id_type=MESH)

    def guard(d, carry):
        row = (d + 1) * PITCH + NS
        for ref in (v0, v1, v2):
            for c in range(3):
                ref[c, pl.ds(row, 8)] = jnp.zeros((8, LANES), F32)
        w[pl.ds(row, 8)] = jnp.zeros((8, LANES), F32)
        return carry

    lax.fori_loop(0, DEPTH, guard, 0)
    for start in (0, (DEPTH + 1) * PITCH):
        for ref in (v0, v1, v2):
            for c in range(3):
                ref[c, pl.ds(start, PITCH)] = jnp.zeros((PITCH, LANES), F32)
        w[pl.ds(start, PITCH)] = jnp.zeros((PITCH, LANES), F32)
    for c in range(3):
        for ref in (v0, v1, v2):
            ref[c, pl.ds((DEPTH + 2) * PITCH, PITCH)] = jnp.zeros((PITCH, LANES), F32)

    has_left = jnp.where(me > 0, 1.0, 0.0).astype(F32)
    has_right = jnp.where(me < count - 1, 1.0, 0.0).astype(F32)
    low = lax.broadcasted_iota(jnp.int32, (8, LANES), 1) < LANES // 2

    def guard_strip(p, carry):
        row = p * SECTION + 8
        for ref in (x0, x1, x2):
            for c in range(3):
                ref[c, pl.ds(row, 8)] = jnp.zeros((8, LANES), F32)
        strip_w[pl.ds(row, 8)] = jnp.zeros((8, LANES), F32)
        valid[p] = jnp.where(
            low,
            jnp.where(p < HALO, has_left, 1.0),
            jnp.where(p >= 2 * HALO, has_right, 1.0),
        )
        return carry

    lax.fori_loop(0, WIDE, guard_strip, 0)

    spans_copy.wait()
    hits = bearing_hits(bearing_ends(spans[...]), me * LANES)
    for s in range(2):
        hit[s] = hits[s]

    for c in range(4):
        if c < 3:
            pltpu.make_async_copy(
                b_ref.at[c], v0.at[c, pl.ds(0, DEPTH * NS)], in_sem.at[c]
            ).wait()
        else:
            pltpu.make_async_copy(mass_ref, mass, in_sem.at[3]).wait()

        def edges(i, carry, c=c):
            for j in range(4):
                t = i * 4 + j
                if c < 3:
                    tile = jnp.concatenate(
                        [v0[c, pl.ds((2 * t + 1 + e) * PITCH, NS)] for e in range(2)], axis=0
                    )
                else:
                    tile = mass[pl.ds(t * LANES, LANES)]
                turned = tile.T
                at = c * PAIRS + t
                pitch = 4 * PAIRS
                near_left[pl.ds(LANDED + at, 8, stride=pitch), :] = turned[0:8]
                near_left[pl.ds(LANDED + 8 * pitch + at, 4, stride=pitch), :] = turned[8:12]
                near_right[pl.ds(at, 4, stride=pitch), :] = turned[LANES - 12 : LANES - 8]
                near_right[pl.ds(4 * pitch + at, 8, stride=pitch), :] = turned[LANES - 8 :]
            return carry

        lax.fori_loop(0, PAIRS // 4, edges, 0)

    pl.semaphore_wait(barrier, len(partners))
    middle = pl.ds(LANDED, LANDED)
    halos = [
        pltpu.make_async_remote_copy(
            src_ref=near_left.at[middle],
            dst_ref=near_right.at[pl.ds(2 * LANDED, LANDED)],
            send_sem=halo_send.at[0],
            recv_sem=halo_recv.at[0],
            device_id=place(left),
            device_id_type=MESH,
        ),
        pltpu.make_async_remote_copy(
            src_ref=near_right.at[middle],
            dst_ref=near_left.at[pl.ds(0, LANDED)],
            send_sem=halo_send.at[1],
            recv_sem=halo_recv.at[1],
            device_id=place(right),
            device_id_type=MESH,
        ),
    ]
    for copy in halos:
        copy.start()

    whole_copy.start()

    def apply(source, target, last, dots):
        quarter = 0.25 * bulk_modulus

        def divergence(base, scale):
            first = source[0, pl.ds(base, NS)]
            along = pltpu.roll(first, LANES - 1, 1) - pltpu.roll(first, 1, 1)
            across = source[1, pl.ds(base + 1, NS)] - source[1, pl.ds(base - 1, NS)]
            depth = source[2, pl.ds(base + PITCH, NS)] - source[2, pl.ds(base - PITCH, NS)]
            return scale * (along + across + depth)

        w[pl.ds(PITCH, NS)] = divergence(PITCH, quarter)
        zero = jnp.zeros((8, LANES), F32)

        def body(d, sums):
            base = (d + 1) * PITCH
            heavy = mass[pl.ds(d * NS, NS)] + 6.0
            ahead = divergence(base + PITCH, jnp.where(d < DEPTH - 1, quarter, 0.0))
            local = w[pl.ds(base, NS)]
            beside = (
                w[pl.ds(base + 1, NS)] - w[pl.ds(base - 1, NS)],
                ahead - w[pl.ds(base - PITCH, NS)],
            )
            terms = [zero] * len(dots)
            for c in range(3):
                here = source[c, pl.ds(base, NS)]
                if c == 0:
                    swept = pltpu.roll(here + local, LANES - 1, 1) + pltpu.roll(
                        here - local, 1, 1
                    )
                else:
                    swept = (
                        pltpu.roll(here, LANES - 1, 1)
                        + pltpu.roll(here, 1, 1)
                        + beside[c - 1]
                    )
                image = heavy * here
                image = image - (
                    source[c, pl.ds(base + 1, NS)] + source[c, pl.ds(base - 1, NS)]
                )
                image = image - (
                    source[c, pl.ds(base + PITCH, NS)] + source[c, pl.ds(base - PITCH, NS)]
                )
                image = image - swept
                if last:
                    target[c, pl.ds(d * NS, NS)] = image
                else:
                    target[c, pl.ds(base, NS)] = image
                for n, kind in enumerate(dots):
                    terms[n] = terms[n] + fold(
                        {"vv": here * here, "vi": here * image, "ii": image * image}[kind]
                    )
            w[pl.ds(base + PITCH, NS)] = ahead
            return tuple(s + t for s, t in zip(sums, terms))

        return lax.fori_loop(0, DEPTH, body, (zero,) * len(dots), unroll=UNROLL)

    mu0, mu1, mu2 = apply(v0, v1, False, ("vv", "vi", "ii"))
    mu3, mu4 = apply(v1, v2, False, ("vi", "ii"))
    (mu5,) = apply(v2, out3_ref, True, ("vi",))
    lane = lax.broadcasted_iota(jnp.int32, (8, LANES), 1)
    inner = (lane >= HALO) & (lane < LANES - HALO)
    moments = tuple(jnp.where(inner, mu, 0.0) for mu in (mu0, mu1, mu2, mu3, mu4, mu5))
    whole_copy.wait()

    half = LANES // 2
    for copy in halos:
        copy.wait_recv()

    def mix(first, second):
        turned = pltpu.roll(jnp.where(low, second, first), half, 1)
        return jnp.where(low, first, turned), jnp.where(low, turned, second)

    def gather(p, carry):
        for c in range(4):
            at = pl.ds(pl.multiple_of((p * 4 + c) * PAIRS, 8), PAIRS)
            even, odd = mix(near_left[at], near_right[at])
            for part, value in ((0, even), (16, odd)):
                to = pl.ds(pl.multiple_of(p * SECTION + part, 8), 8)
                if c < 3:
                    x0[c, to] = value * valid[p]
                else:
                    strip_mass[to] = value
        return carry

    lax.fori_loop(0, WIDE, gather, 0, unroll=6)

    across_at = lax.rem(lax.broadcasted_iota(jnp.int32, (8, LANES), 1), half)

    def after(x):
        return jnp.where(across_at == half - 1, 0.0, pltpu.roll(x, LANES - 1, 1))

    def before(x):
        return jnp.where(across_at == 0, 0.0, pltpu.roll(x, 1, 1))

    def rows(ref, row):
        return ref[pl.ds(row, 8)], ref[pl.ds(row + 16, 8)]

    def beside(ref, row, pair):
        even, odd = pair
        return (odd, ref[pl.ds(row + 15, 8)]), (ref[pl.ds(row + 1, 8)], even)

    zero = jnp.zeros((8, LANES), F32)
    sums = (zero,) * 6
    xs = (x0, x1, x2, x3)
    for k in range(3):
        source, target = xs[k], xs[k + 1]

        def strip_divergence(i, carry, k=k, source=source):
            p = i + 2 * k + 1
            row = p * SECTION
            first, second = rows(source.at[0], row - SECTION), rows(source.at[0], row + SECTION)
            middle = rows(source.at[1], row)
            third = beside(source.at[2], row, rows(source.at[2], row))
            for e in range(2):
                strip_w[pl.ds(row + 16 * e, 8)] = (
                    (0.25 * bulk_modulus)
                    * (
                        (second[e] - first[e])
                        + (after(middle[e]) - before(middle[e]))
                        + (third[e][0] - third[e][1])
                    )
                    * valid[p]
                )
            return carry

        lax.fori_loop(0, WIDE - 2 - 4 * k, strip_divergence, 0, unroll=DIV_UNROLL[k])

        def strip_image(i, sums, k=k, source=source, target=target):
            p = i + 2 * k + 2
            row = p * SECTION
            heavy = rows(strip_mass, row)
            local = rows(strip_w, row)
            around = rows(strip_w, row - SECTION), rows(strip_w, row + SECTION)
            upright = beside(strip_w, row, local)
            images, heres = [], []
            for c in range(3):
                ref = source.at[c]
                here = rows(ref, row)
                along = rows(ref, row - SECTION), rows(ref, row + SECTION)
                depth = beside(ref, row, here)
                for e in range(2):
                    image = (heavy[e] + 6.0) * here[e] - (along[0][e] + along[1][e])
                    image = image - (depth[e][0] + depth[e][1])
                    if c == 1:
                        image = image - (after(here[e] + local[e]) + before(here[e] - local[e]))
                    else:
                        image = image - (after(here[e]) + before(here[e]))
                    if c == 0:
                        image = image - (around[1][e] - around[0][e])
                    elif c == 2:
                        image = image - (upright[e][0] - upright[e][1])
                    images.append(image * valid[p])
                    heres.append(here[e])
            sums = list(sums)
            for n, (image, here) in enumerate(zip(images, heres)):
                at = pl.ds(row + 16 * (n % 2), 8)
                target[n // 2, at] = image
                if k == 2:
                    z0, z1 = x0[n // 2, at], x1[n // 2, at]
                    for m, (p0, p1) in enumerate(
                        ((z0, z0), (z0, z1), (z1, z1), (z1, here), (here, here), (here, image))
                    ):
                        sums[m] = sums[m] + p0 * p1
            return tuple(sums)

        sums = lax.fori_loop(0, WIDE - 4 - 4 * k, strip_image, sums, unroll=IMG_UNROLL[k])
    strips = sums

    def exchange(source, slots, partners, own, send_sems, recv_sems):
        copies = []
        for k, partner in enumerate(partners):
            copy = pltpu.make_async_remote_copy(
                src_ref=source,
                dst_ref=slots.at[own],
                send_sem=send_sems.at[k],
                recv_sem=recv_sems.at[k],
                device_id=partner,
                device_id_type=MESH,
            )
            copy.start()
            copies.append(copy)
        slots[own] = source[...]
        return copies

    def tree(parts, join):
        while len(parts) > 1:
            joined = [join(parts[i], parts[i + 1]) for i in range(0, len(parts) - 1, 2)]
            parts = joined + parts[len(parts) - len(parts) % 2 :]
        return parts[0]

    def join(p, q):
        hi, more = two_sum(p[0], q[0])
        return hi, p[1] + q[1] + more

    def total(slots, number):
        return tree([(slots[i, 0:8], slots[i, 8:16]) for i in range(number)], join)

    head, rest = [], []
    for n in range(6):
        hi, lo = two_sum(moments[n], strips[n])
        for shift in (4, 2, 1):
            hi, more = two_sum(hi, pltpu.roll(hi, shift, 0))
            lo = lo + pltpu.roll(lo, shift, 0) + more
        head.append(hi[0:1])
        rest.append(lo[0:1])
    blank = [jnp.zeros((2, LANES), F32)]
    part_a[...] = jnp.concatenate(head + blank + rest + blank, axis=0)
    copies = list(halos)
    copies_a = exchange(part_a, slots_a, group_a, at_xs, a_send, a_recv)

    edge_rows = 16 * PAIRS
    lanes = lax.broadcasted_iota(jnp.int32, (LANES, LANES), 1)
    outer = (lanes < HALO) | (lanes >= LANES - HALO)
    mains = (v1, v2, None)
    outs = (out1_ref, out2_ref, out3_ref)

    def back_edges(i, carry, ks=(0, 1, 2)):
        for k in ks:
            for c in range(3):
                even, odd = rows(xs[k + 1].at[c], (i + HALO) * SECTION)
                first, second = mix(even, odd)
                slot = (k * 3 + c) * edge_rows
                back[pl.ds(slot + (8 + i) * PAIRS, PAIRS)] = first
                back[pl.ds(slot + (2 + i) * PAIRS, PAIRS)] = second
        return carry

    def merge(k, c, t):
        slot = (k * 3 + c) * edge_rows + t
        edge = jnp.concatenate(
            [
                back[pl.ds(slot + 8 * PAIRS, 8, stride=PAIRS), :],
                jnp.zeros((LANES - 16, LANES), F32),
                back[pl.ds(slot, 8, stride=PAIRS), :],
            ],
            axis=0,
        ).T
        if k < 2:
            main = jnp.concatenate(
                [mains[k][c, pl.ds((2 * t + 1 + e) * PITCH, NS)] for e in range(2)], axis=0
            )
        else:
            main = out3_ref[c, pl.ds(t * LANES, LANES)]
        outs[k][c, pl.ds(t * LANES, LANES)] = jnp.where(outer, edge, main)

    for slot in range(9):
        for r in (0, 1, 14, 15):
            back[pl.ds(slot * edge_rows + r * PAIRS, PAIRS)] = jnp.zeros((PAIRS, LANES), F32)
    lax.fori_loop(0, HALO, back_edges, 0, unroll=HALO)
    for k in (0, 1):
        for c in (0, 1):
            merge(k, c, 0)

    site = jnp.zeros((8, 2 * LANES), F32)
    for s, across in ((0, NS // 4), (1, 3 * NS // 4)):
        picked = [v0[c, pl.ds(PITCH + across, 1)] for c in (0, 1)]
        picked += [out1_ref[c, pl.ds(across, 1)] for c in (0, 1)]
        picked += [out2_ref[c, pl.ds(across, 1)] for c in (0, 1)]
        picked += [jnp.zeros((2, LANES), F32)]
        site = site + jnp.dot(
            jnp.concatenate(picked, axis=0),
            hit[s],
            precision=HIGHEST,
            preferred_element_type=F32,
        )
    site_a[...] = jnp.concatenate([site[:, :LANES], site[:, LANES:]], axis=0)
    copies_sa = exchange(site_a, site_slots_a, group_a, at_xs, site_a_send, site_a_recv)

    for copy in copies_a:
        copy.wait_recv()
    part_b[...] = jnp.concatenate(total(slots_a, xs_size), axis=0)
    copies_b = exchange(part_b, slots_b, group_b, at_len, b_send, b_recv)

    for copy in copies_sa:
        copy.wait_recv()
    site_b[...] = tree([site_slots_a[i] for i in range(xs_size)], jnp.add)
    copies_sb = exchange(site_b, site_slots_b, group_b, at_len, site_b_send, site_b_recv)

    for k, c in ((0, 2), (1, 2), (2, 0), (2, 1), (2, 2)):
        merge(k, c, 0)

    def merge_rest(t, carry):
        for k in range(3):
            for c in range(3):
                merge(k, c, t)
        return carry

    lax.fori_loop(1, PAIRS, merge_rest, 0)

    for copy in copies_b:
        copy.wait_recv()
    increment, solved = steps(*total(slots_b, len_size))
    coefficients_ref[...] = jnp.concatenate(
        list(increment) + list(solved) + [jnp.zeros((1, LANES), F32)], axis=0
    )
    for copy in copies_sb:
        copy.wait_recv()
    sites_ref[...] = tree([site_slots_b[i] for i in range(len_size)], jnp.add)
    for copy in halos + copies_a + copies_b + copies_sa + copies_sb:
        copy.wait_send()


def steps(hi, lo):
    for shift in (64, 32, 16, 8, 4, 2, 1):
        hi, more = two_sum(hi, pltpu.roll(hi, shift, 1))
        lo = lo + pltpu.roll(lo, shift, 1) + more
    hi, lo = two_sum(hi, lo)
    theta = jnp.round(hi[1:2] / hi[0:1] * 64.0) * (1.0 / 64.0)
    central = [hi[0:1]]
    for order in range(5):
        n = 5 - order
        big = hi[:n] * 4097.0
        upper = big - (big - hi[:n])
        lower = hi[:n] - upper
        value, more = two_sum(hi[1 : n + 1], -theta * upper)
        value, extra = two_sum(value, -theta * lower)
        low_part = lo[1 : n + 1] - theta * lo[:n] + (more + extra)
        hi, lo = two_sum(value, low_part)
        central.append(hi[0:1])
    scale = 1.0 / central[0]
    c = [x * scale for x in central]
    c1 = [c[i + 1] + theta * c[i] for i in range(5)]

    def form(p, moments):
        terms = None
        for i in range(len(p)):
            for j in range(i, len(p)):
                term = (1.0 if i == j else 2.0) * (p[i] * p[j]) * moments[i + j]
                terms = term if terms is None else terms + term
        return terms

    one, zero = jnp.ones_like(theta), jnp.zeros_like(theta)
    left, ahead, norm = [one], [one], c[0]
    increment = [zero, zero, zero]
    for iteration in range(3):
        alpha = norm / form(ahead, c1)
        increment = [
            x + alpha * ahead[i] if i < len(ahead) else x for i, x in enumerate(increment)
        ]
        image = [theta * x for x in ahead] + [zero]
        image = [image[i] + (ahead[i - 1] if i else zero) for i in range(len(image))]
        left = left + [zero]
        left = [x - alpha * y for x, y in zip(left, image)]
        if iteration < 2:
            after = form(left, c)
            beta = after / norm
            ahead = ahead + [zero]
            ahead = [x + beta * y for x, y in zip(left, ahead)]
            norm = after
    x0, x1, x2 = increment
    r0, r1, r2, r3 = left
    increment = (x0 - theta * (x1 - theta * x2), x1 - 2.0 * theta * x2, x2)
    solved = (
        r0 - theta * (r1 - theta * (r2 - theta * r3)),
        r1 - theta * (2.0 * r2 - 3.0 * theta * r3),
        r2 - 3.0 * theta * r3,
        r3,
    )
    return increment, solved


def finish_kernel(
    b_ref,
    v1_ref,
    v2_ref,
    v3_ref,
    coefficients_ref,
    sites_ref,
    spans_ref,
    stick_ref,
    load_ref,
    prior_ref,
    inc_ref,
    res_ref,
    friction_ref,
    x,
    r,
    out_sem,
):
    me = lax.axis_index("len") * lax.axis_size("xs") + lax.axis_index("xs")
    row = lambda n: coefficients_ref[pl.ds(n, 1)]
    x0, x1, x2 = row(0), row(1), row(2)
    stores = []

    def combine(c, at):
        p0, p1, p2, p3 = b_ref[c, at], v1_ref[c, at], v2_ref[c, at], v3_ref[c, at]
        x[c, at] = x0 * p0 + x1 * p1 + x2 * p2
        r[c, at] = row(3) * p0 + row(4) * p1 + row(5) * p2 + row(6) * p3

    def store(c, at):
        for ref, dst in ((x, inc_ref), (r, res_ref)):
            copy = pltpu.make_async_copy(ref.at[c, at], dst.at[c, at], out_sem.at[len(stores)])
            copy.start()
            stores.append(copy)

    rows = DEPTH * NS
    for c in range(3):
        for first, last in ((NS, rows // 2), (rows // 2, rows)):

            def body(i, carry, c=c, first=first):
                combine(c, pl.ds(pl.multiple_of(first + i * NS, NS), NS))
                return carry

            lax.fori_loop(0, (last - first) // NS, body, 0)
            store(c, pl.ds(first, last - first))

    wide = lambda a: jnp.concatenate([a, a], axis=1)
    site = jnp.concatenate([sites_ref[0:8], sites_ref[8:16]], axis=1)
    readout = wide(x0) * site[0:2] + wide(x1) * site[2:4] + wide(x2) * site[4:6]
    radius = jnp.where(stick_ref[...] == 1, static_friction, kinetic_friction) * load_ref[...]
    trial = prior_ref[...] + elastic_stiffness * readout
    magnitude = jnp.sqrt(trial[0:1] * trial[0:1] + trial[1:2] * trial[1:2])
    friction = trial * (radius / jnp.maximum(magnitude, radius))
    friction_ref[...] = friction
    force = friction + load_ref[...] / pendulum_radius * readout
    bearings = force.shape[1]
    forces = jnp.concatenate(
        [force, jnp.ones((1, bearings), F32), jnp.zeros((5, bearings), F32)], axis=0
    )
    hits = bearing_hits(bearing_ends(spans_ref[...]), me * LANES)
    placed = [
        lax.dot_general(
            forces,
            hit,
            (((1,), (1,)), ((), ())),
            precision=HIGHEST,
            preferred_element_type=F32,
        )
        for hit in hits
    ]
    for c in range(3):
        combine(c, pl.ds(0, NS))
        for s, across in ((0, NS // 4), (1, 3 * NS // 4)):
            at = pl.ds(across, 1)
            if c < 2:
                drop = placed[s][c : c + 1]
            else:
                drop = vertical_stiffness * x[c, at] * placed[s][2:3]
            r[c, at] = r[c, at] - drop
        store(c, pl.ds(0, NS))
    for copy in stores:
        copy.wait()


def shards(right_side, mass_field, span_lengths, stick_flags, normal_load, prior_friction):
    sizes = (lax.axis_size("len"), lax.axis_size("xs"))
    rows = DEPTH * NS
    field = (3, rows, LANES)
    b = right_side.reshape(field)
    mass = mass_field.reshape(rows, LANES)
    spans = span_lengths.reshape(1, -1)
    stick = stick_flags.reshape(1, -1)
    load = normal_load.reshape(1, -1)
    anywhere = pl.BlockSpec(memory_space=pl.ANY)
    hbm = pl.BlockSpec(memory_space=pltpu.HBM)
    far = lambda a: pltpu.with_memory_space_constraint(a, pltpu.HBM)
    vmem = pl.BlockSpec(memory_space=pltpu.VMEM)
    v0, v1, v2, v3, coefficients, sites = pl.pallas_call(
        lambda *refs: krylov_kernel(sizes, *refs),
        name="krylov",
        out_shape=[pltpu.VMEM(field, F32)] * 4
        + [pltpu.VMEM((8, LANES), F32), pltpu.VMEM((16, LANES), F32)],
        in_specs=[hbm] * 3,
        out_specs=[vmem] * 6,
        scratch_shapes=[pltpu.VMEM((3, PADDED, LANES), F32)] * 3
        + [pltpu.VMEM((rows, LANES), F32), pltpu.VMEM((PADDED, LANES), F32)]
        + [pltpu.VMEM((3, STRIP, LANES), F32)] * 4
        + [pltpu.VMEM((STRIP, LANES), F32)] * 2
        + [pltpu.VMEM((OWN + LANDED, LANES), F32)] * 2
        + [
            pltpu.VMEM((WIDE, 8, LANES), F32),
            pltpu.VMEM((9 * 16 * PAIRS, LANES), F32),
            pltpu.VMEM((2, LANES, 2 * LANES), F32),
            pltpu.VMEM(spans.shape, jnp.int32),
        ]
        + [pltpu.VMEM((16, LANES), F32)] * 2
        + [pltpu.VMEM((n, 16, LANES), F32) for n in (sizes[1], sizes[0])]
        + [pltpu.VMEM((16, LANES), F32)] * 2
        + [pltpu.VMEM((n, 16, LANES), F32) for n in (sizes[1], sizes[0])]
        + [
            pltpu.SemaphoreType.DMA((n,))
            for n in (6, 2, 2) + 2 * (sizes[1], sizes[1], sizes[0], sizes[0])
        ],
        compiler_params=pltpu.CompilerParams(
            collective_id=0, has_side_effects=True, vmem_limit_bytes=32 * 2**20
        ),
    )(far(b), far(mass), far(spans))
    increment, residual, friction = pl.pallas_call(
        finish_kernel,
        name="finish",
        out_shape=[
            jax.ShapeDtypeStruct(field, F32),
            jax.ShapeDtypeStruct(field, F32),
            jax.ShapeDtypeStruct(prior_friction.shape, F32),
        ],
        in_specs=[vmem] * 10,
        out_specs=[anywhere, anywhere, vmem],
        scratch_shapes=[
            pltpu.VMEM(field, F32),
            pltpu.VMEM(field, F32),
            pltpu.SemaphoreType.DMA((18,)),
        ],
        compiler_params=pltpu.CompilerParams(vmem_limit_bytes=24 * 2**20),
    )(v0, v1, v2, v3, coefficients, sites, spans, stick, load, prior_friction)
    return (
        increment.reshape(right_side.shape),
        residual.reshape(right_side.shape),
        friction,
    )


def solution(mesh):
    along = ("len", "xs")
    in_specs = (P(None, None, None, along), P(None, None, along), P(), P(), P(), P())
    out_specs = (P(None, None, None, along), P(None, None, None, along), P())
    return jax.shard_map(shards, mesh=mesh, in_specs=in_specs, out_specs=out_specs, check_vma=False)
```

```python
import jax
import jax.numpy as jnp
from jax import lax
from jax.experimental import pallas as pl
from jax.experimental.pallas import tpu as pltpu
from jax.sharding import PartitionSpec as P

shear_modulus = 1.0
bulk_modulus = 1.5
elastic_stiffness = 8.0
pendulum_radius = 4.0
vertical_stiffness = 5.0
static_friction = 0.6
kinetic_friction = 0.45

DEPTH = 16
NS = 64
LANES = 128
PITCH = NS + 8
PADDED = (DEPTH + 3) * PITCH
HALO = 6
PAIRS = DEPTH * NS // LANES
WIDE = 3 * HALO
SECTION = 24
STRIP = WIDE * SECTION
OWN = 2 * HALO * 4 * PAIRS
LANDED = HALO * 4 * PAIRS

UNROLL = 4
DIV_UNROLL = (16, 12, 8)
IMG_UNROLL = (7, 5, 6)

MESH = pl.DeviceIdType.MESH
HIGHEST = lax.Precision.HIGHEST
F32 = jnp.float32


def two_sum(a, b):
    s = a + b
    t = s - a
    return s, (a - (s - t)) + (b - t)


def fold(block):
    return jnp.sum(block.reshape(block.shape[0] // 8, 8, LANES), axis=0)


def bearing_ends(spans):
    piers = spans.shape[1]
    upto = (
        lax.broadcasted_iota(jnp.int32, (piers, 2 * piers), 0)
        <= lax.broadcasted_iota(jnp.int32, (piers, 2 * piers), 1) // 2
    ).astype(F32)
    return (
        jnp.dot(
            jnp.broadcast_to(spans.astype(F32), (8, piers)),
            upto,
            precision=HIGHEST,
            preferred_element_type=F32,
        )[0:1]
        - 1.0
    )


def bearing_hits(ends, start):
    bearings = ends.shape[1]
    along = lax.broadcasted_iota(jnp.int32, (LANES, bearings), 0) + start
    side = lax.rem(lax.broadcasted_iota(jnp.int32, (LANES, bearings), 1), 2)
    here = along.astype(F32) == ends
    return [jnp.where(here & (side == s), 1.0, 0.0).astype(F32) for s in range(2)]


def krylov_kernel(
    sizes,
    b_ref,
    mass_ref,
    spans_ref,
    inc_ref,
    solved_ref,
    coefficients_ref,
    sites_ref,
    v0,
    v1,
    v2,
    out1_ref,
    out2_ref,
    out3_ref,
    mass,
    w,
    x0,
    x1,
    x2,
    x3,
    strip_mass,
    strip_w,
    near_left,
    near_right,
    valid,
    back,
    hit,
    spans,
    part,
    slots,
    site_a,
    site_b,
    site_slots_a,
    site_slots_b,
    in_sem,
    halo_send,
    halo_recv,
    all_send,
    all_recv,
    ready,
    site_a_send,
    site_a_recv,
    site_b_send,
    site_b_recv,
):
    len_size, xs_size = sizes
    count = len_size * xs_size
    at_len, at_xs = lax.axis_index("len"), lax.axis_index("xs")
    me = at_len * xs_size + at_xs
    left, right = lax.rem(me + count - 1, count), lax.rem(me + 1, count)
    place = lambda i: (i // xs_size, lax.rem(i, xs_size))
    group_a = [(at_len, lax.rem(at_xs + k, xs_size)) for k in range(1, xs_size)]
    group_b = [(lax.rem(at_len + k, len_size), at_xs) for k in range(1, len_size)]

    spans_copy = pltpu.make_async_copy(spans_ref, spans, in_sem.at[4])
    spans_copy.start()
    for c in range(3):

        def load(d, carry, c=c):
            pltpu.make_async_copy(
                b_ref.at[c, pl.ds(d * NS, NS)],
                v0.at[c, pl.ds((d + 1) * PITCH, NS)],
                in_sem.at[c],
            ).start()
            return carry

        lax.fori_loop(0, DEPTH, load, 0)
    pltpu.make_async_copy(mass_ref, mass, in_sem.at[3]).start()

    barrier = pltpu.get_barrier_semaphore()
    partners = [place(left), place(right)] + group_b + group_a
    for partner in partners:
        pl.semaphore_signal(barrier, inc=1, device_id=partner, device_id_type=MESH)

    def guard(d, carry):
        row = (d + 1) * PITCH + NS
        for ref in (v0, v1, v2):
            for c in range(3):
                ref[c, pl.ds(row, 8)] = jnp.zeros((8, LANES), F32)
        w[pl.ds(row, 8)] = jnp.zeros((8, LANES), F32)
        return carry

    lax.fori_loop(0, DEPTH, guard, 0)
    for start in (0, (DEPTH + 1) * PITCH):
        for ref in (v0, v1, v2):
            for c in range(3):
                ref[c, pl.ds(start, PITCH)] = jnp.zeros((PITCH, LANES), F32)
        w[pl.ds(start, PITCH)] = jnp.zeros((PITCH, LANES), F32)
    for c in range(3):
        for ref in (v0, v1, v2):
            ref[c, pl.ds((DEPTH + 2) * PITCH, PITCH)] = jnp.zeros((PITCH, LANES), F32)

    has_left = jnp.where(me > 0, 1.0, 0.0).astype(F32)
    has_right = jnp.where(me < count - 1, 1.0, 0.0).astype(F32)
    low = lax.broadcasted_iota(jnp.int32, (8, LANES), 1) < LANES // 2

    def guard_strip(p, carry):
        row = p * SECTION + 8
        for ref in (x0, x1, x2):
            for c in range(3):
                ref[c, pl.ds(row, 8)] = jnp.zeros((8, LANES), F32)
        strip_w[pl.ds(row, 8)] = jnp.zeros((8, LANES), F32)
        valid[p] = jnp.where(
            low,
            jnp.where(p < HALO, has_left, 1.0),
            jnp.where(p >= 2 * HALO, has_right, 1.0),
        )
        return carry

    lax.fori_loop(0, WIDE, guard_strip, 0)

    spans_copy.wait()
    hits = bearing_hits(bearing_ends(spans[...]), me * LANES)
    for s in range(2):
        hit[s] = hits[s]

    for c in range(4):
        if c < 3:
            pltpu.make_async_copy(
                b_ref.at[c], v0.at[c, pl.ds(0, DEPTH * NS)], in_sem.at[c]
            ).wait()
        else:
            pltpu.make_async_copy(mass_ref, mass, in_sem.at[3]).wait()

        def edges(i, carry, c=c):
            for j in range(4):
                t = i * 4 + j
                if c < 3:
                    tile = jnp.concatenate(
                        [v0[c, pl.ds((2 * t + 1 + e) * PITCH, NS)] for e in range(2)], axis=0
                    )
                else:
                    tile = mass[pl.ds(t * LANES, LANES)]
                turned = tile.T
                at = c * PAIRS + t
                pitch = 4 * PAIRS
                near_left[pl.ds(LANDED + at, 8, stride=pitch), :] = turned[0:8]
                near_left[pl.ds(LANDED + 8 * pitch + at, 4, stride=pitch), :] = turned[8:12]
                near_right[pl.ds(at, 4, stride=pitch), :] = turned[LANES - 12 : LANES - 8]
                near_right[pl.ds(4 * pitch + at, 8, stride=pitch), :] = turned[LANES - 8 :]
            return carry

        lax.fori_loop(0, PAIRS // 4, edges, 0)

    pl.semaphore_wait(barrier, len(partners))
    middle = pl.ds(LANDED, LANDED)
    halos = [
        pltpu.make_async_remote_copy(
            src_ref=near_left.at[middle],
            dst_ref=near_right.at[pl.ds(2 * LANDED, LANDED)],
            send_sem=halo_send.at[0],
            recv_sem=halo_recv.at[0],
            device_id=place(left),
            device_id_type=MESH,
        ),
        pltpu.make_async_remote_copy(
            src_ref=near_right.at[middle],
            dst_ref=near_left.at[pl.ds(0, LANDED)],
            send_sem=halo_send.at[1],
            recv_sem=halo_recv.at[1],
            device_id=place(right),
            device_id_type=MESH,
        ),
    ]
    for copy in halos:
        copy.start()
    for partner in group_a:
        pl.semaphore_signal(ready, inc=1, device_id=partner, device_id_type=MESH)


    def apply(source, target, last, dots):
        quarter = 0.25 * bulk_modulus

        def divergence(base, scale):
            first = source[0, pl.ds(base, NS)]
            along = pltpu.roll(first, LANES - 1, 1) - pltpu.roll(first, 1, 1)
            across = source[1, pl.ds(base + 1, NS)] - source[1, pl.ds(base - 1, NS)]
            depth = source[2, pl.ds(base + PITCH, NS)] - source[2, pl.ds(base - PITCH, NS)]
            return scale * (along + across + depth)

        w[pl.ds(PITCH, NS)] = divergence(PITCH, quarter)
        zero = jnp.zeros((8, LANES), F32)

        def body(d, sums):
            base = (d + 1) * PITCH
            heavy = mass[pl.ds(d * NS, NS)] + 6.0
            ahead = divergence(base + PITCH, jnp.where(d < DEPTH - 1, quarter, 0.0))
            local = w[pl.ds(base, NS)]
            beside = (
                w[pl.ds(base + 1, NS)] - w[pl.ds(base - 1, NS)],
                ahead - w[pl.ds(base - PITCH, NS)],
            )
            terms = [zero] * len(dots)
            for c in range(3):
                here = source[c, pl.ds(base, NS)]
                if c == 0:
                    swept = pltpu.roll(here + local, LANES - 1, 1) + pltpu.roll(
                        here - local, 1, 1
                    )
                else:
                    swept = (
                        pltpu.roll(here, LANES - 1, 1)
                        + pltpu.roll(here, 1, 1)
                        + beside[c - 1]
                    )
                image = heavy * here
                image = image - (
                    source[c, pl.ds(base + 1, NS)] + source[c, pl.ds(base - 1, NS)]
                )
                image = image - (
                    source[c, pl.ds(base + PITCH, NS)] + source[c, pl.ds(base - PITCH, NS)]
                )
                image = image - swept
                if last:
                    target[c, pl.ds(d * NS, NS)] = image
                else:
                    target[c, pl.ds(base, NS)] = image
                for n, kind in enumerate(dots):
                    terms[n] = terms[n] + fold(
                        {"vv": here * here, "vi": here * image, "ii": image * image}[kind]
                    )
            w[pl.ds(base + PITCH, NS)] = ahead
            return tuple(s + t for s, t in zip(sums, terms))

        return lax.fori_loop(0, DEPTH, body, (zero,) * len(dots), unroll=UNROLL)

    mu0, mu1, mu2 = apply(v0, v1, False, ("vv", "vi", "ii"))
    mu3, mu4 = apply(v1, v2, False, ("vi", "ii"))
    (mu5,) = apply(v2, out3_ref, True, ("vi",))
    lane = lax.broadcasted_iota(jnp.int32, (8, LANES), 1)
    inner = (lane >= HALO) & (lane < LANES - HALO)
    moments = tuple(jnp.where(inner, mu, 0.0) for mu in (mu0, mu1, mu2, mu3, mu4, mu5))

    half = LANES // 2
    for copy in halos:
        copy.wait_recv()

    def mix(first, second):
        turned = pltpu.roll(jnp.where(low, second, first), half, 1)
        return jnp.where(low, first, turned), jnp.where(low, turned, second)

    def gather(p, carry):
        for c in range(4):
            at = pl.ds(pl.multiple_of((p * 4 + c) * PAIRS, 8), PAIRS)
            even, odd = mix(near_left[at], near_right[at])
            for part, value in ((0, even), (16, odd)):
                to = pl.ds(pl.multiple_of(p * SECTION + part, 8), 8)
                if c < 3:
                    x0[c, to] = value * valid[p]
                else:
                    strip_mass[to] = value
        return carry

    lax.fori_loop(0, WIDE, gather, 0, unroll=6)

    across_at = lax.rem(lax.broadcasted_iota(jnp.int32, (8, LANES), 1), half)

    def after(x):
        return jnp.where(across_at == half - 1, 0.0, pltpu.roll(x, LANES - 1, 1))

    def before(x):
        return jnp.where(across_at == 0, 0.0, pltpu.roll(x, 1, 1))

    def rows(ref, row):
        return ref[pl.ds(row, 8)], ref[pl.ds(row + 16, 8)]

    def beside(ref, row, pair):
        even, odd = pair
        return (odd, ref[pl.ds(row + 15, 8)]), (ref[pl.ds(row + 1, 8)], even)

    xs = (x0, x1, x2, x3)
    def exchange(source, slots, partners, own, send_sems, recv_sems):
        copies = []
        for k, partner in enumerate(partners):
            copy = pltpu.make_async_remote_copy(
                src_ref=source,
                dst_ref=slots.at[own],
                send_sem=send_sems.at[k],
                recv_sem=recv_sems.at[k],
                device_id=partner,
                device_id_type=MESH,
            )
            copy.start()
            copies.append(copy)
        slots[own] = source[...]
        return copies

    def tree(parts, join):
        while len(parts) > 1:
            joined = [join(parts[i], parts[i + 1]) for i in range(0, len(parts) - 1, 2)]
            parts = joined + parts[len(parts) - len(parts) % 2 :]
        return parts[0]

    def join(p, q):
        hi, more = two_sum(p[0], q[0])
        return hi, p[1] + q[1] + more

    edge_rows = 16 * PAIRS
    lanes = lax.broadcasted_iota(jnp.int32, (LANES, LANES), 1)
    outer = (lanes < HALO) | (lanes >= LANES - HALO)
    mains = (v1, v2, None)
    outs = (out1_ref, out2_ref, out3_ref)

    def back_edges(i, carry, ks=(0, 1, 2)):
        for k in ks:
            for c in range(3):
                even, odd = rows(xs[k + 1].at[c], (i + HALO) * SECTION)
                first, second = mix(even, odd)
                slot = (k * 3 + c) * edge_rows
                back[pl.ds(slot + (8 + i) * PAIRS, PAIRS)] = first
                back[pl.ds(slot + (2 + i) * PAIRS, PAIRS)] = second
        return carry

    def merge(k, c, t):
        slot = (k * 3 + c) * edge_rows + t
        edge = jnp.concatenate(
            [
                back[pl.ds(slot + 8 * PAIRS, 8, stride=PAIRS), :],
                jnp.zeros((LANES - 16, LANES), F32),
                back[pl.ds(slot, 8, stride=PAIRS), :],
            ],
            axis=0,
        ).T
        if k < 2:
            main = jnp.concatenate(
                [mains[k][c, pl.ds((2 * t + 1 + e) * PITCH, NS)] for e in range(2)], axis=0
            )
        else:
            main = out3_ref[c, pl.ds(t * LANES, LANES)]
        outs[k][c, pl.ds(t * LANES, LANES)] = jnp.where(outer, edge, main)

    zero = jnp.zeros((8, LANES), F32)
    sums = (zero,) * 6
    for k in range(3):
        if k == 2:
            for slot in range(9):
                for r in (0, 1, 14, 15):
                    back[pl.ds(slot * edge_rows + r * PAIRS, PAIRS)] = jnp.zeros((PAIRS, LANES), F32)
            for i in range(HALO):
                back_edges(i, 0, (0, 1))
            for n in (0, 1):
                for c in (0, 1):
                    merge(n, c, 0)

            site = jnp.zeros((8, 2 * LANES), F32)
            for s, across in ((0, NS // 4), (1, 3 * NS // 4)):
                picked = [v0[c, pl.ds(PITCH + across, 1)] for c in (0, 1)]
                picked += [out1_ref[c, pl.ds(across, 1)] for c in (0, 1)]
                picked += [out2_ref[c, pl.ds(across, 1)] for c in (0, 1)]
                picked += [jnp.zeros((2, LANES), F32)]
                site = site + jnp.dot(
                    jnp.concatenate(picked, axis=0),
                    hit[s],
                    precision=HIGHEST,
                    preferred_element_type=F32,
                )
            site_a[...] = jnp.concatenate([site[:, :LANES], site[:, LANES:]], axis=0)
        source, target = xs[k], xs[k + 1]

        def strip_divergence(i, carry, k=k, source=source):
            p = i + 2 * k + 1
            row = p * SECTION
            first, second = rows(source.at[0], row - SECTION), rows(source.at[0], row + SECTION)
            middle = rows(source.at[1], row)
            third = beside(source.at[2], row, rows(source.at[2], row))
            for e in range(2):
                strip_w[pl.ds(row + 16 * e, 8)] = (
                    (0.25 * bulk_modulus)
                    * (
                        (second[e] - first[e])
                        + (after(middle[e]) - before(middle[e]))
                        + (third[e][0] - third[e][1])
                    )
                    * valid[p]
                )
            return carry

        lax.fori_loop(0, WIDE - 2 - 4 * k, strip_divergence, 0, unroll=DIV_UNROLL[k])

        def strip_image(i, sums, k=k, source=source, target=target):
            p = i + 2 * k + 2
            row = p * SECTION
            heavy = rows(strip_mass, row)
            local = rows(strip_w, row)
            around = rows(strip_w, row - SECTION), rows(strip_w, row + SECTION)
            upright = beside(strip_w, row, local)
            images, heres = [], []
            for c in range(3):
                ref = source.at[c]
                here = rows(ref, row)
                along = rows(ref, row - SECTION), rows(ref, row + SECTION)
                depth = beside(ref, row, here)
                for e in range(2):
                    image = (heavy[e] + 6.0) * here[e] - (along[0][e] + along[1][e])
                    image = image - (depth[e][0] + depth[e][1])
                    if c == 1:
                        image = image - (after(here[e] + local[e]) + before(here[e] - local[e]))
                    else:
                        image = image - (after(here[e]) + before(here[e]))
                    if c == 0:
                        image = image - (around[1][e] - around[0][e])
                    elif c == 2:
                        image = image - (upright[e][0] - upright[e][1])
                    images.append(image * valid[p])
                    heres.append(here[e])
            sums = list(sums)
            for n, (image, here) in enumerate(zip(images, heres)):
                at = pl.ds(row + 16 * (n % 2), 8)
                target[n // 2, at] = image
                if k == 2:
                    z0, z1 = x0[n // 2, at], x1[n // 2, at]
                    for m, (p0, p1) in enumerate(
                        ((z0, z0), (z0, z1), (z1, z1), (z1, here), (here, here), (here, image))
                    ):
                        sums[m] = sums[m] + p0 * p1
            return tuple(sums)

        sums = lax.fori_loop(0, WIDE - 4 - 4 * k, strip_image, sums, unroll=IMG_UNROLL[k])
    strips = sums

    head, rest = [], []
    for n in range(6):
        hi, lo = two_sum(moments[n], strips[n])
        for shift in (4, 2, 1):
            hi, more = two_sum(hi, pltpu.roll(hi, shift, 0))
            lo = lo + pltpu.roll(lo, shift, 0) + more
        head.append(hi[0:1])
        rest.append(lo[0:1])
    blank = [jnp.zeros((2, LANES), F32)]
    hi, lo = jnp.concatenate(head + blank, axis=0), jnp.concatenate(rest + blank, axis=0)
    for shift in (64, 32, 16, 8, 4, 2, 1):
        hi, more = two_sum(hi, pltpu.roll(hi, shift, 1))
        lo = lo + pltpu.roll(lo, shift, 1) + more
    hi, lo = two_sum(hi, lo)
    sublane = lax.broadcasted_iota(jnp.int32, (8, LANES), 0)
    at_hi, at_lo = lane == sublane, lane == sublane + 8
    packed = jnp.sum(jnp.where(at_hi, hi, 0.0) + jnp.where(at_lo, lo, 0.0), axis=0, keepdims=True)
    part[...] = packed

    copies = exchange(site_a, site_slots_a, group_a, at_xs, site_a_send, site_a_recv)
    copies_a = copies

    pl.semaphore_wait(ready, len(group_a))
    ring = lambda a, n: min(a, n - a)
    far = lambda o: -(ring(o[0] // 4, 4) + ring(o[0] % 4, 4) + ring(o[1] // 2, 4))
    offsets = [(a, b) for a in range(len_size) for b in range(xs_size) if a or b]
    lens = [lax.rem(at_len + a, len_size) for a in range(len_size)]
    spots = [lax.rem(at_xs + b, xs_size) for b in range(xs_size)]
    for a, b in sorted(offsets, key=far):
        pltpu.make_async_remote_copy(
            src_ref=part,
            dst_ref=slots.at[pl.ds(me, 1)],
            send_sem=all_send,
            recv_sem=all_recv,
            device_id=(lens[a], spots[b]),
            device_id_type=MESH,
        ).start()
    slots[pl.ds(me, 1)] = part[...]

    for i in range(HALO):
        back_edges(i, 0, (2,))
    merge(0, 2, 0)
    merge(1, 2, 0)
    for c in range(3):
        merge(2, c, 0)

    for copy in copies_a:
        copy.wait_recv()
    site_b[...] = tree([site_slots_a[i] for i in range(xs_size)], jnp.add)
    copies_b = exchange(site_b, site_slots_b, group_b, at_len, site_b_send, site_b_recv)

    def merge_rest(t, carry):
        for k in range(3):
            for c in range(3):
                merge(k, c, t)
        return carry

    lax.fori_loop(1, PAIRS, merge_rest, 0)

    others = slots.at[pl.ds(0, count - 1)]
    pltpu.make_async_copy(others, others, all_recv).wait()
    hi, lo = tree(
        [(slots[pl.ds(8 * i, 8)], jnp.zeros((8, LANES), F32)) for i in range(count // 8)], join
    )
    for shift in (4, 2, 1):
        hi, more = two_sum(hi, pltpu.roll(hi, shift, 0))
        lo = lo + pltpu.roll(lo, shift, 0) + more
    pick = lambda mask, x: jnp.broadcast_to(
        jnp.sum(jnp.where(mask, x, 0.0), axis=1, keepdims=True), (8, LANES)
    )
    increment, solved = steps(pick(at_hi, hi), pick(at_lo, hi) + pick(at_hi, lo))
    coefficients_ref[...] = jnp.concatenate(
        list(increment) + list(solved) + [jnp.zeros((1, LANES), F32)], axis=0
    )

    def combine(d, carry):
        at = pl.ds(pl.multiple_of(d * NS, NS), NS)
        for c in range(3):
            p0 = v0[c, pl.ds((d + 1) * PITCH, NS)]
            p1, p2, p3 = out1_ref[c, at], out2_ref[c, at], out3_ref[c, at]
            inc_ref[c, at] = increment[0] * p0 + increment[1] * p1 + increment[2] * p2
            solved_ref[c, at] = (
                solved[0] * p0 + solved[1] * p1 + solved[2] * p2 + solved[3] * p3
            )
        return carry

    lax.fori_loop(0, DEPTH, combine, 0)

    for copy in copies_b:
        copy.wait_recv()
    sites_ref[...] = tree([site_slots_b[i] for i in range(len_size)], jnp.add)
    pltpu.make_async_copy(others, others, all_send).wait()
    for copy in halos + copies_a + copies_b:
        copy.wait_send()


def steps(hi, lo):
    for shift in (64, 32, 16, 8, 4, 2, 1):
        hi, more = two_sum(hi, pltpu.roll(hi, shift, 1))
        lo = lo + pltpu.roll(lo, shift, 1) + more
    hi, lo = two_sum(hi, lo)
    theta = jnp.round(hi[1:2] / hi[0:1] * 64.0) * (1.0 / 64.0)
    central = [hi[0:1]]
    for order in range(5):
        n = 5 - order
        big = hi[:n] * 4097.0
        upper = big - (big - hi[:n])
        lower = hi[:n] - upper
        value, more = two_sum(hi[1 : n + 1], -theta * upper)
        value, extra = two_sum(value, -theta * lower)
        low_part = lo[1 : n + 1] - theta * lo[:n] + (more + extra)
        hi, lo = two_sum(value, low_part)
        central.append(hi[0:1])
    scale = 1.0 / central[0]
    c = [x * scale for x in central]
    c1 = [c[i + 1] + theta * c[i] for i in range(5)]

    def form(p, moments):
        terms = None
        for i in range(len(p)):
            for j in range(i, len(p)):
                term = (1.0 if i == j else 2.0) * (p[i] * p[j]) * moments[i + j]
                terms = term if terms is None else terms + term
        return terms

    one, zero = jnp.ones_like(theta), jnp.zeros_like(theta)
    left, ahead, norm = [one], [one], c[0]
    increment = [zero, zero, zero]
    for iteration in range(3):
        alpha = norm / form(ahead, c1)
        increment = [
            x + alpha * ahead[i] if i < len(ahead) else x for i, x in enumerate(increment)
        ]
        image = [theta * x for x in ahead] + [zero]
        image = [image[i] + (ahead[i - 1] if i else zero) for i in range(len(image))]
        left = left + [zero]
        left = [x - alpha * y for x, y in zip(left, image)]
        if iteration < 2:
            after = form(left, c)
            beta = after / norm
            ahead = ahead + [zero]
            ahead = [x + beta * y for x, y in zip(left, ahead)]
            norm = after
    x0, x1, x2 = increment
    r0, r1, r2, r3 = left
    increment = (x0 - theta * (x1 - theta * x2), x1 - 2.0 * theta * x2, x2)
    solved = (
        r0 - theta * (r1 - theta * (r2 - theta * r3)),
        r1 - theta * (2.0 * r2 - 3.0 * theta * r3),
        r2 - 3.0 * theta * r3,
        r3,
    )
    return increment, solved


def finish_kernel(
    increment_ref,
    solved_ref,
    coefficients_ref,
    sites_ref,
    spans_ref,
    stick_ref,
    load_ref,
    prior_ref,
    inc_ref,
    res_ref,
    friction_ref,
    first,
    out_sem,
):
    rows = DEPTH * NS
    at, top = pl.ds(NS, rows - NS), pl.ds(0, NS)
    stores = []

    def store(source, target):
        copy = pltpu.make_async_copy(source, target, out_sem.at[len(stores)])
        copy.start()
        stores.append(copy)

    for c in range(3):
        store(increment_ref.at[c], inc_ref.at[c])
        store(solved_ref.at[c, at], res_ref.at[c, at])

    me = lax.axis_index("len") * lax.axis_size("xs") + lax.axis_index("xs")

    wide = lambda n: jnp.concatenate([coefficients_ref[pl.ds(n, 1)]] * 2, axis=1)
    site = jnp.concatenate([sites_ref[0:8], sites_ref[8:16]], axis=1)
    readout = wide(0) * site[0:2] + wide(1) * site[2:4] + wide(2) * site[4:6]
    radius = jnp.where(stick_ref[...] == 1, static_friction, kinetic_friction) * load_ref[...]
    trial = prior_ref[...] + elastic_stiffness * readout
    magnitude = jnp.sqrt(trial[0:1] * trial[0:1] + trial[1:2] * trial[1:2])
    friction = trial * (radius / jnp.maximum(magnitude, radius))
    friction_ref[...] = friction
    force = friction + load_ref[...] / pendulum_radius * readout
    bearings = force.shape[1]
    forces = jnp.concatenate(
        [force, jnp.ones((1, bearings), F32), jnp.zeros((5, bearings), F32)], axis=0
    )
    hits = bearing_hits(bearing_ends(spans_ref[...]), me * LANES)
    placed = [
        lax.dot_general(
            forces,
            hit,
            (((1,), (1,)), ((), ())),
            precision=HIGHEST,
            preferred_element_type=F32,
        )
        for hit in hits
    ]
    for c in range(3):
        first[c] = solved_ref[c, top]
        for s, across in ((0, NS // 4), (1, 3 * NS // 4)):
            node = pl.ds(across, 1)
            if c < 2:
                drop = placed[s][c : c + 1]
            else:
                drop = vertical_stiffness * increment_ref[c, node] * placed[s][2:3]
            first[c, node] = first[c, node] - drop
        store(first.at[c], res_ref.at[c, top])
    for copy in stores:
        copy.wait()


def shards(right_side, mass_field, span_lengths, stick_flags, normal_load, prior_friction):
    sizes = (lax.axis_size("len"), lax.axis_size("xs"))
    count = sizes[0] * sizes[1]
    rows = DEPTH * NS
    field = (3, rows, LANES)
    b = right_side.reshape(field)
    mass = mass_field.reshape(rows, LANES)
    spans = span_lengths.reshape(1, -1)
    stick = stick_flags.reshape(1, -1)
    load = normal_load.reshape(1, -1)
    anywhere = pl.BlockSpec(memory_space=pl.ANY)
    hbm = pl.BlockSpec(memory_space=pltpu.HBM)
    far = lambda a: pltpu.with_memory_space_constraint(a, pltpu.HBM)
    vmem = pl.BlockSpec(memory_space=pltpu.VMEM)
    increment, solved, coefficients, sites = pl.pallas_call(
        lambda *refs: krylov_kernel(sizes, *refs),
        name="krylov",
        out_shape=[pltpu.VMEM(field, F32)] * 2
        + [pltpu.VMEM((8, LANES), F32), pltpu.VMEM((16, LANES), F32)],
        in_specs=[hbm] * 3,
        out_specs=[vmem] * 4,
        scratch_shapes=[pltpu.VMEM((3, PADDED, LANES), F32)] * 3
        + [pltpu.VMEM(field, F32)] * 3
        + [pltpu.VMEM((rows, LANES), F32), pltpu.VMEM((PADDED, LANES), F32)]
        + [pltpu.VMEM((3, STRIP, LANES), F32)] * 4
        + [pltpu.VMEM((STRIP, LANES), F32)] * 2
        + [pltpu.VMEM((OWN + LANDED, LANES), F32)] * 2
        + [
            pltpu.VMEM((WIDE, 8, LANES), F32),
            pltpu.VMEM((9 * 16 * PAIRS, LANES), F32),
            pltpu.VMEM((2, LANES, 2 * LANES), F32),
            pltpu.VMEM(spans.shape, jnp.int32),
        ]
        + [pltpu.VMEM((1, LANES), F32), pltpu.VMEM((count, LANES), F32)]
        + [pltpu.VMEM((16, LANES), F32)] * 2
        + [pltpu.VMEM((n, 16, LANES), F32) for n in (sizes[1], sizes[0])]
        + [pltpu.SemaphoreType.DMA((n,)) for n in (5, 2, 2)]
        + [pltpu.SemaphoreType.DMA, pltpu.SemaphoreType.DMA, pltpu.SemaphoreType.REGULAR]
        + [pltpu.SemaphoreType.DMA((n,)) for n in (sizes[1], sizes[1], sizes[0], sizes[0])],
        compiler_params=pltpu.CompilerParams(
            collective_id=0, has_side_effects=True, vmem_limit_bytes=32 * 2**20
        ),
    )(far(b), far(mass), far(spans))
    increment, residual, friction = pl.pallas_call(
        finish_kernel,
        name="finish",
        out_shape=[
            jax.ShapeDtypeStruct(field, F32),
            jax.ShapeDtypeStruct(field, F32),
            jax.ShapeDtypeStruct(prior_friction.shape, F32),
        ],
        in_specs=[vmem] * 8,
        out_specs=[anywhere, anywhere, vmem],
        scratch_shapes=[
            pltpu.VMEM((3, NS, LANES), F32),
            pltpu.SemaphoreType.DMA((9,)),
        ],
        compiler_params=pltpu.CompilerParams(vmem_limit_bytes=24 * 2**20),
    )(increment, solved, coefficients, sites, spans, stick, load, prior_friction)
    return (
        increment.reshape(right_side.shape),
        residual.reshape(right_side.shape),
        friction,
    )


def solution(mesh):
    along = ("len", "xs")
    in_specs = (P(None, None, None, along), P(None, None, along), P(), P(), P(), P())
    out_specs = (P(None, None, None, along), P(None, None, None, along), P())
    return jax.shard_map(shards, mesh=mesh, in_specs=in_specs, out_specs=out_specs, check_vma=False)
```

```python
import jax
import jax.numpy as jnp
from jax import lax
from jax.experimental import pallas as pl
from jax.experimental.pallas import tpu as pltpu
from jax.sharding import PartitionSpec as P

shear_modulus = 1.0
bulk_modulus = 1.5
elastic_stiffness = 8.0
pendulum_radius = 4.0
vertical_stiffness = 5.0
static_friction = 0.6
kinetic_friction = 0.45

DEPTH = 16
NS = 64
LANES = 128
PITCH = NS + 8
PADDED = (DEPTH + 3) * PITCH
HALO = 6
PAIRS = DEPTH * NS // LANES
WIDE = 3 * HALO
SECTION = 24
STRIP = WIDE * SECTION
OWN = 2 * HALO * 4 * PAIRS
LANDED = HALO * 4 * PAIRS

UNROLL = 4
DIV_UNROLL = (16, 12, 8)
IMG_UNROLL = (7, 5, 6)

MESH = pl.DeviceIdType.MESH
HIGHEST = lax.Precision.HIGHEST
F32 = jnp.float32


def two_sum(a, b):
    s = a + b
    t = s - a
    return s, (a - (s - t)) + (b - t)


def fold(block):
    return jnp.sum(block.reshape(block.shape[0] // 8, 8, LANES), axis=0)


def bearing_ends(spans):
    piers = spans.shape[1]
    upto = (
        lax.broadcasted_iota(jnp.int32, (piers, 2 * piers), 0)
        <= lax.broadcasted_iota(jnp.int32, (piers, 2 * piers), 1) // 2
    ).astype(F32)
    return (
        jnp.dot(
            jnp.broadcast_to(spans.astype(F32), (8, piers)),
            upto,
            precision=HIGHEST,
            preferred_element_type=F32,
        )[0:1]
        - 1.0
    )


def bearing_hits(ends, start):
    bearings = ends.shape[1]
    along = lax.broadcasted_iota(jnp.int32, (LANES, bearings), 0) + start
    side = lax.rem(lax.broadcasted_iota(jnp.int32, (LANES, bearings), 1), 2)
    here = along.astype(F32) == ends
    return [jnp.where(here & (side == s), 1.0, 0.0).astype(F32) for s in range(2)]


def krylov_kernel(
    sizes,
    b_ref,
    mass_ref,
    spans_ref,
    inc_ref,
    solved_ref,
    coefficients_ref,
    sites_ref,
    v0,
    v1,
    v2,
    out1_ref,
    out2_ref,
    out3_ref,
    mass,
    w,
    x0,
    x1,
    x2,
    x3,
    strip_mass,
    strip_w,
    near_left,
    near_right,
    valid,
    back,
    hit,
    spans,
    part,
    slots,
    site_a,
    site_b,
    site_slots_a,
    site_slots_b,
    in_sem,
    halo_send,
    halo_recv,
    all_send,
    all_recv,
    ready,
    site_a_send,
    site_a_recv,
    site_b_send,
    site_b_recv,
):
    len_size, xs_size = sizes
    count = len_size * xs_size
    at_len, at_xs = lax.axis_index("len"), lax.axis_index("xs")
    me = at_len * xs_size + at_xs
    left, right = lax.rem(me + count - 1, count), lax.rem(me + 1, count)
    place = lambda i: (i // xs_size, lax.rem(i, xs_size))
    group_a = [(at_len, lax.rem(at_xs + k, xs_size)) for k in range(1, xs_size)]
    group_b = [(lax.rem(at_len + k, len_size), at_xs) for k in range(1, len_size)]

    barrier = pltpu.get_barrier_semaphore()
    partners = [place(left), place(right)] + group_b + group_a
    for partner in partners:
        pl.semaphore_signal(barrier, inc=1, device_id=partner, device_id_type=MESH)

    spans_copy = pltpu.make_async_copy(spans_ref, spans, in_sem.at[4])
    spans_copy.start()
    for c in range(3):

        def load(d, carry, c=c):
            pltpu.make_async_copy(
                b_ref.at[c, pl.ds(d * NS, NS)],
                v0.at[c, pl.ds((d + 1) * PITCH, NS)],
                in_sem.at[c],
            ).start()
            return carry

        lax.fori_loop(0, DEPTH, load, 0)
    pltpu.make_async_copy(mass_ref, mass, in_sem.at[3]).start()

    def guard(d, carry):
        row = (d + 1) * PITCH + NS
        for ref in (v0, v1, v2):
            for c in range(3):
                ref[c, pl.ds(row, 8)] = jnp.zeros((8, LANES), F32)
        w[pl.ds(row, 8)] = jnp.zeros((8, LANES), F32)
        return carry

    lax.fori_loop(0, DEPTH, guard, 0)
    for start in (0, (DEPTH + 1) * PITCH):
        for ref in (v0, v1, v2):
            for c in range(3):
                ref[c, pl.ds(start, PITCH)] = jnp.zeros((PITCH, LANES), F32)
        w[pl.ds(start, PITCH)] = jnp.zeros((PITCH, LANES), F32)
    for c in range(3):
        for ref in (v0, v1, v2):
            ref[c, pl.ds((DEPTH + 2) * PITCH, PITCH)] = jnp.zeros((PITCH, LANES), F32)

    has_left = jnp.where(me > 0, 1.0, 0.0).astype(F32)
    has_right = jnp.where(me < count - 1, 1.0, 0.0).astype(F32)
    low = lax.broadcasted_iota(jnp.int32, (8, LANES), 1) < LANES // 2

    def guard_strip(p, carry):
        row = p * SECTION + 8
        for ref in (x0, x1, x2):
            for c in range(3):
                ref[c, pl.ds(row, 8)] = jnp.zeros((8, LANES), F32)
        strip_w[pl.ds(row, 8)] = jnp.zeros((8, LANES), F32)
        valid[p] = jnp.where(
            low,
            jnp.where(p < HALO, has_left, 1.0),
            jnp.where(p >= 2 * HALO, has_right, 1.0),
        )
        return carry

    lax.fori_loop(0, WIDE, guard_strip, 0)

    spans_copy.wait()
    hits = bearing_hits(bearing_ends(spans[...]), me * LANES)
    for s in range(2):
        hit[s] = hits[s]

    for c in range(4):
        if c < 3:
            pltpu.make_async_copy(
                b_ref.at[c], v0.at[c, pl.ds(0, DEPTH * NS)], in_sem.at[c]
            ).wait()
        else:
            pltpu.make_async_copy(mass_ref, mass, in_sem.at[3]).wait()

        def edges(i, carry, c=c):
            for j in range(4):
                t = i * 4 + j
                if c < 3:
                    tile = jnp.concatenate(
                        [v0[c, pl.ds((2 * t + 1 + e) * PITCH, NS)] for e in range(2)], axis=0
                    )
                else:
                    tile = mass[pl.ds(t * LANES, LANES)]
                turned = tile.T
                at = c * PAIRS + t
                pitch = 4 * PAIRS
                near_left[pl.ds(LANDED + at, 8, stride=pitch), :] = turned[0:8]
                near_left[pl.ds(LANDED + 8 * pitch + at, 4, stride=pitch), :] = turned[8:12]
                near_right[pl.ds(at, 4, stride=pitch), :] = turned[LANES - 12 : LANES - 8]
                near_right[pl.ds(4 * pitch + at, 8, stride=pitch), :] = turned[LANES - 8 :]
            return carry

        lax.fori_loop(0, PAIRS // 4, edges, 0)

    pl.semaphore_wait(barrier, len(partners))
    middle = pl.ds(LANDED, LANDED)
    halos = [
        pltpu.make_async_remote_copy(
            src_ref=near_left.at[middle],
            dst_ref=near_right.at[pl.ds(2 * LANDED, LANDED)],
            send_sem=halo_send.at[0],
            recv_sem=halo_recv.at[0],
            device_id=place(left),
            device_id_type=MESH,
        ),
        pltpu.make_async_remote_copy(
            src_ref=near_right.at[middle],
            dst_ref=near_left.at[pl.ds(0, LANDED)],
            send_sem=halo_send.at[1],
            recv_sem=halo_recv.at[1],
            device_id=place(right),
            device_id_type=MESH,
        ),
    ]
    for copy in halos:
        copy.start()
    for partner in group_a:
        pl.semaphore_signal(ready, inc=1, device_id=partner, device_id_type=MESH)


    def apply(source, target, last, dots):
        quarter = 0.25 * bulk_modulus

        def divergence(base, scale):
            first = source[0, pl.ds(base, NS)]
            along = pltpu.roll(first, LANES - 1, 1) - pltpu.roll(first, 1, 1)
            across = source[1, pl.ds(base + 1, NS)] - source[1, pl.ds(base - 1, NS)]
            depth = source[2, pl.ds(base + PITCH, NS)] - source[2, pl.ds(base - PITCH, NS)]
            return scale * (along + across + depth)

        w[pl.ds(PITCH, NS)] = divergence(PITCH, quarter)
        zero = jnp.zeros((8, LANES), F32)

        def body(d, sums):
            base = (d + 1) * PITCH
            heavy = mass[pl.ds(d * NS, NS)] + 6.0
            ahead = divergence(base + PITCH, jnp.where(d < DEPTH - 1, quarter, 0.0))
            local = w[pl.ds(base, NS)]
            beside = (
                w[pl.ds(base + 1, NS)] - w[pl.ds(base - 1, NS)],
                ahead - w[pl.ds(base - PITCH, NS)],
            )
            terms = [zero] * len(dots)
            for c in range(3):
                here = source[c, pl.ds(base, NS)]
                if c == 0:
                    swept = pltpu.roll(here + local, LANES - 1, 1) + pltpu.roll(
                        here - local, 1, 1
                    )
                else:
                    swept = (
                        pltpu.roll(here, LANES - 1, 1)
                        + pltpu.roll(here, 1, 1)
                        + beside[c - 1]
                    )
                image = heavy * here
                image = image - (
                    source[c, pl.ds(base + 1, NS)] + source[c, pl.ds(base - 1, NS)]
                )
                image = image - (
                    source[c, pl.ds(base + PITCH, NS)] + source[c, pl.ds(base - PITCH, NS)]
                )
                image = image - swept
                if last:
                    target[c, pl.ds(d * NS, NS)] = image
                else:
                    target[c, pl.ds(base, NS)] = image
                for n, kind in enumerate(dots):
                    terms[n] = terms[n] + fold(
                        {"vv": here * here, "vi": here * image, "ii": image * image}[kind]
                    )
            w[pl.ds(base + PITCH, NS)] = ahead
            return tuple(s + t for s, t in zip(sums, terms))

        return lax.fori_loop(0, DEPTH, body, (zero,) * len(dots), unroll=UNROLL)

    mu0, mu1, mu2 = apply(v0, v1, False, ("vv", "vi", "ii"))
    mu3, mu4 = apply(v1, v2, False, ("vi", "ii"))
    (mu5,) = apply(v2, out3_ref, True, ("vi",))
    lane = lax.broadcasted_iota(jnp.int32, (8, LANES), 1)
    inner = (lane >= HALO) & (lane < LANES - HALO)
    moments = tuple(jnp.where(inner, mu, 0.0) for mu in (mu0, mu1, mu2, mu3, mu4, mu5))

    half = LANES // 2
    for copy in halos:
        copy.wait_recv()

    def mix(first, second):
        turned = pltpu.roll(jnp.where(low, second, first), half, 1)
        return jnp.where(low, first, turned), jnp.where(low, turned, second)

    def gather(p, carry):
        for c in range(4):
            at = pl.ds(pl.multiple_of((p * 4 + c) * PAIRS, 8), PAIRS)
            even, odd = mix(near_left[at], near_right[at])
            for part, value in ((0, even), (16, odd)):
                to = pl.ds(pl.multiple_of(p * SECTION + part, 8), 8)
                if c < 3:
                    x0[c, to] = value * valid[p]
                else:
                    strip_mass[to] = value
        return carry

    lax.fori_loop(0, WIDE, gather, 0, unroll=6)

    across_at = lax.rem(lax.broadcasted_iota(jnp.int32, (8, LANES), 1), half)

    def after(x):
        return jnp.where(across_at == half - 1, 0.0, pltpu.roll(x, LANES - 1, 1))

    def before(x):
        return jnp.where(across_at == 0, 0.0, pltpu.roll(x, 1, 1))

    def rows(ref, row):
        return ref[pl.ds(row, 8)], ref[pl.ds(row + 16, 8)]

    def beside(ref, row, pair):
        even, odd = pair
        return (odd, ref[pl.ds(row + 15, 8)]), (ref[pl.ds(row + 1, 8)], even)

    xs = (x0, x1, x2, x3)
    def exchange(source, slots, partners, own, send_sems, recv_sems):
        copies = []
        for k, partner in enumerate(partners):
            copy = pltpu.make_async_remote_copy(
                src_ref=source,
                dst_ref=slots.at[own],
                send_sem=send_sems.at[k],
                recv_sem=recv_sems.at[k],
                device_id=partner,
                device_id_type=MESH,
            )
            copy.start()
            copies.append(copy)
        slots[own] = source[...]
        return copies

    def tree(parts, join):
        while len(parts) > 1:
            joined = [join(parts[i], parts[i + 1]) for i in range(0, len(parts) - 1, 2)]
            parts = joined + parts[len(parts) - len(parts) % 2 :]
        return parts[0]

    def join(p, q):
        hi, more = two_sum(p[0], q[0])
        return hi, p[1] + q[1] + more

    edge_rows = 16 * PAIRS
    lanes = lax.broadcasted_iota(jnp.int32, (LANES, LANES), 1)
    outer = (lanes < HALO) | (lanes >= LANES - HALO)
    mains = (v1, v2, None)
    outs = (out1_ref, out2_ref, out3_ref)

    def back_edges(i, carry, ks=(0, 1, 2)):
        for k in ks:
            for c in range(3):
                even, odd = rows(xs[k + 1].at[c], (i + HALO) * SECTION)
                first, second = mix(even, odd)
                slot = (k * 3 + c) * edge_rows
                back[pl.ds(slot + (8 + i) * PAIRS, PAIRS)] = first
                back[pl.ds(slot + (2 + i) * PAIRS, PAIRS)] = second
        return carry

    def merge(k, c, t):
        slot = (k * 3 + c) * edge_rows + t
        edge = jnp.concatenate(
            [
                back[pl.ds(slot + 8 * PAIRS, 8, stride=PAIRS), :],
                jnp.zeros((LANES - 16, LANES), F32),
                back[pl.ds(slot, 8, stride=PAIRS), :],
            ],
            axis=0,
        ).T
        if k < 2:
            main = jnp.concatenate(
                [mains[k][c, pl.ds((2 * t + 1 + e) * PITCH, NS)] for e in range(2)], axis=0
            )
        else:
            main = out3_ref[c, pl.ds(t * LANES, LANES)]
        outs[k][c, pl.ds(t * LANES, LANES)] = jnp.where(outer, edge, main)

    zero = jnp.zeros((8, LANES), F32)
    sums = (zero,) * 6
    for k in range(3):
        if k == 2:
            for slot in range(9):
                for r in (0, 1, 14, 15):
                    back[pl.ds(slot * edge_rows + r * PAIRS, PAIRS)] = jnp.zeros((PAIRS, LANES), F32)
            for i in range(HALO):
                back_edges(i, 0, (0, 1))
            for n in (0, 1):
                for c in (0, 1):
                    merge(n, c, 0)

            site = jnp.zeros((8, 2 * LANES), F32)
            for s, across in ((0, NS // 4), (1, 3 * NS // 4)):
                picked = [v0[c, pl.ds(PITCH + across, 1)] for c in (0, 1)]
                picked += [out1_ref[c, pl.ds(across, 1)] for c in (0, 1)]
                picked += [out2_ref[c, pl.ds(across, 1)] for c in (0, 1)]
                picked += [jnp.zeros((2, LANES), F32)]
                site = site + jnp.dot(
                    jnp.concatenate(picked, axis=0),
                    hit[s],
                    precision=HIGHEST,
                    preferred_element_type=F32,
                )
            site_a[...] = jnp.concatenate([site[:, :LANES], site[:, LANES:]], axis=0)
        source, target = xs[k], xs[k + 1]

        def strip_divergence(i, carry, k=k, source=source):
            p = i + 2 * k + 1
            row = p * SECTION
            first, second = rows(source.at[0], row - SECTION), rows(source.at[0], row + SECTION)
            middle = rows(source.at[1], row)
            third = beside(source.at[2], row, rows(source.at[2], row))
            for e in range(2):
                strip_w[pl.ds(row + 16 * e, 8)] = (
                    (0.25 * bulk_modulus)
                    * (
                        (second[e] - first[e])
                        + (after(middle[e]) - before(middle[e]))
                        + (third[e][0] - third[e][1])
                    )
                    * valid[p]
                )
            return carry

        lax.fori_loop(0, WIDE - 2 - 4 * k, strip_divergence, 0, unroll=DIV_UNROLL[k])

        def strip_image(i, sums, k=k, source=source, target=target):
            p = i + 2 * k + 2
            row = p * SECTION
            heavy = rows(strip_mass, row)
            local = rows(strip_w, row)
            around = rows(strip_w, row - SECTION), rows(strip_w, row + SECTION)
            upright = beside(strip_w, row, local)
            images, heres = [], []
            for c in range(3):
                ref = source.at[c]
                here = rows(ref, row)
                along = rows(ref, row - SECTION), rows(ref, row + SECTION)
                depth = beside(ref, row, here)
                for e in range(2):
                    image = (heavy[e] + 6.0) * here[e] - (along[0][e] + along[1][e])
                    image = image - (depth[e][0] + depth[e][1])
                    if c == 1:
                        image = image - (after(here[e] + local[e]) + before(here[e] - local[e]))
                    else:
                        image = image - (after(here[e]) + before(here[e]))
                    if c == 0:
                        image = image - (around[1][e] - around[0][e])
                    elif c == 2:
                        image = image - (upright[e][0] - upright[e][1])
                    images.append(image * valid[p])
                    heres.append(here[e])
            sums = list(sums)
            for n, (image, here) in enumerate(zip(images, heres)):
                at = pl.ds(row + 16 * (n % 2), 8)
                target[n // 2, at] = image
                if k == 2:
                    z0, z1 = x0[n // 2, at], x1[n // 2, at]
                    for m, (p0, p1) in enumerate(
                        ((z0, z0), (z0, z1), (z1, z1), (z1, here), (here, here), (here, image))
                    ):
                        sums[m] = sums[m] + p0 * p1
            return tuple(sums)

        sums = lax.fori_loop(0, WIDE - 4 - 4 * k, strip_image, sums, unroll=IMG_UNROLL[k])
    strips = sums

    head, rest = [], []
    for n in range(6):
        hi, lo = two_sum(moments[n], strips[n])
        for shift in (4, 2, 1):
            hi, more = two_sum(hi, pltpu.roll(hi, shift, 0))
            lo = lo + pltpu.roll(lo, shift, 0) + more
        head.append(hi[0:1])
        rest.append(lo[0:1])
    blank = [jnp.zeros((2, LANES), F32)]
    hi, lo = jnp.concatenate(head + blank, axis=0), jnp.concatenate(rest + blank, axis=0)
    for shift in (64, 32, 16, 8, 4, 2, 1):
        hi, more = two_sum(hi, pltpu.roll(hi, shift, 1))
        lo = lo + pltpu.roll(lo, shift, 1) + more
    hi, lo = two_sum(hi, lo)
    sublane = lax.broadcasted_iota(jnp.int32, (8, LANES), 0)
    at_hi, at_lo = lane == sublane, lane == sublane + 8
    packed = jnp.sum(jnp.where(at_hi, hi, 0.0) + jnp.where(at_lo, lo, 0.0), axis=0, keepdims=True)
    part[...] = packed

    copies = exchange(site_a, site_slots_a, group_a, at_xs, site_a_send, site_a_recv)
    copies_a = copies

    pl.semaphore_wait(ready, len(group_a))
    ring = lambda a, n: min(a, n - a)
    far = lambda o: -(ring(o[0] // 4, 4) + ring(o[0] % 4, 4) + ring(o[1] // 2, 4))
    offsets = [(a, b) for a in range(len_size) for b in range(xs_size) if a or b]
    lens = [lax.rem(at_len + a, len_size) for a in range(len_size)]
    spots = [lax.rem(at_xs + b, xs_size) for b in range(xs_size)]
    for a, b in sorted(offsets, key=far):
        pltpu.make_async_remote_copy(
            src_ref=part,
            dst_ref=slots.at[pl.ds(me, 1)],
            send_sem=all_send,
            recv_sem=all_recv,
            device_id=(lens[a], spots[b]),
            device_id_type=MESH,
        ).start()
    slots[pl.ds(me, 1)] = part[...]

    for i in range(HALO):
        back_edges(i, 0, (2,))
    merge(0, 2, 0)
    merge(1, 2, 0)
    for c in range(3):
        merge(2, c, 0)

    for copy in copies_a:
        copy.wait_recv()
    site_b[...] = tree([site_slots_a[i] for i in range(xs_size)], jnp.add)
    copies_b = exchange(site_b, site_slots_b, group_b, at_len, site_b_send, site_b_recv)

    def merge_rest(t, carry):
        for k in range(3):
            for c in range(3):
                merge(k, c, t)
        return carry

    lax.fori_loop(1, PAIRS, merge_rest, 0)

    others = slots.at[pl.ds(0, count - 1)]
    pltpu.make_async_copy(others, others, all_recv).wait()
    hi, lo = tree(
        [(slots[pl.ds(8 * i, 8)], jnp.zeros((8, LANES), F32)) for i in range(count // 8)], join
    )
    for shift in (4, 2, 1):
        hi, more = two_sum(hi, pltpu.roll(hi, shift, 0))
        lo = lo + pltpu.roll(lo, shift, 0) + more
    pick = lambda mask, x: jnp.broadcast_to(
        jnp.sum(jnp.where(mask, x, 0.0), axis=1, keepdims=True), (8, LANES)
    )
    increment, solved = steps(pick(at_hi, hi), pick(at_lo, hi) + pick(at_hi, lo))
    coefficients_ref[...] = jnp.concatenate(
        list(increment) + list(solved) + [jnp.zeros((1, LANES), F32)], axis=0
    )

    def combine(d, carry):
        at = pl.ds(pl.multiple_of(d * NS, NS), NS)
        for c in range(3):
            p0 = v0[c, pl.ds((d + 1) * PITCH, NS)]
            p1, p2, p3 = out1_ref[c, at], out2_ref[c, at], out3_ref[c, at]
            inc_ref[c, at] = increment[0] * p0 + increment[1] * p1 + increment[2] * p2
            solved_ref[c, at] = (
                solved[0] * p0 + solved[1] * p1 + solved[2] * p2 + solved[3] * p3
            )
        return carry

    lax.fori_loop(0, DEPTH, combine, 0)

    for copy in copies_b:
        copy.wait_recv()
    sites_ref[...] = tree([site_slots_b[i] for i in range(len_size)], jnp.add)
    pltpu.make_async_copy(others, others, all_send).wait()
    for copy in halos + copies_a + copies_b:
        copy.wait_send()


def steps(hi, lo):
    for shift in (64, 32, 16, 8, 4, 2, 1):
        hi, more = two_sum(hi, pltpu.roll(hi, shift, 1))
        lo = lo + pltpu.roll(lo, shift, 1) + more
    hi, lo = two_sum(hi, lo)
    theta = jnp.round(hi[1:2] / hi[0:1] * 64.0) * (1.0 / 64.0)
    central = [hi[0:1]]
    for order in range(5):
        n = 5 - order
        big = hi[:n] * 4097.0
        upper = big - (big - hi[:n])
        lower = hi[:n] - upper
        value, more = two_sum(hi[1 : n + 1], -theta * upper)
        value, extra = two_sum(value, -theta * lower)
        low_part = lo[1 : n + 1] - theta * lo[:n] + (more + extra)
        hi, lo = two_sum(value, low_part)
        central.append(hi[0:1])
    scale = 1.0 / central[0]
    c = [x * scale for x in central]
    c1 = [c[i + 1] + theta * c[i] for i in range(5)]

    def form(p, moments):
        terms = None
        for i in range(len(p)):
            for j in range(i, len(p)):
                term = (1.0 if i == j else 2.0) * (p[i] * p[j]) * moments[i + j]
                terms = term if terms is None else terms + term
        return terms

    one, zero = jnp.ones_like(theta), jnp.zeros_like(theta)
    left, ahead, norm = [one], [one], c[0]
    increment = [zero, zero, zero]
    for iteration in range(3):
        alpha = norm / form(ahead, c1)
        increment = [
            x + alpha * ahead[i] if i < len(ahead) else x for i, x in enumerate(increment)
        ]
        image = [theta * x for x in ahead] + [zero]
        image = [image[i] + (ahead[i - 1] if i else zero) for i in range(len(image))]
        left = left + [zero]
        left = [x - alpha * y for x, y in zip(left, image)]
        if iteration < 2:
            after = form(left, c)
            beta = after / norm
            ahead = ahead + [zero]
            ahead = [x + beta * y for x, y in zip(left, ahead)]
            norm = after
    x0, x1, x2 = increment
    r0, r1, r2, r3 = left
    increment = (x0 - theta * (x1 - theta * x2), x1 - 2.0 * theta * x2, x2)
    solved = (
        r0 - theta * (r1 - theta * (r2 - theta * r3)),
        r1 - theta * (2.0 * r2 - 3.0 * theta * r3),
        r2 - 3.0 * theta * r3,
        r3,
    )
    return increment, solved


def finish_kernel(
    increment_ref,
    solved_ref,
    coefficients_ref,
    sites_ref,
    spans_ref,
    stick_ref,
    load_ref,
    prior_ref,
    inc_ref,
    res_ref,
    friction_ref,
    first,
    out_sem,
):
    rows = DEPTH * NS
    at, top = pl.ds(NS, rows - NS), pl.ds(0, NS)
    stores = []

    def store(source, target):
        copy = pltpu.make_async_copy(source, target, out_sem.at[len(stores)])
        copy.start()
        stores.append(copy)

    for c in range(3):
        store(increment_ref.at[c], inc_ref.at[c])
        store(solved_ref.at[c, at], res_ref.at[c, at])

    me = lax.axis_index("len") * lax.axis_size("xs") + lax.axis_index("xs")

    wide = lambda n: jnp.concatenate([coefficients_ref[pl.ds(n, 1)]] * 2, axis=1)
    site = jnp.concatenate([sites_ref[0:8], sites_ref[8:16]], axis=1)
    readout = wide(0) * site[0:2] + wide(1) * site[2:4] + wide(2) * site[4:6]
    radius = jnp.where(stick_ref[...] == 1, static_friction, kinetic_friction) * load_ref[...]
    trial = prior_ref[...] + elastic_stiffness * readout
    magnitude = jnp.sqrt(trial[0:1] * trial[0:1] + trial[1:2] * trial[1:2])
    friction = trial * (radius / jnp.maximum(magnitude, radius))
    friction_ref[...] = friction
    force = friction + load_ref[...] / pendulum_radius * readout
    bearings = force.shape[1]
    forces = jnp.concatenate(
        [force, jnp.ones((1, bearings), F32), jnp.zeros((5, bearings), F32)], axis=0
    )
    hits = bearing_hits(bearing_ends(spans_ref[...]), me * LANES)
    placed = [
        lax.dot_general(
            forces,
            hit,
            (((1,), (1,)), ((), ())),
            precision=HIGHEST,
            preferred_element_type=F32,
        )
        for hit in hits
    ]
    for c in range(3):
        first[c] = solved_ref[c, top]
        for s, across in ((0, NS // 4), (1, 3 * NS // 4)):
            node = pl.ds(across, 1)
            if c < 2:
                drop = placed[s][c : c + 1]
            else:
                drop = vertical_stiffness * increment_ref[c, node] * placed[s][2:3]
            first[c, node] = first[c, node] - drop
        store(first.at[c], res_ref.at[c, top])
    for copy in stores:
        copy.wait()


def shards(right_side, mass_field, span_lengths, stick_flags, normal_load, prior_friction):
    sizes = (lax.axis_size("len"), lax.axis_size("xs"))
    count = sizes[0] * sizes[1]
    rows = DEPTH * NS
    field = (3, rows, LANES)
    b = right_side.reshape(field)
    mass = mass_field.reshape(rows, LANES)
    spans = span_lengths.reshape(1, -1)
    stick = stick_flags.reshape(1, -1)
    load = normal_load.reshape(1, -1)
    anywhere = pl.BlockSpec(memory_space=pl.ANY)
    hbm = pl.BlockSpec(memory_space=pltpu.HBM)
    far = lambda a: pltpu.with_memory_space_constraint(a, pltpu.HBM)
    vmem = pl.BlockSpec(memory_space=pltpu.VMEM)
    increment, solved, coefficients, sites = pl.pallas_call(
        lambda *refs: krylov_kernel(sizes, *refs),
        name="krylov",
        out_shape=[pltpu.VMEM(field, F32)] * 2
        + [pltpu.VMEM((8, LANES), F32), pltpu.VMEM((16, LANES), F32)],
        in_specs=[hbm] * 3,
        out_specs=[vmem] * 4,
        scratch_shapes=[pltpu.VMEM((3, PADDED, LANES), F32)] * 3
        + [pltpu.VMEM(field, F32)] * 3
        + [pltpu.VMEM((rows, LANES), F32), pltpu.VMEM((PADDED, LANES), F32)]
        + [pltpu.VMEM((3, STRIP, LANES), F32)] * 4
        + [pltpu.VMEM((STRIP, LANES), F32)] * 2
        + [pltpu.VMEM((OWN + LANDED, LANES), F32)] * 2
        + [
            pltpu.VMEM((WIDE, 8, LANES), F32),
            pltpu.VMEM((9 * 16 * PAIRS, LANES), F32),
            pltpu.VMEM((2, LANES, 2 * LANES), F32),
            pltpu.VMEM(spans.shape, jnp.int32),
        ]
        + [pltpu.VMEM((1, LANES), F32), pltpu.VMEM((count, LANES), F32)]
        + [pltpu.VMEM((16, LANES), F32)] * 2
        + [pltpu.VMEM((n, 16, LANES), F32) for n in (sizes[1], sizes[0])]
        + [pltpu.SemaphoreType.DMA((n,)) for n in (5, 2, 2)]
        + [pltpu.SemaphoreType.DMA, pltpu.SemaphoreType.DMA, pltpu.SemaphoreType.REGULAR]
        + [pltpu.SemaphoreType.DMA((n,)) for n in (sizes[1], sizes[1], sizes[0], sizes[0])],
        compiler_params=pltpu.CompilerParams(
            collective_id=0, has_side_effects=True, vmem_limit_bytes=32 * 2**20
        ),
    )(far(b), far(mass), far(spans))
    increment, residual, friction = pl.pallas_call(
        finish_kernel,
        name="finish",
        out_shape=[
            jax.ShapeDtypeStruct(field, F32),
            jax.ShapeDtypeStruct(field, F32),
            jax.ShapeDtypeStruct(prior_friction.shape, F32),
        ],
        in_specs=[vmem] * 8,
        out_specs=[anywhere, anywhere, vmem],
        scratch_shapes=[
            pltpu.VMEM((3, NS, LANES), F32),
            pltpu.SemaphoreType.DMA((9,)),
        ],
        compiler_params=pltpu.CompilerParams(vmem_limit_bytes=24 * 2**20),
    )(increment, solved, coefficients, sites, spans, stick, load, prior_friction)
    return (
        increment.reshape(right_side.shape),
        residual.reshape(right_side.shape),
        friction,
    )


def solution(mesh):
    along = ("len", "xs")
    in_specs = (P(None, None, None, along), P(None, None, along), P(), P(), P(), P())
    out_specs = (P(None, None, None, along), P(None, None, None, along), P())
    return jax.shard_map(shards, mesh=mesh, in_specs=in_specs, out_specs=out_specs, check_vma=False)
```

```python
import jax
import jax.numpy as jnp
from jax import lax
from jax.experimental import pallas as pl
from jax.experimental.pallas import tpu as pltpu
from jax.sharding import PartitionSpec as P

shear_modulus = 1.0
bulk_modulus = 1.5
elastic_stiffness = 8.0
pendulum_radius = 4.0
vertical_stiffness = 5.0
static_friction = 0.6
kinetic_friction = 0.45

DEPTH = 16
NS = 64
LANES = 128
PITCH = NS + 8
PADDED = (DEPTH + 3) * PITCH
HALO = 6
PAIRS = DEPTH * NS // LANES
WIDE = 3 * HALO
SECTION = 24
STRIP = WIDE * SECTION
OWN = 2 * HALO * 4 * PAIRS
LANDED = HALO * 4 * PAIRS

UNROLL = 8
DIV_UNROLL = (16, 12, 8)
IMG_UNROLL = (14, 10, 6)

MESH = pl.DeviceIdType.MESH
HIGHEST = lax.Precision.HIGHEST
F32 = jnp.float32


def two_sum(a, b):
    s = a + b
    t = s - a
    return s, (a - (s - t)) + (b - t)


def fold(block):
    return jnp.sum(block.reshape(block.shape[0] // 8, 8, LANES), axis=0)


def bearing_ends(spans):
    piers = spans.shape[1]
    upto = (
        lax.broadcasted_iota(jnp.int32, (piers, 2 * piers), 0)
        <= lax.broadcasted_iota(jnp.int32, (piers, 2 * piers), 1) // 2
    ).astype(F32)
    return (
        jnp.dot(
            jnp.broadcast_to(spans.astype(F32), (8, piers)),
            upto,
            precision=HIGHEST,
            preferred_element_type=F32,
        )[0:1]
        - 1.0
    )


def bearing_hits(ends, start):
    bearings = ends.shape[1]
    along = lax.broadcasted_iota(jnp.int32, (LANES, bearings), 0) + start
    side = lax.rem(lax.broadcasted_iota(jnp.int32, (LANES, bearings), 1), 2)
    here = along.astype(F32) == ends
    return [jnp.where(here & (side == s), 1.0, 0.0).astype(F32) for s in range(2)]


def krylov_kernel(
    sizes,
    b_ref,
    mass_ref,
    spans_ref,
    inc_ref,
    solved_ref,
    coefficients_ref,
    sites_ref,
    v0,
    v1,
    v2,
    out1_ref,
    out2_ref,
    out3_ref,
    mass,
    w,
    x0,
    x1,
    x2,
    x3,
    strip_mass,
    strip_w,
    near_left,
    near_right,
    valid,
    back,
    hit,
    spans,
    part,
    slots,
    site_a,
    site_b,
    site_slots_a,
    site_slots_b,
    in_sem,
    halo_send,
    halo_recv,
    all_send,
    all_recv,
    ready,
    site_a_send,
    site_a_recv,
    site_b_send,
    site_b_recv,
):
    len_size, xs_size = sizes
    count = len_size * xs_size
    at_len, at_xs = lax.axis_index("len"), lax.axis_index("xs")
    me = at_len * xs_size + at_xs
    left, right = lax.rem(me + count - 1, count), lax.rem(me + 1, count)
    place = lambda i: (i // xs_size, lax.rem(i, xs_size))
    group_a = [(at_len, lax.rem(at_xs + k, xs_size)) for k in range(1, xs_size)]
    group_b = [(lax.rem(at_len + k, len_size), at_xs) for k in range(1, len_size)]

    barrier = pltpu.get_barrier_semaphore()
    partners = [place(left), place(right)] + group_b + group_a
    for partner in partners:
        pl.semaphore_signal(barrier, inc=1, device_id=partner, device_id_type=MESH)

    spans_copy = pltpu.make_async_copy(spans_ref, spans, in_sem.at[4])
    spans_copy.start()
    for c in range(3):

        def load(d, carry, c=c):
            pltpu.make_async_copy(
                b_ref.at[c, pl.ds(d * NS, NS)],
                v0.at[c, pl.ds((d + 1) * PITCH, NS)],
                in_sem.at[c],
            ).start()
            return carry

        lax.fori_loop(0, DEPTH, load, 0)
    pltpu.make_async_copy(mass_ref, mass, in_sem.at[3]).start()

    def guard(d, carry):
        row = (d + 1) * PITCH + NS
        for ref in (v0, v1, v2):
            for c in range(3):
                ref[c, pl.ds(row, 8)] = jnp.zeros((8, LANES), F32)
        w[pl.ds(row, 8)] = jnp.zeros((8, LANES), F32)
        return carry

    lax.fori_loop(0, DEPTH, guard, 0)
    for start in (0, (DEPTH + 1) * PITCH):
        for ref in (v0, v1, v2):
            for c in range(3):
                ref[c, pl.ds(start, PITCH)] = jnp.zeros((PITCH, LANES), F32)
        w[pl.ds(start, PITCH)] = jnp.zeros((PITCH, LANES), F32)
    for c in range(3):
        for ref in (v0, v1, v2):
            ref[c, pl.ds((DEPTH + 2) * PITCH, PITCH)] = jnp.zeros((PITCH, LANES), F32)

    has_left = jnp.where(me > 0, 1.0, 0.0).astype(F32)
    has_right = jnp.where(me < count - 1, 1.0, 0.0).astype(F32)
    low = lax.broadcasted_iota(jnp.int32, (8, LANES), 1) < LANES // 2

    def guard_strip(p, carry):
        row = p * SECTION + 8
        for ref in (x0, x1, x2):
            for c in range(3):
                ref[c, pl.ds(row, 8)] = jnp.zeros((8, LANES), F32)
        strip_w[pl.ds(row, 8)] = jnp.zeros((8, LANES), F32)
        valid[p] = jnp.where(
            low,
            jnp.where(p < HALO, has_left, 1.0),
            jnp.where(p >= 2 * HALO, has_right, 1.0),
        )
        return carry

    lax.fori_loop(0, WIDE, guard_strip, 0)

    spans_copy.wait()
    hits = bearing_hits(bearing_ends(spans[...]), me * LANES)
    for s in range(2):
        hit[s] = hits[s]

    for c in range(4):
        if c < 3:
            pltpu.make_async_copy(
                b_ref.at[c], v0.at[c, pl.ds(0, DEPTH * NS)], in_sem.at[c]
            ).wait()
        else:
            pltpu.make_async_copy(mass_ref, mass, in_sem.at[3]).wait()

        def edges(i, carry, c=c):
            for j in range(4):
                t = i * 4 + j
                if c < 3:
                    tile = jnp.concatenate(
                        [v0[c, pl.ds((2 * t + 1 + e) * PITCH, NS)] for e in range(2)], axis=0
                    )
                else:
                    tile = mass[pl.ds(t * LANES, LANES)]
                turned = tile.T
                at = c * PAIRS + t
                pitch = 4 * PAIRS
                near_left[pl.ds(LANDED + at, 8, stride=pitch), :] = turned[0:8]
                near_left[pl.ds(LANDED + 8 * pitch + at, 4, stride=pitch), :] = turned[8:12]
                near_right[pl.ds(at, 4, stride=pitch), :] = turned[LANES - 12 : LANES - 8]
                near_right[pl.ds(4 * pitch + at, 8, stride=pitch), :] = turned[LANES - 8 :]
            return carry

        lax.fori_loop(0, PAIRS // 4, edges, 0)

    pl.semaphore_wait(barrier, len(partners))
    middle = pl.ds(LANDED, LANDED)
    halos = [
        pltpu.make_async_remote_copy(
            src_ref=near_left.at[middle],
            dst_ref=near_right.at[pl.ds(2 * LANDED, LANDED)],
            send_sem=halo_send.at[0],
            recv_sem=halo_recv.at[0],
            device_id=place(left),
            device_id_type=MESH,
        ),
        pltpu.make_async_remote_copy(
            src_ref=near_right.at[middle],
            dst_ref=near_left.at[pl.ds(0, LANDED)],
            send_sem=halo_send.at[1],
            recv_sem=halo_recv.at[1],
            device_id=place(right),
            device_id_type=MESH,
        ),
    ]
    for copy in halos:
        copy.start()
    for partner in group_a:
        pl.semaphore_signal(ready, inc=1, device_id=partner, device_id_type=MESH)


    def apply(source, target, last, dots):
        quarter = 0.25 * bulk_modulus

        def divergence(base, scale):
            first = source[0, pl.ds(base, NS)]
            along = pltpu.roll(first, LANES - 1, 1) - pltpu.roll(first, 1, 1)
            across = source[1, pl.ds(base + 1, NS)] - source[1, pl.ds(base - 1, NS)]
            depth = source[2, pl.ds(base + PITCH, NS)] - source[2, pl.ds(base - PITCH, NS)]
            return scale * (along + across + depth)

        w[pl.ds(PITCH, NS)] = divergence(PITCH, quarter)
        zero = jnp.zeros((8, LANES), F32)

        def body(d, sums):
            base = (d + 1) * PITCH
            heavy = mass[pl.ds(d * NS, NS)] + 6.0
            ahead = divergence(base + PITCH, jnp.where(d < DEPTH - 1, quarter, 0.0))
            local = w[pl.ds(base, NS)]
            beside = (
                w[pl.ds(base + 1, NS)] - w[pl.ds(base - 1, NS)],
                ahead - w[pl.ds(base - PITCH, NS)],
            )
            terms = [zero] * len(dots)
            for c in range(3):
                here = source[c, pl.ds(base, NS)]
                if c == 0:
                    swept = pltpu.roll(here + local, LANES - 1, 1) + pltpu.roll(
                        here - local, 1, 1
                    )
                else:
                    swept = (
                        pltpu.roll(here, LANES - 1, 1)
                        + pltpu.roll(here, 1, 1)
                        + beside[c - 1]
                    )
                image = heavy * here
                image = image - (
                    source[c, pl.ds(base + 1, NS)] + source[c, pl.ds(base - 1, NS)]
                )
                image = image - (
                    source[c, pl.ds(base + PITCH, NS)] + source[c, pl.ds(base - PITCH, NS)]
                )
                image = image - swept
                if last:
                    target[c, pl.ds(d * NS, NS)] = image
                else:
                    target[c, pl.ds(base, NS)] = image
                for n, kind in enumerate(dots):
                    terms[n] = terms[n] + fold(
                        {"vv": here * here, "vi": here * image, "ii": image * image}[kind]
                    )
            w[pl.ds(base + PITCH, NS)] = ahead
            return tuple(s + t for s, t in zip(sums, terms))

        return lax.fori_loop(0, DEPTH, body, (zero,) * len(dots), unroll=UNROLL)

    mu0, mu1, mu2 = apply(v0, v1, False, ("vv", "vi", "ii"))
    mu3, mu4 = apply(v1, v2, False, ("vi", "ii"))
    (mu5,) = apply(v2, out3_ref, True, ("vi",))
    lane = lax.broadcasted_iota(jnp.int32, (8, LANES), 1)
    inner = (lane >= HALO) & (lane < LANES - HALO)
    moments = tuple(jnp.where(inner, mu, 0.0) for mu in (mu0, mu1, mu2, mu3, mu4, mu5))

    half = LANES // 2
    for copy in halos:
        copy.wait_recv()

    def mix(first, second):
        turned = pltpu.roll(jnp.where(low, second, first), half, 1)
        return jnp.where(low, first, turned), jnp.where(low, turned, second)

    def gather(p, carry):
        for c in range(4):
            at = pl.ds(pl.multiple_of((p * 4 + c) * PAIRS, 8), PAIRS)
            even, odd = mix(near_left[at], near_right[at])
            for part, value in ((0, even), (16, odd)):
                to = pl.ds(pl.multiple_of(p * SECTION + part, 8), 8)
                if c < 3:
                    x0[c, to] = value * valid[p]
                else:
                    strip_mass[to] = value
        return carry

    lax.fori_loop(0, WIDE, gather, 0, unroll=6)

    across_at = lax.rem(lax.broadcasted_iota(jnp.int32, (8, LANES), 1), half)

    def after(x):
        return jnp.where(across_at == half - 1, 0.0, pltpu.roll(x, LANES - 1, 1))

    def before(x):
        return jnp.where(across_at == 0, 0.0, pltpu.roll(x, 1, 1))

    def rows(ref, row):
        return ref[pl.ds(row, 8)], ref[pl.ds(row + 16, 8)]

    def beside(ref, row, pair):
        even, odd = pair
        return (odd, ref[pl.ds(row + 15, 8)]), (ref[pl.ds(row + 1, 8)], even)

    xs = (x0, x1, x2, x3)
    def exchange(source, slots, partners, own, send_sems, recv_sems):
        copies = []
        for k, partner in enumerate(partners):
            copy = pltpu.make_async_remote_copy(
                src_ref=source,
                dst_ref=slots.at[own],
                send_sem=send_sems.at[k],
                recv_sem=recv_sems.at[k],
                device_id=partner,
                device_id_type=MESH,
            )
            copy.start()
            copies.append(copy)
        slots[own] = source[...]
        return copies

    def tree(parts, join):
        while len(parts) > 1:
            joined = [join(parts[i], parts[i + 1]) for i in range(0, len(parts) - 1, 2)]
            parts = joined + parts[len(parts) - len(parts) % 2 :]
        return parts[0]

    def join(p, q):
        hi, more = two_sum(p[0], q[0])
        return hi, p[1] + q[1] + more

    edge_rows = 16 * PAIRS
    lanes = lax.broadcasted_iota(jnp.int32, (LANES, LANES), 1)
    outer = (lanes < HALO) | (lanes >= LANES - HALO)
    mains = (v1, v2, None)
    outs = (out1_ref, out2_ref, out3_ref)

    def back_edges(i, carry, ks=(0, 1, 2)):
        for k in ks:
            for c in range(3):
                even, odd = rows(xs[k + 1].at[c], (i + HALO) * SECTION)
                first, second = mix(even, odd)
                slot = (k * 3 + c) * edge_rows
                back[pl.ds(slot + (8 + i) * PAIRS, PAIRS)] = first
                back[pl.ds(slot + (2 + i) * PAIRS, PAIRS)] = second
        return carry

    def merge(k, c, t):
        slot = (k * 3 + c) * edge_rows + t
        edge = jnp.concatenate(
            [
                back[pl.ds(slot + 8 * PAIRS, 8, stride=PAIRS), :],
                jnp.zeros((LANES - 16, LANES), F32),
                back[pl.ds(slot, 8, stride=PAIRS), :],
            ],
            axis=0,
        ).T
        if k < 2:
            main = jnp.concatenate(
                [mains[k][c, pl.ds((2 * t + 1 + e) * PITCH, NS)] for e in range(2)], axis=0
            )
        else:
            main = out3_ref[c, pl.ds(t * LANES, LANES)]
        outs[k][c, pl.ds(t * LANES, LANES)] = jnp.where(outer, edge, main)

    zero = jnp.zeros((8, LANES), F32)
    sums = (zero,) * 6
    for k in range(3):
        if k == 2:
            for slot in range(9):
                for r in (0, 1, 14, 15):
                    back[pl.ds(slot * edge_rows + r * PAIRS, PAIRS)] = jnp.zeros((PAIRS, LANES), F32)
            for i in range(HALO):
                back_edges(i, 0, (0, 1))
            for n in (0, 1):
                for c in (0, 1):
                    merge(n, c, 0)

            site = jnp.zeros((8, 2 * LANES), F32)
            for s, across in ((0, NS // 4), (1, 3 * NS // 4)):
                picked = [v0[c, pl.ds(PITCH + across, 1)] for c in (0, 1)]
                picked += [out1_ref[c, pl.ds(across, 1)] for c in (0, 1)]
                picked += [out2_ref[c, pl.ds(across, 1)] for c in (0, 1)]
                picked += [jnp.zeros((2, LANES), F32)]
                site = site + jnp.dot(
                    jnp.concatenate(picked, axis=0),
                    hit[s],
                    precision=HIGHEST,
                    preferred_element_type=F32,
                )
            site_a[...] = jnp.concatenate([site[:, :LANES], site[:, LANES:]], axis=0)
        source, target = xs[k], xs[k + 1]

        def strip_divergence(i, carry, k=k, source=source):
            p = i + 2 * k + 1
            row = p * SECTION
            first, second = rows(source.at[0], row - SECTION), rows(source.at[0], row + SECTION)
            middle = rows(source.at[1], row)
            third = beside(source.at[2], row, rows(source.at[2], row))
            for e in range(2):
                strip_w[pl.ds(row + 16 * e, 8)] = (
                    (0.25 * bulk_modulus)
                    * (
                        (second[e] - first[e])
                        + (after(middle[e]) - before(middle[e]))
                        + (third[e][0] - third[e][1])
                    )
                    * valid[p]
                )
            return carry

        lax.fori_loop(0, WIDE - 2 - 4 * k, strip_divergence, 0, unroll=DIV_UNROLL[k])

        def strip_image(i, sums, k=k, source=source, target=target):
            p = i + 2 * k + 2
            row = p * SECTION
            heavy = rows(strip_mass, row)
            local = rows(strip_w, row)
            around = rows(strip_w, row - SECTION), rows(strip_w, row + SECTION)
            upright = beside(strip_w, row, local)
            images, heres = [], []
            for c in range(3):
                ref = source.at[c]
                here = rows(ref, row)
                along = rows(ref, row - SECTION), rows(ref, row + SECTION)
                depth = beside(ref, row, here)
                for e in range(2):
                    image = (heavy[e] + 6.0) * here[e] - (along[0][e] + along[1][e])
                    image = image - (depth[e][0] + depth[e][1])
                    if c == 1:
                        image = image - (after(here[e] + local[e]) + before(here[e] - local[e]))
                    else:
                        image = image - (after(here[e]) + before(here[e]))
                    if c == 0:
                        image = image - (around[1][e] - around[0][e])
                    elif c == 2:
                        image = image - (upright[e][0] - upright[e][1])
                    images.append(image * valid[p])
                    heres.append(here[e])
            sums = list(sums)
            for n, (image, here) in enumerate(zip(images, heres)):
                at = pl.ds(row + 16 * (n % 2), 8)
                target[n // 2, at] = image
                if k == 2:
                    z0, z1 = x0[n // 2, at], x1[n // 2, at]
                    for m, (p0, p1) in enumerate(
                        ((z0, z0), (z0, z1), (z1, z1), (z1, here), (here, here), (here, image))
                    ):
                        sums[m] = sums[m] + p0 * p1
            return tuple(sums)

        sums = lax.fori_loop(0, WIDE - 4 - 4 * k, strip_image, sums, unroll=IMG_UNROLL[k])
    strips = sums

    head, rest = [], []
    for n in range(6):
        hi, lo = two_sum(moments[n], strips[n])
        for shift in (4, 2, 1):
            hi, more = two_sum(hi, pltpu.roll(hi, shift, 0))
            lo = lo + pltpu.roll(lo, shift, 0) + more
        head.append(hi[0:1])
        rest.append(lo[0:1])
    blank = [jnp.zeros((2, LANES), F32)]
    hi, lo = jnp.concatenate(head + blank, axis=0), jnp.concatenate(rest + blank, axis=0)
    for shift in (64, 32, 16, 8, 4, 2, 1):
        hi, more = two_sum(hi, pltpu.roll(hi, shift, 1))
        lo = lo + pltpu.roll(lo, shift, 1) + more
    hi, lo = two_sum(hi, lo)
    sublane = lax.broadcasted_iota(jnp.int32, (8, LANES), 0)
    at_hi, at_lo = lane == sublane, lane == sublane + 8
    packed = jnp.sum(jnp.where(at_hi, hi, 0.0) + jnp.where(at_lo, lo, 0.0), axis=0, keepdims=True)
    part[...] = packed

    copies = exchange(site_a, site_slots_a, group_a, at_xs, site_a_send, site_a_recv)
    copies_a = copies

    pl.semaphore_wait(ready, len(group_a))
    ring = lambda a, n: min(a, n - a)
    far = lambda o: -(ring(o[0] // 4, 4) + ring(o[0] % 4, 4) + ring(o[1] // 2, 4))
    offsets = [(a, b) for a in range(len_size) for b in range(xs_size) if a or b]
    lens = [lax.rem(at_len + a, len_size) for a in range(len_size)]
    spots = [lax.rem(at_xs + b, xs_size) for b in range(xs_size)]
    for a, b in sorted(offsets, key=far):
        pltpu.make_async_remote_copy(
            src_ref=part,
            dst_ref=slots.at[pl.ds(me, 1)],
            send_sem=all_send,
            recv_sem=all_recv,
            device_id=(lens[a], spots[b]),
            device_id_type=MESH,
        ).start()
    slots[pl.ds(me, 1)] = part[...]

    for i in range(HALO):
        back_edges(i, 0, (2,))
    merge(0, 2, 0)
    merge(1, 2, 0)
    for c in range(3):
        merge(2, c, 0)

    for copy in copies_a:
        copy.wait_recv()
    site_b[...] = tree([site_slots_a[i] for i in range(xs_size)], jnp.add)
    copies_b = exchange(site_b, site_slots_b, group_b, at_len, site_b_send, site_b_recv)

    def merge_rest(t, carry):
        for k in range(3):
            for c in range(3):
                merge(k, c, t)
        return carry

    lax.fori_loop(1, PAIRS, merge_rest, 0)

    others = slots.at[pl.ds(0, count - 1)]
    pltpu.make_async_copy(others, others, all_recv).wait()
    hi, lo = tree(
        [(slots[pl.ds(8 * i, 8)], jnp.zeros((8, LANES), F32)) for i in range(count // 8)], join
    )
    for shift in (4, 2, 1):
        hi, more = two_sum(hi, pltpu.roll(hi, shift, 0))
        lo = lo + pltpu.roll(lo, shift, 0) + more
    pick = lambda mask, x: jnp.broadcast_to(
        jnp.sum(jnp.where(mask, x, 0.0), axis=1, keepdims=True), (8, LANES)
    )
    increment, solved = steps(pick(at_hi, hi), pick(at_lo, hi) + pick(at_hi, lo))
    coefficients_ref[...] = jnp.concatenate(
        list(increment) + list(solved) + [jnp.zeros((1, LANES), F32)], axis=0
    )

    def combine(d, carry):
        at = pl.ds(pl.multiple_of(d * NS, NS), NS)
        for c in range(3):
            p0 = v0[c, pl.ds((d + 1) * PITCH, NS)]
            p1, p2, p3 = out1_ref[c, at], out2_ref[c, at], out3_ref[c, at]
            inc_ref[c, at] = increment[0] * p0 + increment[1] * p1 + increment[2] * p2
            solved_ref[c, at] = (
                solved[0] * p0 + solved[1] * p1 + solved[2] * p2 + solved[3] * p3
            )
        return carry

    lax.fori_loop(0, DEPTH, combine, 0)

    for copy in copies_b:
        copy.wait_recv()
    sites_ref[...] = tree([site_slots_b[i] for i in range(len_size)], jnp.add)
    pltpu.make_async_copy(others, others, all_send).wait()
    for copy in halos + copies_a + copies_b:
        copy.wait_send()


def steps(hi, lo):
    for shift in (64, 32, 16, 8, 4, 2, 1):
        hi, more = two_sum(hi, pltpu.roll(hi, shift, 1))
        lo = lo + pltpu.roll(lo, shift, 1) + more
    hi, lo = two_sum(hi, lo)
    theta = jnp.round(hi[1:2] / hi[0:1] * 64.0) * (1.0 / 64.0)
    central = [hi[0:1]]
    for order in range(5):
        n = 5 - order
        big = hi[:n] * 4097.0
        upper = big - (big - hi[:n])
        lower = hi[:n] - upper
        value, more = two_sum(hi[1 : n + 1], -theta * upper)
        value, extra = two_sum(value, -theta * lower)
        low_part = lo[1 : n + 1] - theta * lo[:n] + (more + extra)
        hi, lo = two_sum(value, low_part)
        central.append(hi[0:1])
    scale = 1.0 / central[0]
    c = [x * scale for x in central]
    c1 = [c[i + 1] + theta * c[i] for i in range(5)]

    def form(p, moments):
        terms = None
        for i in range(len(p)):
            for j in range(i, len(p)):
                term = (1.0 if i == j else 2.0) * (p[i] * p[j]) * moments[i + j]
                terms = term if terms is None else terms + term
        return terms

    one, zero = jnp.ones_like(theta), jnp.zeros_like(theta)
    left, ahead, norm = [one], [one], c[0]
    increment = [zero, zero, zero]
    for iteration in range(3):
        alpha = norm / form(ahead, c1)
        increment = [
            x + alpha * ahead[i] if i < len(ahead) else x for i, x in enumerate(increment)
        ]
        image = [theta * x for x in ahead] + [zero]
        image = [image[i] + (ahead[i - 1] if i else zero) for i in range(len(image))]
        left = left + [zero]
        left = [x - alpha * y for x, y in zip(left, image)]
        if iteration < 2:
            after = form(left, c)
            beta = after / norm
            ahead = ahead + [zero]
            ahead = [x + beta * y for x, y in zip(left, ahead)]
            norm = after
    x0, x1, x2 = increment
    r0, r1, r2, r3 = left
    increment = (x0 - theta * (x1 - theta * x2), x1 - 2.0 * theta * x2, x2)
    solved = (
        r0 - theta * (r1 - theta * (r2 - theta * r3)),
        r1 - theta * (2.0 * r2 - 3.0 * theta * r3),
        r2 - 3.0 * theta * r3,
        r3,
    )
    return increment, solved


def finish_kernel(
    increment_ref,
    solved_ref,
    coefficients_ref,
    sites_ref,
    spans_ref,
    stick_ref,
    load_ref,
    prior_ref,
    inc_ref,
    res_ref,
    friction_ref,
    first,
    out_sem,
):
    rows = DEPTH * NS
    at, top = pl.ds(NS, rows - NS), pl.ds(0, NS)
    stores = []

    def store(source, target):
        copy = pltpu.make_async_copy(source, target, out_sem.at[len(stores)])
        copy.start()
        stores.append(copy)

    for c in range(3):
        store(increment_ref.at[c], inc_ref.at[c])
        store(solved_ref.at[c, at], res_ref.at[c, at])

    me = lax.axis_index("len") * lax.axis_size("xs") + lax.axis_index("xs")

    wide = lambda n: jnp.concatenate([coefficients_ref[pl.ds(n, 1)]] * 2, axis=1)
    site = jnp.concatenate([sites_ref[0:8], sites_ref[8:16]], axis=1)
    readout = wide(0) * site[0:2] + wide(1) * site[2:4] + wide(2) * site[4:6]
    radius = jnp.where(stick_ref[...] == 1, static_friction, kinetic_friction) * load_ref[...]
    trial = prior_ref[...] + elastic_stiffness * readout
    magnitude = jnp.sqrt(trial[0:1] * trial[0:1] + trial[1:2] * trial[1:2])
    friction = trial * (radius / jnp.maximum(magnitude, radius))
    friction_ref[...] = friction
    force = friction + load_ref[...] / pendulum_radius * readout
    bearings = force.shape[1]
    forces = jnp.concatenate(
        [force, jnp.ones((1, bearings), F32), jnp.zeros((5, bearings), F32)], axis=0
    )
    hits = bearing_hits(bearing_ends(spans_ref[...]), me * LANES)
    placed = [
        lax.dot_general(
            forces,
            hit,
            (((1,), (1,)), ((), ())),
            precision=HIGHEST,
            preferred_element_type=F32,
        )
        for hit in hits
    ]
    for c in range(3):
        first[c] = solved_ref[c, top]
        for s, across in ((0, NS // 4), (1, 3 * NS // 4)):
            node = pl.ds(across, 1)
            if c < 2:
                drop = placed[s][c : c + 1]
            else:
                drop = vertical_stiffness * increment_ref[c, node] * placed[s][2:3]
            first[c, node] = first[c, node] - drop
        store(first.at[c], res_ref.at[c, top])
    for copy in stores:
        copy.wait()


def shards(right_side, mass_field, span_lengths, stick_flags, normal_load, prior_friction):
    sizes = (lax.axis_size("len"), lax.axis_size("xs"))
    count = sizes[0] * sizes[1]
    rows = DEPTH * NS
    field = (3, rows, LANES)
    b = right_side.reshape(field)
    mass = mass_field.reshape(rows, LANES)
    spans = span_lengths.reshape(1, -1)
    stick = stick_flags.reshape(1, -1)
    load = normal_load.reshape(1, -1)
    anywhere = pl.BlockSpec(memory_space=pl.ANY)
    hbm = pl.BlockSpec(memory_space=pltpu.HBM)
    far = lambda a: pltpu.with_memory_space_constraint(a, pltpu.HBM)
    vmem = pl.BlockSpec(memory_space=pltpu.VMEM)
    increment, solved, coefficients, sites = pl.pallas_call(
        lambda *refs: krylov_kernel(sizes, *refs),
        name="krylov",
        out_shape=[pltpu.VMEM(field, F32)] * 2
        + [pltpu.VMEM((8, LANES), F32), pltpu.VMEM((16, LANES), F32)],
        in_specs=[hbm] * 3,
        out_specs=[vmem] * 4,
        scratch_shapes=[pltpu.VMEM((3, PADDED, LANES), F32)] * 3
        + [pltpu.VMEM(field, F32)] * 3
        + [pltpu.VMEM((rows, LANES), F32), pltpu.VMEM((PADDED, LANES), F32)]
        + [pltpu.VMEM((3, STRIP, LANES), F32)] * 4
        + [pltpu.VMEM((STRIP, LANES), F32)] * 2
        + [pltpu.VMEM((OWN + LANDED, LANES), F32)] * 2
        + [
            pltpu.VMEM((WIDE, 8, LANES), F32),
            pltpu.VMEM((9 * 16 * PAIRS, LANES), F32),
            pltpu.VMEM((2, LANES, 2 * LANES), F32),
            pltpu.VMEM(spans.shape, jnp.int32),
        ]
        + [pltpu.VMEM((1, LANES), F32), pltpu.VMEM((count, LANES), F32)]
        + [pltpu.VMEM((16, LANES), F32)] * 2
        + [pltpu.VMEM((n, 16, LANES), F32) for n in (sizes[1], sizes[0])]
        + [pltpu.SemaphoreType.DMA((n,)) for n in (5, 2, 2)]
        + [pltpu.SemaphoreType.DMA, pltpu.SemaphoreType.DMA, pltpu.SemaphoreType.REGULAR]
        + [pltpu.SemaphoreType.DMA((n,)) for n in (sizes[1], sizes[1], sizes[0], sizes[0])],
        compiler_params=pltpu.CompilerParams(
            collective_id=0, has_side_effects=True, vmem_limit_bytes=32 * 2**20
        ),
    )(far(b), far(mass), far(spans))
    increment, residual, friction = pl.pallas_call(
        finish_kernel,
        name="finish",
        out_shape=[
            jax.ShapeDtypeStruct(field, F32),
            jax.ShapeDtypeStruct(field, F32),
            jax.ShapeDtypeStruct(prior_friction.shape, F32),
        ],
        in_specs=[vmem] * 8,
        out_specs=[anywhere, anywhere, vmem],
        scratch_shapes=[
            pltpu.VMEM((3, NS, LANES), F32),
            pltpu.SemaphoreType.DMA((9,)),
        ],
        compiler_params=pltpu.CompilerParams(vmem_limit_bytes=24 * 2**20),
    )(increment, solved, coefficients, sites, spans, stick, load, prior_friction)
    return (
        increment.reshape(right_side.shape),
        residual.reshape(right_side.shape),
        friction,
    )


def solution(mesh):
    along = ("len", "xs")
    in_specs = (P(None, None, None, along), P(None, None, along), P(), P(), P(), P())
    out_specs = (P(None, None, None, along), P(None, None, None, along), P())
    return jax.shard_map(shards, mesh=mesh, in_specs=in_specs, out_specs=out_specs, check_vma=False)
```
